256 devices in a mesh: seq: 64 (over z, x, y_hi), head: 4 (over y_lo, core).
Axes of the slice: x: 4, y: 4 (y_hi: 2, y_lo: 2; y = y_hi * 2 + y_lo), z: 8, core: 2. Of those that a mesh axis runs over, the one named last changes fastest.
Arguments:
- hidden_in: bfloat16 [8192, 2048], P('seq'), may hold values from -6 to 6
- attn_gain: float32 [2048], replicated, may hold values from 0.1 to 1.9
- w_query: bfloat16 [2048, 3072], P(None, 'head'), may hold values from -2 to 2
- w_latent: bfloat16 [2048, 576], P(None, 'head'), may hold values from -2 to 2
- latent_gain: float32 [512], replicated, may hold values from 0.1 to 1.9
- w_expand: bfloat16 [512, 4096], P(None, 'head'), may hold values from -0.25 to 0.25
- w_out: bfloat16 [2048, 2048], P('head'), may hold values from -0.125 to 0.125
- moe_gain: float32 [2048], replicated, may hold values from 0.1 to 1.9
- w_gate: bfloat16 [64, 2048, 1408], P('seq', None, 'head'), may hold values from -0.125 to 0.125
- w_up: bfloat16 [64, 2048, 1408], P('seq', None, 'head'), may hold values from -0.125 to 0.125
- w_down: bfloat16 [64, 1408, 2048], P('seq', 'head'), may hold values from -0.15625 to 0.15625
- routes: int32 [8192, 6], P('seq'), may hold values from 0 to 63, all different within a row; in each aligned block of 128 rows (0 to 127, 128 to 255, ...) at most 15 rows name the same one
- gates: float32 [8192, 6], P('seq'), may hold values from 0.1 to 0.6
- segment: int32 [8192], P('seq'), may hold values from 0 to 16, never falling along the last dimension, each value on 1 to 6144 neighbouring positions
- page_table: int32 [64, 4], P('seq'), may hold values from 0 to 3, each once within a row
Outputs:
- hidden_out: bfloat16 [8192, 2048], P('seq')
- latent_cache: bfloat16 [256, 18432], P(('seq', 'head'))
The draws below stay inside these ranges and needn't reach their ends.
Inputs may be any that keep to these rules, and one draw needn't show every extreme that they name: `routes`: each row names 6 different experts; among the 128 rows of one device no expert is named more than 15 times, a bound that some block reaches. `segment`: ids never fall along the stream; each of the 17 documents is contiguous, and the longest has exactly 6144 tokens. `page_table`: each row is a permutation of the 4 slots of one token block.
All inputs are finite; a program needn't handle non-finite values.
Results may differ from the reference program's by a relative error of at most 0.015.
Values may be sent and summed in bfloat16 or wider, within the bound.
A program may use at most 192 MiB of HBM per device.

```python
import math
import jax
import jax.numpy as jnp
import numpy as np
from jax import lax

D = 2048
HEADS = 16
NOPE = 128
ROPE = 64
VDIM = 128
LATENT = 512
FF = 1408
TOPK = 6
TOK_DEV = 128
DOCS = 17
PAGE = 32
EXPERTS = 64
TOKENS = 8192
LONGEST = 6144
PPD = 4
CAP = 15
N_SEQ = 64
N_HEAD = 4


def draw_hidden_in(key, part):
    base = jnp.clip(jax.random.normal(jax.random.fold_in(key, 9102), (TOKENS, D), jnp.float32), -6.0, 6.0)
    return base.astype(jnp.bfloat16)


def draw_w_query(key, part):
    width = HEADS * (NOPE + ROPE)
    base = jnp.clip(jax.random.normal(jax.random.fold_in(key, 9105), (D, width), jnp.float32), -4.0, 4.0) * D ** (-0.5)
    return base.astype(jnp.bfloat16)


def draw_w_latent(key, part):
    width = LATENT + ROPE
    base = jnp.clip(jax.random.normal(jax.random.fold_in(key, 9106), (D, width), jnp.float32), -4.0, 4.0) * D ** (-0.5)
    return base.astype(jnp.bfloat16)


def steps_of(key, extent, shards, low, largest):
    loudness, own = 1.0, jax.random.fold_in(key, 6)
    for axis_at, parts in shards:
        steps = jnp.exp(jax.random.uniform(jax.random.fold_in(own, axis_at), (parts,), jnp.float32, low / len(shards), largest / len(shards)))
        loudness = loudness * jnp.repeat(steps, extent[axis_at] // parts).reshape([-1 if axis == axis_at else 1 for axis in range(len(extent))])
    return loudness


def length_profile(amount, total, reach, lean):
    loads = [(1 << 20) // math.isqrt(standing ** lean) + 1 for standing in range(2, amount + 1)]
    rest, holding = total - reach - (amount - 1), [1] * (amount - 1)
    while rest > 0:
        movable = [i for i in range(amount - 1) if holding[i] < reach]
        pool, budget = sum([loads[i] for i in movable]), rest
        for i in movable:
            extra = min(reach - holding[i], max(1, budget * loads[i] // pool), rest)
            holding[i] = holding[i] + extra
            rest = rest - extra
    return np.array([reach] + holding)


def ragged(own_key, number_of, total, bound, slope):
    if number_of == 2:
        one = jax.random.randint(own_key, (), max(1, total - bound), min(bound, total - 1) + 1)
        return jnp.stack([one, total - one])
    tallies = jnp.asarray(length_profile(number_of, total, bound, slope), jnp.int32)
    twos = (number_of - 1) // 2
    giver, taker = tallies[1:1 + 2 * twos:2], tallies[2:2 + 2 * twos:2]
    room = jnp.minimum(giver - 1, bound - taker)
    passed = jax.random.randint(jax.random.fold_in(own_key, 1), (twos,), 0, 1 << 20) % (room + 1)
    tallies = tallies.at[1:1 + 2 * twos:2].set(giver - passed).at[2:2 + 2 * twos:2].set(taker + passed)
    return tallies[jax.random.permutation(jax.random.fold_in(own_key, 2), number_of)]


def routed_block(key, own, number, rows, number_of, top, reach, skew):
    sequence = jax.random.permutation(key, number_of)
    crowded, usual = portions_of(number_of, rows * top, reach, skew, True), portions_of(number_of, rows * top, reach, skew, False)
    places = jnp.arange(number_of)

    def named(lengths, offset_by):
        used = int((lengths > 0).sum())
        fixed = max(1, used // 4)
        moved = fixed + (places - fixed + offset_by * (used - fixed)) % max(1, number_of - fixed)
        return jnp.zeros((number_of,), jnp.int32).at[sequence[jnp.where(places < fixed, places, moved)]].set(jnp.asarray(lengths, jnp.int32))

    lengths = jnp.where(number % 4 == 0, named(crowded, number // 4), named(usual, number - number // 4 - 1))
    mixed = jax.random.permutation(jax.random.fold_in(own, 3), number_of)
    giver, taker = mixed[0:number_of // 2 * 2:2], mixed[1:number_of // 2 * 2:2]
    room = jnp.minimum(lengths[giver] - 1, reach - lengths[taker]) // 2
    room = jnp.where((giver == sequence[0]) | (taker == sequence[0]) | (lengths[taker] == 0), 0, jnp.maximum(room, 0))
    moved = jax.random.randint(jax.random.fold_in(own, 4), (number_of // 2,), 0, 1 << 20) % (room + 1)
    lengths = lengths.at[giver].add(-moved).at[taker].add(moved)
    items = jnp.searchsorted(jnp.cumsum(lengths), jnp.arange(rows * top), side="right").astype(jnp.int32)
    listing = items.reshape(top, rows).T
    listing = listing[jax.random.permutation(jax.random.fold_in(own, 1), rows)]
    offset_by = jax.random.randint(jax.random.fold_in(own, 2), (rows, 1), 0, top)
    return jnp.take_along_axis(listing, (jnp.arange(top)[None, :] + offset_by) % top, axis=1)


def portions_of(count, total, bound, skew, full):
    loads = [(1 << 20) // math.isqrt(grade ** skew) + 1 for grade in range(1, count + 1)]
    largest = bound if full else min(bound, max(-(-total // count), total * loads[0] // sum(loads)))
    least = 1 if total - largest >= count - 1 else 0
    given, rest = [largest] + [least] * (count - 1), total - largest - least * (count - 1)
    while rest > 0:
        candidates = [i for i in range(1, count) if given[i] < largest] or [i for i in range(1, count) if given[i] < bound]
        pool, budget = sum([loads[i] for i in candidates]), rest
        for i in candidates:
            addition = min(bound - given[i], max(1, budget * loads[i] // pool), rest)
            given[i] = given[i] + addition
            rest = rest - addition
    return np.array(given)


def bell_draw(stream_key, dims, scale, bound, shards=(), kind=jnp.bfloat16):
    result = scale * jax.random.normal(stream_key, dims, jnp.float32)
    if shards:
        result = result * steps_of(stream_key, dims, shards, -0.22, 0.18)
    return jnp.clip(result, -bound, bound).astype(kind)


def setup_inputs(seed: int = 0) -> dict:
    key_list = jax.random.split(jax.random.key(seed), 16)
    hidden_in = draw_hidden_in(jax.random.fold_in(key_list[15], 71), 0)
    attn_gain = jnp.clip(1.0 + 0.18 * jax.random.normal(key_list[1], (D,), jnp.float32), 0.1, 1.9)
    w_query = draw_w_query(jax.random.fold_in(key_list[15], 71), 0)
    w_latent = draw_w_latent(jax.random.fold_in(key_list[15], 71), 0)
    latent_gain = jnp.clip(1.0 + 0.18 * jax.random.normal(key_list[4], (LATENT,), jnp.float32), 0.1, 1.9)
    w_expand = bell_draw(key_list[5], (LATENT, HEADS * (NOPE + VDIM)), LATENT ** -0.5, 0.25, ((1, 4),))
    w_out = bell_draw(key_list[6], (HEADS * VDIM, D), (HEADS * VDIM) ** -0.5, 0.125, ((0, 4),))
    moe_gain = jnp.clip(1.0 + 0.18 * jax.random.normal(key_list[7], (D,), jnp.float32), 0.1, 1.9)
    w_gate = bell_draw(key_list[8], (EXPERTS, D, FF), D ** -0.5, 0.125, ((0, 64), (2, 4)))
    w_up = bell_draw(key_list[9], (EXPERTS, D, FF), D ** -0.5, 0.125, ((0, 64), (2, 4)))
    w_down = bell_draw(key_list[10], (EXPERTS, FF, D), FF ** -0.5, 0.15625, ((0, 64), (1, 4)))
    routes_keys = jax.random.split(jax.random.fold_in(key_list[11], 1), TOKENS // TOK_DEV)
    routes_turns = jax.random.permutation(jax.random.fold_in(key_list[11], 3), TOKENS // TOK_DEV)
    routes = jax.vmap(lambda own, number: routed_block(jax.random.fold_in(key_list[11], 2), own, number, TOK_DEV, EXPERTS, TOPK, CAP, 2))(routes_keys, routes_turns).reshape((TOKENS, TOPK))
    gates = jnp.clip(0.1 + 0.5 * jax.random.uniform(key_list[12], (TOKENS, TOPK), jnp.float32) ** steps_of(key_list[12], (TOKENS, TOPK), ((0, 64),), -0.2, 0.2), 0.1, 0.6)
    segment = jnp.searchsorted(jnp.cumsum(ragged(key_list[13], DOCS, TOKENS, LONGEST, 0)), jnp.arange(TOKENS), side="right").astype(jnp.int32)
    page_table = jax.vmap(lambda own: jax.random.permutation(own, PPD))(jax.random.split(key_list[14], N_SEQ)).reshape((N_SEQ, PPD)).astype(jnp.int32)
    return {"hidden_in": hidden_in, "attn_gain": attn_gain, "w_query": w_query, "w_latent": w_latent, "latent_gain": latent_gain, "w_expand": w_expand, "w_out": w_out, "moe_gain": moe_gain, "w_gate": w_gate, "w_up": w_up, "w_down": w_down, "routes": routes, "gates": gates, "segment": segment, "page_table": page_table}


EPS = 1e-06
THETA = 50000.0

def rms_scale(values, scale_gain):
    mean_sq = lax.optimization_barrier(jnp.mean(values * values, axis=-1, keepdims=True))
    return values * lax.rsqrt(mean_sq + EPS) * scale_gain

def rope_tables(positions, feat_width):
    half_width = feat_width // 2
    inv_freq = THETA ** (-jnp.arange(half_width, dtype=jnp.float32) * 2.0 / feat_width)
    angles = positions.astype(jnp.float32)[:, None] * inv_freq[None, :]
    return (jnp.cos(angles), jnp.sin(angles))

def rotate(values, cosine, sine_table):
    half_width = values.shape[-1] // 2
    table_shape = cosine.shape[:1] + (1,) * (values.ndim - 2) + cosine.shape[1:]
    cosine = cosine.reshape(table_shape)
    sine_table = sine_table.reshape(table_shape)
    lower_half = values[..., :half_width]
    upper_half = values[..., half_width:]
    return jnp.concatenate([lower_half * cosine - upper_half * sine_table, upper_half * cosine + lower_half * sine_table], axis=-1)

def reference(hidden_in, attn_gain, w_query, w_latent, latent_gain, w_expand, w_out, moe_gain, w_gate, w_up, w_down, routes, gates, segment, page_table):
    tokens = hidden_in.shape[0]
    positions = jnp.arange(tokens, dtype=jnp.int32)
    cosine, sine_table = rope_tables(positions, ROPE)
    residual_in = hidden_in.astype(jnp.float32)
    normed = rms_scale(residual_in, attn_gain).astype(jnp.bfloat16)
    latent_raw = jnp.dot(normed, w_latent, preferred_element_type=jnp.float32).astype(jnp.bfloat16)
    compressed = rms_scale(latent_raw[:, :LATENT].astype(jnp.float32), latent_gain).astype(jnp.bfloat16)
    key_rope = rotate(latent_raw[:, LATENT:].astype(jnp.float32), cosine, sine_table).astype(jnp.bfloat16)
    queries = jnp.dot(normed, w_query, preferred_element_type=jnp.float32).reshape(tokens, HEADS, NOPE + ROPE)
    query_nope = queries[:, :, :NOPE].astype(jnp.bfloat16)
    query_rope = rotate(queries[:, :, NOPE:], cosine, sine_table).astype(jnp.bfloat16)
    expanded = jnp.dot(compressed, w_expand, preferred_element_type=jnp.float32).astype(jnp.bfloat16)
    expanded = expanded.reshape(tokens, HEADS, NOPE + VDIM)
    key_nope = expanded[:, :, :NOPE]
    key_values = expanded[:, :, NOPE:]
    softmax_scale = (NOPE + ROPE) ** (-0.5)
    allowed = (segment[:, None] == segment[None, :]) & (positions[None, :] <= positions[:, None])

    def one_head(operands):
        head_qn, head_qr, head_kn, head_val = operands
        scores = jnp.dot(head_qn, head_kn.T, preferred_element_type=jnp.float32)
        scores = scores + jnp.dot(head_qr, key_rope.T, preferred_element_type=jnp.float32)
        scores = jnp.where(allowed, scores * softmax_scale, -jnp.inf)
        row_max = lax.optimization_barrier(jnp.max(scores, axis=1, keepdims=True))
        weights = jnp.exp(scores - row_max)
        denom_sum = lax.optimization_barrier(jnp.sum(weights, axis=1, keepdims=True))
        head_mix = jnp.dot(weights.astype(jnp.bfloat16), head_val, preferred_element_type=jnp.float32) / denom_sum
        return head_mix.astype(jnp.bfloat16)
    heads_out = lax.map(one_head, (query_nope.transpose(1, 0, 2), query_rope.transpose(1, 0, 2), key_nope.transpose(1, 0, 2), key_values.transpose(1, 0, 2)))
    attention = jnp.einsum('htd,hde->te', heads_out.astype(jnp.float32), w_out.reshape(HEADS, VDIM, D).astype(jnp.float32))
    residual = (residual_in + attention).astype(jnp.bfloat16)
    moe_in = rms_scale(residual.astype(jnp.float32), moe_gain).astype(jnp.bfloat16)
    moe_ext = jnp.concatenate([moe_in, jnp.zeros((1, D), jnp.bfloat16)], axis=0)
    flat_expert = routes.reshape(-1).astype(jnp.int32)
    flat_count = flat_expert.shape[0]
    gate_ext = jnp.concatenate([gates.reshape(-1), jnp.zeros((1,), jnp.float32)], axis=0)
    sort_order = jnp.argsort(flat_expert, stable=True).astype(jnp.int32)
    counts = lax.optimization_barrier(jnp.sum((flat_expert[:, None] == jnp.arange(EXPERTS, dtype=jnp.int32)[None, :]).astype(jnp.int32), axis=0))
    starts = (jnp.cumsum(counts) - counts).astype(jnp.int32)
    max_rows = N_SEQ * CAP
    order_ext = jnp.concatenate([sort_order, jnp.full((max_rows,), flat_count, jnp.int32)], axis=0)
    group_width = FF // N_HEAD

    def one_expert(moe_sum, expert):
        chosen = lax.dynamic_slice_in_dim(order_ext, starts[expert], max_rows)
        active = jnp.arange(max_rows, dtype=jnp.int32) < counts[expert]
        chosen = jnp.where(active, chosen, flat_count).astype(jnp.int32)
        tok_index = (chosen // TOPK).astype(jnp.int32)
        expert_rows = moe_ext[tok_index]
        gate_proj = jnp.dot(expert_rows, w_gate[expert], preferred_element_type=jnp.float32)
        up_proj = jnp.dot(expert_rows, w_up[expert], preferred_element_type=jnp.float32)
        hidden = (jax.nn.silu(gate_proj) * up_proj).astype(jnp.bfloat16)
        part_sums = jnp.einsum('rgf,gfd->grd', hidden.reshape(max_rows, N_HEAD, group_width).astype(jnp.float32), w_down[expert].reshape(N_HEAD, group_width, D).astype(jnp.float32))
        part_sums = part_sums.astype(jnp.bfloat16)
        combined = lax.optimization_barrier(jnp.sum(part_sums.astype(jnp.float32), axis=0))
        weight = jnp.where(active, gate_ext[chosen], 0.0)
        moe_sum = moe_sum.at[tok_index].add(combined * weight[:, None])
        return (moe_sum, None)
    moe_sum, _ = lax.scan(one_expert, jnp.zeros((tokens + 1, D), jnp.float32), jnp.arange(EXPERTS, dtype=jnp.int32))
    hidden_out = (residual.astype(jnp.float32) + moe_sum[:tokens]).astype(jnp.bfloat16)
    page_rows = jnp.concatenate([compressed, key_rope], axis=1).reshape(N_SEQ, PPD, PAGE * (LATENT + ROPE))
    inverse = jnp.argsort(page_table, axis=1).astype(jnp.int32)
    latent_cache = jnp.take_along_axis(page_rows, inverse[:, :, None], axis=1).reshape(N_SEQ * PPD, PAGE * (LATENT + ROPE))
    return (hidden_out, latent_cache)
```

```python
import functools

import jax
import jax.numpy as jnp
from jax import lax
from jax.experimental import pallas as pl
from jax.experimental.pallas import tpu as pltpu
from jax.sharding import PartitionSpec as P

D = 2048
NOPE = 128
ROPE = 64
VDIM = 128
LATENT = 512
TOPK = 6
PAGE = 32
LONGEST = 6144
SLOTS = 16
KT = 512

EPS = 1e-06
THETA = 50000.0
F32 = jnp.float32
BF16 = jnp.bfloat16


def rms_scale(values, scale_gain):
    mean_sq = jnp.mean(values * values, axis=-1, keepdims=True)
    return values * lax.rsqrt(mean_sq + EPS) * scale_gain


def rope_tables(positions, feat_width):
    half_width = feat_width // 2
    inv_freq = THETA ** (-jnp.arange(half_width, dtype=F32) * 2.0 / feat_width)
    angles = positions.astype(F32)[:, None] * inv_freq[None, :]
    return (jnp.cos(angles), jnp.sin(angles))


def rotate(values, cosine, sine_table):
    half_width = values.shape[-1] // 2
    table_shape = cosine.shape[:1] + (1,) * (values.ndim - 2) + cosine.shape[1:]
    cosine = cosine.reshape(table_shape)
    sine_table = sine_table.reshape(table_shape)
    lower_half = values[..., :half_width]
    upper_half = values[..., half_width:]
    return jnp.concatenate(
        [
            lower_half * cosine - upper_half * sine_table,
            upper_half * cosine + lower_half * sine_table,
        ],
        axis=-1,
    )


def dot(a, b):
    return jnp.dot(a, b, preferred_element_type=F32)


def attend_kernel(tok, heads, ql_ref, qr_ref, keys_ref, qseg_ref, kseg_ref, o_ref, m_ref, l_ref, acc_ref):
    s = lax.axis_index("seq")
    rows = heads * tok
    m_ref[...] = jnp.full_like(m_ref, -1e30)
    l_ref[...] = jnp.zeros_like(l_ref)
    acc_ref[...] = jnp.zeros_like(acc_ref)
    qpos = s * tok + lax.broadcasted_iota(jnp.int32, (rows, 1), 0) % tok
    first = jnp.maximum(s * tok - (LONGEST - 1), 0) // KT
    last = (s * tok + tok - 1) // KT + 1

    def step(kt, carry):
        at = pl.multiple_of(kt * KT, KT)
        c = keys_ref[pl.ds(at, KT), :LATENT]
        kr = keys_ref[pl.ds(at, KT), LATENT:]
        sc = lax.dot_general(ql_ref[...], c, (((1,), (1,)), ((), ())), preferred_element_type=F32)
        sc = sc + lax.dot_general(qr_ref[...], kr, (((1,), (1,)), ((), ())), preferred_element_type=F32)
        kpos = at + lax.broadcasted_iota(jnp.int32, (1, KT), 1)
        ok = (qseg_ref[...] == kseg_ref[kt]) & (kpos <= qpos)
        sc = jnp.where(ok, sc, -1e30)
        m_old = m_ref[...]
        m_new = jnp.maximum(m_old, jnp.max(sc, axis=1, keepdims=True))
        p = jnp.where(ok, jnp.exp(sc - m_new), 0.0)
        scale = jnp.exp(m_old - m_new)
        l_ref[...] = l_ref[...] * scale + jnp.sum(p, axis=1, keepdims=True)
        acc_ref[...] = acc_ref[...] * scale + dot(p.astype(BF16), c)
        m_ref[...] = m_new
        return carry

    lax.fori_loop(first, last, step, 0)
    o_ref[...] = (acc_ref[...] / l_ref[...]).astype(BF16)


def attend(ql, qr, keys, qseg, kseg, tok, heads):
    rows = heads * tok
    return pl.pallas_call(
        functools.partial(attend_kernel, tok, heads),
        out_shape=jax.ShapeDtypeStruct((rows, LATENT), BF16),
        in_specs=[pl.BlockSpec(memory_space=pltpu.VMEM)] * 5,
        out_specs=pl.BlockSpec(memory_space=pltpu.VMEM),
        scratch_shapes=[
            pltpu.VMEM((rows, 1), F32),
            pltpu.VMEM((rows, 1), F32),
            pltpu.VMEM((rows, LATENT), F32),
        ],
        compiler_params=pltpu.CompilerParams(vmem_limit_bytes=48 << 20),
    )(ql, qr, keys, qseg, kseg)


def local(
    hidden_in,
    attn_gain,
    w_query,
    w_latent,
    latent_gain,
    w_expand,
    w_out,
    moe_gain,
    w_gate,
    w_up,
    w_down,
    routes,
    gates,
    segment,
    page_table,
):
    tok = hidden_in.shape[0]
    heads = w_out.shape[0] // VDIM
    n_head = lax.axis_size("head")
    seq_index = lax.axis_index("seq")
    head_index = lax.axis_index("head")
    positions = seq_index * tok + jnp.arange(tok, dtype=jnp.int32)
    cosine, sine_table = rope_tables(positions, ROPE)
    residual_in = hidden_in.astype(F32)
    normed = rms_scale(residual_in, attn_gain).astype(BF16)
    latent_part = dot(normed, w_latent).astype(BF16)
    latent_raw = lax.all_gather(latent_part, "head", axis=1, tiled=True)
    compressed = rms_scale(latent_raw[:, :LATENT].astype(F32), latent_gain).astype(BF16)
    key_rope = rotate(latent_raw[:, LATENT:].astype(F32), cosine, sine_table).astype(BF16)
    latent = jnp.concatenate([compressed, key_rope], axis=1)
    part = tok // n_head
    mine = lax.dynamic_slice_in_dim(latent, head_index * part, part, 0)
    keys = lax.all_gather(mine, ("seq", "head"), axis=0, tiled=True)
    key_seg = lax.all_gather(segment, "seq", axis=0, tiled=True)

    scale = (NOPE + ROPE) ** (-0.5)
    queries = dot(normed, w_query).reshape(tok, heads, NOPE + ROPE)
    query_nope = queries[:, :, :NOPE].astype(BF16)
    query_rope = (rotate(queries[:, :, NOPE:], cosine, sine_table) * scale).astype(BF16)
    expand = w_expand.reshape(LATENT, heads, NOPE + VDIM)
    q_lat = jnp.einsum("qhd,chd->hqc", query_nope, expand[:, :, :NOPE], preferred_element_type=F32)
    q_lat = (q_lat * scale).astype(BF16).reshape(heads * tok, LATENT)
    q_rope = query_rope.transpose(1, 0, 2).reshape(heads * tok, ROPE)
    qseg = jnp.tile(segment, heads)[:, None]
    mixed = attend(q_lat, q_rope, keys, qseg, key_seg.reshape(-1, 1, KT), tok, heads)
    head_mix = jnp.einsum(
        "hqc,chd->qhd", mixed.reshape(heads, tok, LATENT), expand[:, :, NOPE:], preferred_element_type=F32
    ).astype(BF16)
    attn_part = dot(head_mix.reshape(tok, heads * VDIM), w_out).astype(BF16)
    attention = lax.psum_scatter(attn_part, "head", scatter_dimension=1, tiled=True).astype(F32)
    cols = D // n_head
    own_in = lax.dynamic_slice_in_dim(residual_in, head_index * cols, cols, 1)
    residual = (own_in + attention).astype(BF16)

    experts = lax.axis_size("seq")
    names = routes[:, :, None] == jnp.arange(experts, dtype=jnp.int32)
    picked = jnp.any(names, axis=1)
    gate_of = jnp.sum(jnp.where(names, gates[:, :, None], 0.0), axis=1)
    below = jnp.tril(jnp.ones((tok, tok), F32), -1)
    rank = dot(below.astype(BF16), picked.astype(BF16)).astype(jnp.int32)
    place = (rank.T[:, None, :] == jnp.arange(SLOTS, dtype=jnp.int32)[None, :, None]) & picked.T[:, None, :]
    send = place.astype(BF16).reshape(experts * SLOTS, tok)
    weight = jnp.where(place, gate_of.T[:, None, :], 0.0).reshape(experts * SLOTS, tok)
    outgoing = dot(send, residual).astype(BF16)
    items = lax.all_to_all(
        outgoing.reshape(experts, SLOTS, cols), "seq", split_axis=0, concat_axis=0, tiled=True
    ).reshape(experts * SLOTS, cols)
    rows = lax.all_gather(items, "head", axis=0)
    rows = rows.transpose(1, 0, 2).reshape(experts * SLOTS, D)
    moe_in = rms_scale(rows.astype(F32), moe_gain).astype(BF16)
    gate_proj = dot(moe_in, w_gate[0])
    up_proj = dot(moe_in, w_up[0])
    hidden = (jax.nn.silu(gate_proj) * up_proj).astype(BF16)
    partial_out = dot(hidden, w_down[0]).astype(BF16)
    total = lax.psum_scatter(partial_out, "head", scatter_dimension=1, tiled=True).astype(BF16)
    returned = lax.all_to_all(
        total.reshape(experts, SLOTS, cols), "seq", split_axis=0, concat_axis=0, tiled=True
    ).reshape(experts * SLOTS, cols)
    high = weight.astype(BF16)
    low = (weight - high.astype(F32)).astype(BF16)
    moe = lax.dot_general(high, returned, (((0,), (0,)), ((), ())), preferred_element_type=F32)
    moe = moe + lax.dot_general(low, returned, (((0,), (0,)), ((), ())), preferred_element_type=F32)
    out = (residual.astype(F32) + moe).astype(BF16)
    hidden_out = lax.all_gather(out, "head", axis=1, tiled=True)

    page_rows = latent.reshape(-1, PAGE * (LATENT + ROPE))
    slots_here = page_rows.shape[0] // n_head
    wanted = head_index * slots_here + jnp.arange(slots_here, dtype=jnp.int32)
    select = (page_table[0][None, :] == wanted[:, None]).astype(BF16)
    latent_cache = dot(select, page_rows).astype(BF16)
    return (hidden_out, latent_cache)


def solution(mesh):
    return jax.shard_map(
        local,
        mesh=mesh,
        in_specs=(
            P("seq", None),
            P(),
            P(None, "head"),
            P(None, "head"),
            P(),
            P(None, "head"),
            P("head", None),
            P(),
            P("seq", None, "head"),
            P("seq", None, "head"),
            P("seq", "head", None),
            P("seq", None),
            P("seq", None),
            P("seq"),
            P("seq", None),
        ),
        out_specs=(P("seq", None), P(("seq", "head"), None)),
        check_vma=False,
    )
```

```python
import functools

import jax
import jax.numpy as jnp
from jax import lax
from jax.experimental import pallas as pl
from jax.experimental.pallas import tpu as pltpu
from jax.sharding import PartitionSpec as P

D = 2048
NOPE = 128
ROPE = 64
VDIM = 128
LATENT = 512
TOPK = 6
PAGE = 32
LONGEST = 6144
SLOTS = 16
KT = 512
PART = 32
WIDTH = 640

EPS = 1e-06
THETA = 50000.0
F32 = jnp.float32
BF16 = jnp.bfloat16


def rms_scale(values, scale_gain):
    mean_sq = jnp.mean(values * values, axis=-1, keepdims=True)
    return values * lax.rsqrt(mean_sq + EPS) * scale_gain


def rope_tables(positions, feat_width):
    half_width = feat_width // 2
    inv_freq = THETA ** (-jnp.arange(half_width, dtype=F32) * 2.0 / feat_width)
    angles = positions.astype(F32)[:, None] * inv_freq[None, :]
    return (jnp.cos(angles), jnp.sin(angles))


def rotate(values, cosine, sine_table):
    half_width = values.shape[-1] // 2
    table_shape = cosine.shape[:1] + (1,) * (values.ndim - 2) + cosine.shape[1:]
    cosine = cosine.reshape(table_shape)
    sine_table = sine_table.reshape(table_shape)
    lower_half = values[..., :half_width]
    upper_half = values[..., half_width:]
    return jnp.concatenate(
        [
            lower_half * cosine - upper_half * sine_table,
            upper_half * cosine + lower_half * sine_table,
        ],
        axis=-1,
    )


def dot(a, b):
    return jnp.dot(a, b, preferred_element_type=F32)


def place_of():
    seq, head = lax.axis_index("seq"), lax.axis_index("head")
    return seq // 8, (seq // 2) % 4, (seq % 2) * 2 + head // 2, head % 2


def device(z, x, y, core):
    return (z * 8 + x * 2 + y // 2, (y % 2) * 2 + core)


def remote(src, dst, send_sem, recv_sem, target):
    return pltpu.make_async_remote_copy(
        src_ref=src, dst_ref=dst, send_sem=send_sem, recv_sem=recv_sem,
        device_id=target, device_id_type=pl.DeviceIdType.MESH,
    )


def gather_keys(mine_ref, keys, own_sem, zs, zr, ps, pr, cs, cr):
    z, x, y, core = place_of()
    partner = device(z, x, y, 1 - core)
    up = lambda v: (v + 1) % 4
    down = lambda v: (v + 3) % 4
    z_peers = [device((z + d) % 8, x, y, core) for d in range(1, 8)]
    x_peers = (device(z, up(x), y, core), device(z, down(x), y, core))
    y_peers = (device(z, x, up(y), core), device(z, x, down(y), core))
    barrier = pltpu.get_barrier_semaphore()
    for peer in z_peers + list(x_peers) + list(y_peers) + [partner]:
        pl.semaphore_signal(barrier, inc=1, device_id=peer, device_id_type=pl.DeviceIdType.MESH)
    own = pltpu.make_async_copy(mine_ref, keys.at[z, x, y, core], own_sem)
    own.start()
    pl.semaphore_wait(barrier, 12)

    z_sends = []
    for d in (4, 3, 5, 2, 6, 1, 7):
        copy = remote(mine_ref, keys.at[z, x, y, core], zs.at[d - 1], zr.at[d - 1], z_peers[d - 1])
        copy.start()
        z_sends.append(copy)
    own.wait()
    for d in range(1, 8):
        there = keys.at[(z + 8 - d) % 8, x, y, core]
        remote(there, there, zs.at[d - 1], zr.at[d - 1], partner).wait_recv()

    def pieces(c, first):
        def one(along, lo, n, step):
            if along == "x":
                return keys.at[pl.ds(lo, n), (x + step) % 4, y, c]
            return keys.at[pl.ds(lo, n), x, (y + step) % 4, c]

        def two(along, lo, n, step):
            if along == "x":
                return keys.at[pl.ds(lo, n), (x + step) % 4, :, c]
            return keys.at[pl.ds(lo, n), :, (y + step) % 4, c]

        other = "y" if first == "x" else "x"
        out = [one(first, 0, 8, 0)]
        for form, along in ((one, first), (two, other)):
            out += [form(along, 0, 8, 3), form(along, 0, 8, 1), form(along, 0, 4, 2), form(along, 4, 4, 2)]
        return out, one, two

    def run(c, first):
        mine, one, two = pieces(c, first)
        theirs = pieces(1 - c, "y" if first == "x" else "x")[0]
        sends = []

        def share(i):
            copy = remote(mine[i], mine[i], cs.at[i], cr.at[i], partner)
            copy.start()
            sends.append(copy)

        share(0)
        other = "y" if first == "x" else "x"
        for ring, (form, along) in enumerate(((one, first), (two, other))):
            right, left = x_peers if along == "x" else y_peers
            base = 4 * ring

            def push(k, region, target):
                copy = remote(region, region, ps.at[base + k], pr.at[base + k], target)
                copy.start()
                sends.append(copy)

            def arrive(k):
                region = mine[1 + base + k]
                remote(region, region, ps.at[base + k], pr.at[base + k], partner).wait_recv()

            push(0, form(along, 0, 8, 0), right)
            push(1, form(along, 0, 8, 0), left)
            arrive(0)
            push(2, form(along, 0, 4, 3), right)
            share(1 + base)
            arrive(1)
            push(3, form(along, 4, 4, 1), left)
            share(2 + base)
            arrive(2)
            share(3 + base)
            arrive(3)
            share(4 + base)
        for i, region in enumerate(theirs):
            remote(region, region, cs.at[i], cr.at[i], partner).wait_recv()
        for copy in sends:
            copy.wait_send()

    @pl.when(core == 0)
    def _():
        run(0, "x")

    @pl.when(core == 1)
    def _():
        run(1, "y")

    for copy in z_sends:
        copy.wait_send()


def attend_kernel(
    tok, heads, mine_ref, ql_ref, qr_ref, qseg_ref, o_ref,
    keys, m_ref, l_ref, acc_ref, own_sem, zs, zr, ps, pr, cs, cr,
):
    gather_keys(mine_ref, keys, own_sem, zs, zr, ps, pr, cs, cr)
    s = lax.axis_index("seq")
    rows = heads * tok
    m_ref[...] = jnp.full_like(m_ref, -1e30)
    l_ref[...] = jnp.zeros_like(l_ref)
    acc_ref[...] = jnp.zeros_like(acc_ref)
    qpos = s * tok + lax.broadcasted_iota(jnp.int32, (rows, 1), 0) % tok
    first = jnp.maximum(s * tok - (LONGEST - 1), 0) // KT
    last = (s * tok + tok - 1) // KT + 1

    def step(kt, carry):
        block = keys[kt // 2, pl.ds((kt % 2) * 2, 2)].reshape(KT, WIDTH)
        c = block[:, :LATENT]
        sc = lax.dot_general(ql_ref[...], c, (((1,), (1,)), ((), ())), preferred_element_type=F32)
        more = lax.dot_general(qr_ref[...], block[:, LATENT:], (((1,), (1,)), ((), ())), preferred_element_type=F32)
        sc = sc + more[:rows]
        kseg = more[rows : rows + 1]
        kpos = kt * KT + lax.broadcasted_iota(jnp.int32, (1, KT), 1)
        ok = (qseg_ref[...] == kseg) & (kpos <= qpos)
        sc = jnp.where(ok, sc, -1e30)
        m_old = m_ref[...]
        m_new = jnp.maximum(m_old, jnp.max(sc, axis=1, keepdims=True))
        p = jnp.where(ok, jnp.exp(sc - m_new), 0.0)
        scale = jnp.exp(m_old - m_new)
        l_ref[...] = l_ref[...] * scale + jnp.sum(p, axis=1, keepdims=True)
        acc_ref[...] = acc_ref[...] * scale + dot(p.astype(BF16), c)
        m_ref[...] = m_new
        return carry

    lax.fori_loop(first, last, step, 0)
    o_ref[...] = (acc_ref[...] / l_ref[...]).astype(BF16)


def attend(mine, ql, qr, qseg, tok, heads):
    rows = heads * tok
    dma = pltpu.SemaphoreType.DMA
    return pl.pallas_call(
        functools.partial(attend_kernel, tok, heads),
        out_shape=jax.ShapeDtypeStruct((rows, LATENT), BF16),
        in_specs=[pl.BlockSpec(memory_space=pltpu.VMEM)] * 4,
        out_specs=pl.BlockSpec(memory_space=pltpu.VMEM),
        scratch_shapes=[
            pltpu.VMEM((8, 4, 4, 2, PART, WIDTH), BF16),
            pltpu.VMEM((rows, 1), F32),
            pltpu.VMEM((rows, 1), F32),
            pltpu.VMEM((rows, LATENT), F32),
            dma(()), dma((7,)), dma((7,)), dma((8,)), dma((8,)), dma((9,)), dma((9,)),
        ],
        compiler_params=pltpu.CompilerParams(
            collective_id=0, has_side_effects=True, vmem_limit_bytes=48 << 20
        ),
    )(mine, ql, qr, qseg)


def local(
    hidden_in,
    attn_gain,
    w_query,
    w_latent,
    latent_gain,
    w_expand,
    w_out,
    moe_gain,
    w_gate,
    w_up,
    w_down,
    routes,
    gates,
    segment,
    page_table,
):
    tok = hidden_in.shape[0]
    heads = w_out.shape[0] // VDIM
    n_head = lax.axis_size("head")
    seq_index = lax.axis_index("seq")
    head_index = lax.axis_index("head")
    positions = seq_index * tok + jnp.arange(tok, dtype=jnp.int32)
    cosine, sine_table = rope_tables(positions, ROPE)
    residual_in = hidden_in.astype(F32)
    normed = rms_scale(residual_in, attn_gain).astype(BF16)
    latent_part = dot(normed, w_latent).astype(BF16)
    latent_raw = lax.all_gather(latent_part, "head", axis=1, tiled=True)
    compressed = rms_scale(latent_raw[:, :LATENT].astype(F32), latent_gain).astype(BF16)
    key_rope = rotate(latent_raw[:, LATENT:].astype(F32), cosine, sine_table).astype(BF16)
    latent = jnp.concatenate([compressed, key_rope], axis=1)
    part = tok // n_head
    tagged = jnp.concatenate(
        [latent, segment[:, None].astype(BF16), jnp.zeros((tok, WIDTH - LATENT - ROPE - 1), BF16)], axis=1
    )
    mine = lax.dynamic_slice_in_dim(tagged, head_index * part, part, 0)

    scale = (NOPE + ROPE) ** (-0.5)
    queries = dot(normed, w_query).reshape(tok, heads, NOPE + ROPE)
    query_nope = queries[:, :, :NOPE].astype(BF16)
    query_rope = (rotate(queries[:, :, NOPE:], cosine, sine_table) * scale).astype(BF16)
    expand = w_expand.reshape(LATENT, heads, NOPE + VDIM)
    q_lat = jnp.einsum("qhd,chd->hqc", query_nope, expand[:, :, :NOPE], preferred_element_type=F32)
    q_lat = (q_lat * scale).astype(BF16).reshape(heads * tok, LATENT)
    q_rope = query_rope.transpose(1, 0, 2).reshape(heads * tok, ROPE)
    pick = (jnp.arange(WIDTH - LATENT) == ROPE).astype(BF16)
    q_more = jnp.concatenate(
        [
            jnp.pad(q_rope, ((0, 0), (0, WIDTH - LATENT - ROPE))),
            jnp.broadcast_to(pick[None, :], (16, WIDTH - LATENT)),
        ],
        axis=0,
    )
    qseg = jnp.tile(segment, heads)[:, None].astype(F32)
    mixed = attend(mine, q_lat, q_more, qseg, tok, heads)
    head_mix = jnp.einsum(
        "hqc,chd->qhd", mixed.reshape(heads, tok, LATENT), expand[:, :, NOPE:], preferred_element_type=F32
    ).astype(BF16)
    attn_part = dot(head_mix.reshape(tok, heads * VDIM), w_out).astype(BF16)
    attention = lax.psum_scatter(attn_part, "head", scatter_dimension=1, tiled=True).astype(F32)
    cols = D // n_head
    own_in = lax.dynamic_slice_in_dim(residual_in, head_index * cols, cols, 1)
    residual = (own_in + attention).astype(BF16)

    experts = lax.axis_size("seq")
    names = routes[:, :, None] == jnp.arange(experts, dtype=jnp.int32)
    picked = jnp.any(names, axis=1)
    gate_of = jnp.sum(jnp.where(names, gates[:, :, None], 0.0), axis=1)
    below = jnp.tril(jnp.ones((tok, tok), F32), -1)
    rank = dot(below.astype(BF16), picked.astype(BF16)).astype(jnp.int32)
    place = (rank.T[:, None, :] == jnp.arange(SLOTS, dtype=jnp.int32)[None, :, None]) & picked.T[:, None, :]
    send = place.astype(BF16).reshape(experts * SLOTS, tok)
    weight = jnp.where(place, gate_of.T[:, None, :], 0.0).reshape(experts * SLOTS, tok)
    outgoing = dot(send, residual).astype(BF16)
    items = lax.all_to_all(
        outgoing.reshape(experts, SLOTS, cols), "seq", split_axis=0, concat_axis=0, tiled=True
    ).reshape(experts * SLOTS, cols)
    rows = lax.all_gather(items, "head", axis=0)
    rows = rows.transpose(1, 0, 2).reshape(experts * SLOTS, D)
    moe_in = rms_scale(rows.astype(F32), moe_gain).astype(BF16)
    gate_proj = dot(moe_in, w_gate[0])
    up_proj = dot(moe_in, w_up[0])
    hidden = (jax.nn.silu(gate_proj) * up_proj).astype(BF16)
    partial_out = dot(hidden, w_down[0]).astype(BF16)
    total = lax.psum_scatter(partial_out, "head", scatter_dimension=1, tiled=True).astype(BF16)
    returned = lax.all_to_all(
        total.reshape(experts, SLOTS, cols), "seq", split_axis=0, concat_axis=0, tiled=True
    ).reshape(experts * SLOTS, cols)
    high = weight.astype(BF16)
    low = (weight - high.astype(F32)).astype(BF16)
    moe = lax.dot_general(high, returned, (((0,), (0,)), ((), ())), preferred_element_type=F32)
    moe = moe + lax.dot_general(low, returned, (((0,), (0,)), ((), ())), preferred_element_type=F32)
    out = (residual.astype(F32) + moe).astype(BF16)
    hidden_out = lax.all_gather(out, "head", axis=1, tiled=True)

    page_rows = latent.reshape(-1, PAGE * (LATENT + ROPE))
    slots_here = page_rows.shape[0] // n_head
    wanted = head_index * slots_here + jnp.arange(slots_here, dtype=jnp.int32)
    select = (page_table[0][None, :] == wanted[:, None]).astype(BF16)
    latent_cache = dot(select, page_rows).astype(BF16)
    return (hidden_out, latent_cache)


def solution(mesh):
    return jax.shard_map(
        local,
        mesh=mesh,
        in_specs=(
            P("seq", None),
            P(),
            P(None, "head"),
            P(None, "head"),
            P(),
            P(None, "head"),
            P("head", None),
            P(),
            P("seq", None, "head"),
            P("seq", None, "head"),
            P("seq", "head", None),
            P("seq", None),
            P("seq", None),
            P("seq"),
            P("seq", None),
        ),
        out_specs=(P("seq", None), P(("seq", "head"), None)),
        check_vma=False,
    )
```

```python
import functools

import jax
import jax.numpy as jnp
from jax import lax
from jax.experimental import pallas as pl
from jax.experimental.pallas import tpu as pltpu
from jax.sharding import PartitionSpec as P

D = 2048
NOPE = 128
ROPE = 64
VDIM = 128
LATENT = 512
TOPK = 6
PAGE = 32
LONGEST = 6144
SLOTS = 16
KT = 512
PART = 32
WIDTH = 640

EPS = 1e-06
THETA = 50000.0
F32 = jnp.float32
BF16 = jnp.bfloat16


def rms_scale(values, scale_gain):
    mean_sq = jnp.mean(values * values, axis=-1, keepdims=True)
    return values * lax.rsqrt(mean_sq + EPS) * scale_gain


def rope_tables(positions, feat_width):
    half_width = feat_width // 2
    inv_freq = THETA ** (-jnp.arange(half_width, dtype=F32) * 2.0 / feat_width)
    angles = positions.astype(F32)[:, None] * inv_freq[None, :]
    return (jnp.cos(angles), jnp.sin(angles))


def rotate(values, cosine, sine_table):
    half_width = values.shape[-1] // 2
    table_shape = cosine.shape[:1] + (1,) * (values.ndim - 2) + cosine.shape[1:]
    cosine = cosine.reshape(table_shape)
    sine_table = sine_table.reshape(table_shape)
    lower_half = values[..., :half_width]
    upper_half = values[..., half_width:]
    return jnp.concatenate(
        [
            lower_half * cosine - upper_half * sine_table,
            upper_half * cosine + lower_half * sine_table,
        ],
        axis=-1,
    )


def dot(a, b):
    return jnp.dot(a, b, preferred_element_type=F32)


def place_of():
    seq, head = lax.axis_index("seq"), lax.axis_index("head")
    return seq // 8, (seq // 2) % 4, (seq % 2) * 2 + head // 2, head % 2


def device(z, x, y, core):
    return (z * 8 + x * 2 + y // 2, (y % 2) * 2 + core)


def remote(src, dst, send_sem, recv_sem, target):
    return pltpu.make_async_remote_copy(
        src_ref=src, dst_ref=dst, send_sem=send_sem, recv_sem=recv_sem,
        device_id=target, device_id_type=pl.DeviceIdType.MESH,
    )


def gather_keys(mine_ref, keys, own_sem, zs, zr, ps, pr, cs, cr):
    z, x, y, core = place_of()
    partner = device(z, x, y, 1 - core)
    up = lambda v: (v + 1) % 4
    down = lambda v: (v + 3) % 4
    z_peers = [device((z + d) % 8, x, y, core) for d in range(1, 8)]
    x_peers = (device(z, up(x), y, core), device(z, down(x), y, core))
    y_peers = (device(z, x, up(y), core), device(z, x, down(y), core))
    barrier = pltpu.get_barrier_semaphore()
    for peer in z_peers + list(x_peers) + list(y_peers) + [partner]:
        pl.semaphore_signal(barrier, inc=1, device_id=peer, device_id_type=pl.DeviceIdType.MESH)
    own = pltpu.make_async_copy(mine_ref, keys.at[z, x, y, core], own_sem)
    own.start()
    pl.semaphore_wait(barrier, 12)

    z_sends = []
    for d in (4, 3, 5, 2, 6, 1, 7):
        copy = remote(mine_ref, keys.at[z, x, y, core], zs.at[d - 1], zr.at[d - 1], z_peers[d - 1])
        copy.start()
        z_sends.append(copy)
    own.wait()
    for d in range(1, 8):
        there = keys.at[(z + 8 - d) % 8, x, y, core]
        remote(there, there, zs.at[d - 1], zr.at[d - 1], partner).wait_recv()

    def pieces(c, first):
        def one(along, lo, n, step):
            if along == "x":
                return keys.at[pl.ds(lo, n), (x + step) % 4, y, c]
            return keys.at[pl.ds(lo, n), x, (y + step) % 4, c]

        def two(along, lo, n, step):
            if along == "x":
                return keys.at[pl.ds(lo, n), (x + step) % 4, :, c]
            return keys.at[pl.ds(lo, n), :, (y + step) % 4, c]

        other = "y" if first == "x" else "x"
        out = [one(first, 0, 8, 0)]
        for form, along in ((one, first), (two, other)):
            out += [form(along, 0, 8, 3), form(along, 0, 8, 1), form(along, 0, 4, 2), form(along, 4, 4, 2)]
        return out, one, two

    def run(c, first):
        mine, one, two = pieces(c, first)
        theirs = pieces(1 - c, "y" if first == "x" else "x")[0]
        sends = []

        def share(i):
            copy = remote(mine[i], mine[i], cs.at[i], cr.at[i], partner)
            copy.start()
            sends.append(copy)

        share(0)
        other = "y" if first == "x" else "x"
        for ring, (form, along) in enumerate(((one, first), (two, other))):
            right, left = x_peers if along == "x" else y_peers
            base = 4 * ring

            def push(k, region, target):
                copy = remote(region, region, ps.at[base + k], pr.at[base + k], target)
                copy.start()
                sends.append(copy)

            def arrive(k):
                region = mine[1 + base + k]
                remote(region, region, ps.at[base + k], pr.at[base + k], partner).wait_recv()

            push(0, form(along, 0, 8, 0), right)
            push(1, form(along, 0, 8, 0), left)
            arrive(0)
            push(2, form(along, 0, 4, 3), right)
            share(1 + base)
            arrive(1)
            push(3, form(along, 4, 4, 1), left)
            share(2 + base)
            arrive(2)
            share(3 + base)
            arrive(3)
            share(4 + base)
        for i, region in enumerate(theirs):
            remote(region, region, cs.at[i], cr.at[i], partner).wait_recv()
        for copy in sends:
            copy.wait_send()

    @pl.when(core == 0)
    def _():
        run(0, "x")

    @pl.when(core == 1)
    def _():
        run(1, "y")

    for copy in z_sends:
        copy.wait_send()


def attend_kernel(
    tok, heads, mine_ref, ql_ref, qr_ref, qseg_ref, o_ref,
    keys, m_ref, l_ref, acc_ref, own_sem, zs, zr, ps, pr, cs, cr,
):
    gather_keys(mine_ref, keys, own_sem, zs, zr, ps, pr, cs, cr)
    s = lax.axis_index("seq")
    rows = heads * tok
    m_ref[...] = jnp.full_like(m_ref, -1e30)
    l_ref[...] = jnp.zeros_like(l_ref)
    acc_ref[...] = jnp.zeros_like(acc_ref)
    qpos = s * tok + lax.broadcasted_iota(jnp.int32, (rows, 1), 0) % tok
    first = jnp.maximum(s * tok - (LONGEST - 1), 0) // KT
    last = (s * tok + tok - 1) // KT + 1

    def step(kt, carry):
        block = keys[kt // 2, pl.ds((kt % 2) * 2, 2)].reshape(KT, WIDTH)
        c = block[:, :LATENT]
        sc = lax.dot_general(ql_ref[...], c, (((1,), (1,)), ((), ())), preferred_element_type=F32)
        more = lax.dot_general(qr_ref[...], block[:, LATENT:], (((1,), (1,)), ((), ())), preferred_element_type=F32)
        sc = sc + more[:rows]
        kseg = more[rows : rows + 1]
        kpos = kt * KT + lax.broadcasted_iota(jnp.int32, (1, KT), 1)
        ok = (qseg_ref[...] == kseg) & (kpos <= qpos)
        sc = jnp.where(ok, sc, -1e30)
        m_old = m_ref[...]
        m_new = jnp.maximum(m_old, jnp.max(sc, axis=1, keepdims=True))
        p = jnp.where(ok, jnp.exp(sc - m_new), 0.0)
        scale = jnp.exp(m_old - m_new)
        l_ref[...] = l_ref[...] * scale + jnp.sum(p, axis=1, keepdims=True)
        acc_ref[...] = acc_ref[...] * scale + dot(p.astype(BF16), c)
        m_ref[...] = m_new
        return carry

    lax.fori_loop(first, last, step, 0)
    o_ref[...] = (acc_ref[...] / l_ref[...]).astype(BF16)


def attend(mine, ql, qr, qseg, tok, heads):
    rows = heads * tok
    dma = pltpu.SemaphoreType.DMA
    return pl.pallas_call(
        functools.partial(attend_kernel, tok, heads),
        out_shape=jax.ShapeDtypeStruct((rows, LATENT), BF16),
        in_specs=[pl.BlockSpec(memory_space=pltpu.VMEM)] * 4,
        out_specs=pl.BlockSpec(memory_space=pltpu.VMEM),
        scratch_shapes=[
            pltpu.VMEM((8, 4, 4, 2, PART, WIDTH), BF16),
            pltpu.VMEM((rows, 1), F32),
            pltpu.VMEM((rows, 1), F32),
            pltpu.VMEM((rows, LATENT), F32),
            dma(()), dma((7,)), dma((7,)), dma((8,)), dma((8,)), dma((9,)), dma((9,)),
        ],
        compiler_params=pltpu.CompilerParams(
            collective_id=0, has_side_effects=True, vmem_limit_bytes=48 << 20
        ),
    )(mine, ql, qr, qseg)


ORDER = ((0, 1), (7, 2), (6, 3), (5, 4))


def experts_kernel(
    mixed_ref, expand_ref, wout_ref, own_ref, pick_ref, high_ref, low_ref, gain_ref, wg_hbm, wu_hbm, wd_hbm, o_ref,
    mix, apart, ain, res, outgoing, items, xin, wg, wu, wd, pout, cin, ysend, yin, back, ret, acc, fin,
    w_sem, own_sem, rs, rr, a0s, a0r, as_, ar, fys, fyr, fps, fpr, fqs, fqr, xs, xr, ys, yr, b0s, b0r, bs, br, es, er,
):
    z, x, y, core = place_of()
    seq, head = lax.axis_index("seq"), lax.axis_index("head")
    yl = head // 2
    here = seq % 8
    partner = (seq, yl * 2 + 1 - core)
    across = (seq, (1 - yl) * 2 + core)
    q_partner = yl * 2 + 1 - core
    q_across = (1 - yl) * 2 + core
    q_far = (1 - yl) * 2 + 1 - core
    tok = mix.shape[0]
    mesh_id = pl.DeviceIdType.MESH

    loads = [
        pltpu.make_async_copy(src.at[0], dst, w_sem.at[i])
        for i, (src, dst) in enumerate(((wg_hbm, wg), (wu_hbm, wu), (wd_hbm, wd)))
    ]
    for copy in loads:
        copy.start()

    barrier = pltpu.get_barrier_semaphore()

    def greet(k, carry):
        pl.semaphore_signal(barrier, inc=1, device_id=((seq + k) % 64, head), device_id_type=mesh_id)
        return carry

    lax.fori_loop(1, 64, greet, 0)
    for d in range(1, 4):
        pl.semaphore_signal(barrier, inc=1, device_id=(seq, (head + d) % 4), device_id_type=mesh_id)

    heads = mixed_ref.shape[0] // tok
    for h in range(heads):
        value = expand_ref[:, h * (NOPE + VDIM) + NOPE : (h + 1) * (NOPE + VDIM)]
        mix[:, h * VDIM : (h + 1) * VDIM] = dot(mixed_ref[h * tok : (h + 1) * tok, :], value).astype(BF16)
    for q in range(4):
        apart[q] = dot(mix[...], wout_ref[:, q * 512 : (q + 1) * 512]).astype(BF16)

    pl.semaphore_wait(barrier, 66)

    sends = []

    def push(src, dst, send_sem, recv_sem, target):
        copy = remote(src, dst, send_sem, recv_sem, target)
        copy.start()
        sends.append(copy)

    def arrive(region, recv_sem):
        remote(region, region, own_sem.at[2], recv_sem, partner).wait_recv()

    for d in range(1, 4):
        q = (head + d) % 4
        push(apart.at[q], ain.at[d - 1], rs.at[d - 1], rr.at[d - 1], (seq, q))
    total = apart[head].astype(F32)
    for d in range(1, 4):
        arrive(ain.at[d - 1], rr.at[d - 1])
        total = total + ain[d - 1].astype(F32)
    res[...] = (own_ref[...].astype(F32) + total).astype(BF16)

    locals_ = []
    for ja, jb in ORDER:
        for j in (ja, jb):
            zt = (z + j) % 8
            outgoing[zt] = dot(pick_ref[zt], res[...]).astype(BF16).reshape(8, SLOTS, 512)
            if j == 0:
                copy = pltpu.make_async_copy(outgoing.at[z, here], items.at[head, z, here], own_sem.at[0])
                copy.start()
                locals_.append(copy)
                for k in range(1, 8):
                    to = (here + k) % 8
                    push(
                        outgoing.at[z, to], items.at[head, z, here], a0s.at[k - 1], a0r.at[k - 1], (z * 8 + to, head)
                    )
            else:

                def send(i, carry, zt=zt, j=j):
                    remote(
                        outgoing.at[zt, i], items.at[head, z, here], as_.at[j], ar.at[j], (zt * 8 + i, head)
                    ).start()
                    return carry

                lax.fori_loop(0, 8, send, 0)

    def stage_a(g):
        for j in ORDER[g]:
            zs = (z + 8 - j) % 8
            slab = items.at[head, zs]
            if j == 0:
                locals_[0].wait()
                for k in range(1, 8):
                    arrive(items.at[head, z, (here + 8 - k) % 8], a0r.at[k - 1])
            else:
                arrive(slab, ar.at[j])
            push(slab, slab, fys.at[j], fyr.at[j], across)
            push(slab, slab, fps.at[j], fpr.at[j], partner)

    def stage_b(g):
        for j in ORDER[g]:
            slab = items.at[q_across, (z + 8 - j) % 8]
            arrive(slab, fyr.at[j])
            push(slab, slab, fqs.at[j], fqr.at[j], partner)

    def stage_c(g):
        if g == 0:
            for copy in loads:
                copy.wait()
        for t, j in enumerate(ORDER[g]):
            zs = (z + 8 - j) % 8
            arrive(items.at[q_partner, zs], fpr.at[j])
            arrive(items.at[q_far, zs], fqr.at[j])
            mean_sq = jnp.zeros((tok, 1), F32)
            for q in range(4):
                v = items[q, zs].reshape(tok, 512).astype(F32)
                mean_sq = mean_sq + jnp.sum(v * v, axis=1, keepdims=True)
            inv = lax.rsqrt(mean_sq * (1.0 / D) + EPS)
            for q in range(4):
                v = items[q, zs].reshape(tok, 512).astype(F32)
                cols = slice(q * 512, (q + 1) * 512)
                xin[t * tok : (t + 1) * tok, cols] = (v * inv * gain_ref[:, cols]).astype(BF16)
        gate = dot(xin[...], wg[...])
        up = dot(xin[...], wu[...])
        hidden = (gate / (1.0 + jnp.exp(-gate)) * up).astype(BF16)
        for q in range(4):
            part = dot(hidden, wd[:, q * 512 : (q + 1) * 512]).astype(BF16)
            for t, j in enumerate(ORDER[g]):
                pout[q, (z + 8 - j) % 8] = part[t * tok : (t + 1) * tok].reshape(8, SLOTS, 512)
        for j in ORDER[g]:
            zs = (z + 8 - j) % 8
            for side in range(2):
                push(
                    pout.at[side * 2 + 1 - core, zs], cin.at[side, zs], xs.at[side, j], xr.at[side, j], partner
                )

    def stage_d(g):
        for j in ORDER[g]:
            zs = (z + 8 - j) % 8
            for side in range(2):
                arrive(cin.at[side, zs], xr.at[side, j])
            ysend[zs] = (pout[q_across, zs].astype(F32) + cin[1 - yl, zs].astype(F32)).astype(BF16)
            push(ysend.at[zs], yin.at[zs], ys.at[j], yr.at[j], across)

    def stage_e(g):
        for j in ORDER[g]:
            zs = (z + 8 - j) % 8
            arrive(yin.at[zs], yr.at[j])
            both = pout[head, zs].astype(F32) + cin[yl, zs].astype(F32)
            back[zs] = (both + yin[zs].astype(F32)).astype(BF16)
            if j == 0:
                copy = pltpu.make_async_copy(back.at[z, here], ret.at[z, here], own_sem.at[1])
                copy.start()
                locals_.append(copy)
                for k in range(1, 8):
                    to = (here + k) % 8
                    push(back.at[z, to], ret.at[z, here], b0s.at[k - 1], b0r.at[k - 1], (z * 8 + to, head))
            else:

                def send(i, carry, zs=zs, j=j):
                    remote(back.at[zs, i], ret.at[z, here], bs.at[j], br.at[j], (zs * 8 + i, head)).start()
                    return carry

                lax.fori_loop(0, 8, send, 0)

    a, b, c, d, e = stage_a, stage_b, stage_c, stage_d, stage_e
    for stage, g in (
        (a, 0), (b, 0), (a, 1), (c, 0), (b, 1), (d, 0), (a, 2), (c, 1), (e, 0), (b, 2),
        (d, 1), (a, 3), (c, 2), (e, 1), (b, 3), (d, 2), (c, 3), (e, 2), (d, 3), (e, 3),
    ):
        stage(g)

    acc[...] = res[...].astype(F32)
    for ja, jb in ORDER:
        for j in (ja, jb):
            ze = (z + j) % 8
            if j == 0:
                locals_[1].wait()
                for k in range(1, 8):
                    arrive(ret.at[z, (here + 8 - k) % 8], b0r.at[k - 1])
            else:
                arrive(ret.at[ze], br.at[j])
            got = ret[ze].reshape(tok, 512)
            acc[...] += dot(high_ref[ze], got) + dot(low_ref[ze], got)
    fin[head] = acc[...].astype(BF16)
    push(fin.at[head], fin.at[head], es.at[0], er.at[0], across)
    push(fin.at[head], fin.at[head], es.at[1], er.at[1], partner)
    arrive(fin.at[q_across], er.at[0])
    push(fin.at[q_across], fin.at[q_across], es.at[2], er.at[2], partner)
    arrive(fin.at[q_partner], er.at[1])
    arrive(fin.at[q_far], er.at[2])
    for q in range(4):
        o_ref[:, q * 512 : (q + 1) * 512] = fin[q]
    for copy in sends:
        copy.wait_send()
    for j in range(1, 8):
        slab = outgoing.at[(z + j) % 8]
        remote(slab, slab, as_.at[j], ar.at[j], partner).wait_send()
        slab = back.at[(z + 8 - j) % 8]
        remote(slab, slab, bs.at[j], br.at[j], partner).wait_send()


def run_experts(mixed, expand, w_out, own_in, pick, high, low, gain, w_gate, w_up, w_down, tok):
    dma = pltpu.SemaphoreType.DMA
    vmem, hbm = pl.BlockSpec(memory_space=pltpu.VMEM), pl.BlockSpec(memory_space=pl.ANY)
    ff = w_gate.shape[2]
    rows = (8, 8, SLOTS, 512)
    quarter = (tok, 512)
    eight = [dma((8,))] * 2
    return pl.pallas_call(
        experts_kernel,
        out_shape=jax.ShapeDtypeStruct((tok, D), BF16),
        in_specs=[vmem] * 8 + [hbm] * 3,
        out_specs=vmem,
        scratch_shapes=[
            pltpu.VMEM((tok, 512), BF16),
            pltpu.VMEM((4,) + quarter, BF16),
            pltpu.VMEM((3,) + quarter, BF16),
            pltpu.VMEM(quarter, BF16),
            pltpu.VMEM(rows, BF16),
            pltpu.VMEM((4,) + rows, BF16),
            pltpu.VMEM((2 * tok, D), BF16),
            pltpu.VMEM((D, ff), BF16),
            pltpu.VMEM((D, ff), BF16),
            pltpu.VMEM((ff, D), BF16),
            pltpu.VMEM((4,) + rows, BF16),
            pltpu.VMEM((2,) + rows, BF16),
            pltpu.VMEM(rows, BF16),
            pltpu.VMEM(rows, BF16),
            pltpu.VMEM(rows, BF16),
            pltpu.VMEM(rows, BF16),
            pltpu.VMEM(quarter, F32),
            pltpu.VMEM((4,) + quarter, BF16),
            dma((3,)), dma((3,)), dma((3,)), dma((3,)), dma((7,)), dma((7,)),
            *eight, *eight, *eight, *eight,
            dma((2, 8)), dma((2, 8)), *eight, dma((7,)), dma((7,)), *eight, dma((3,)), dma((3,)),
        ],
        compiler_params=pltpu.CompilerParams(
            collective_id=1, has_side_effects=True, vmem_limit_bytes=56 << 20
        ),
    )(mixed, expand, w_out, own_in, pick, high, low, gain, w_gate, w_up, w_down)


def local(
    hidden_in,
    attn_gain,
    w_query,
    w_latent,
    latent_gain,
    w_expand,
    w_out,
    moe_gain,
    w_gate,
    w_up,
    w_down,
    routes,
    gates,
    segment,
    page_table,
):
    tok = hidden_in.shape[0]
    heads = w_out.shape[0] // VDIM
    n_head = lax.axis_size("head")
    seq_index = lax.axis_index("seq")
    head_index = lax.axis_index("head")
    positions = seq_index * tok + jnp.arange(tok, dtype=jnp.int32)
    cosine, sine_table = rope_tables(positions, ROPE)
    residual_in = hidden_in.astype(F32)
    normed = rms_scale(residual_in, attn_gain).astype(BF16)
    latent_part = dot(normed, w_latent).astype(BF16)
    latent_raw = lax.all_gather(latent_part, "head", axis=1, tiled=True)
    compressed = rms_scale(latent_raw[:, :LATENT].astype(F32), latent_gain).astype(BF16)
    key_rope = rotate(latent_raw[:, LATENT:].astype(F32), cosine, sine_table).astype(BF16)
    latent = jnp.concatenate([compressed, key_rope], axis=1)
    part = tok // n_head
    tagged = jnp.concatenate(
        [latent, segment[:, None].astype(BF16), jnp.zeros((tok, WIDTH - LATENT - ROPE - 1), BF16)], axis=1
    )
    mine = lax.dynamic_slice_in_dim(tagged, head_index * part, part, 0)

    scale = (NOPE + ROPE) ** (-0.5)
    queries = dot(normed, w_query).reshape(tok, heads, NOPE + ROPE)
    query_nope = queries[:, :, :NOPE].astype(BF16)
    query_rope = (rotate(queries[:, :, NOPE:], cosine, sine_table) * scale).astype(BF16)
    expand = w_expand.reshape(LATENT, heads, NOPE + VDIM)
    q_lat = jnp.einsum("qhd,chd->hqc", query_nope, expand[:, :, :NOPE], preferred_element_type=F32)
    q_lat = (q_lat * scale).astype(BF16).reshape(heads * tok, LATENT)
    q_rope = query_rope.transpose(1, 0, 2).reshape(heads * tok, ROPE)
    pick = (jnp.arange(WIDTH - LATENT) == ROPE).astype(BF16)
    q_more = jnp.concatenate(
        [
            jnp.pad(q_rope, ((0, 0), (0, WIDTH - LATENT - ROPE))),
            jnp.broadcast_to(pick[None, :], (16, WIDTH - LATENT)),
        ],
        axis=0,
    )
    qseg = jnp.tile(segment, heads)[:, None].astype(F32)
    mixed = attend(mine, q_lat, q_more, qseg, tok, heads)
    cols = D // n_head
    own_in = lax.dynamic_slice_in_dim(hidden_in, head_index * cols, cols, 1)
    experts = lax.axis_size("seq")
    names = routes[:, :, None] == jnp.arange(experts, dtype=jnp.int32)
    picked = jnp.any(names, axis=1)
    gate_of = jnp.sum(jnp.where(names, gates[:, :, None], 0.0), axis=1)
    below = jnp.tril(jnp.ones((tok, tok), F32), -1)
    rank = dot(below.astype(BF16), picked.astype(BF16)).astype(jnp.int32)
    slots = jnp.arange(SLOTS, dtype=jnp.int32)
    place = (rank.T[:, None, :] == slots[None, :, None]) & picked.T[:, None, :]
    pick = place.astype(BF16).reshape(8, experts // 8 * SLOTS, tok)
    ranks = rank.reshape(tok, 8, 8).transpose(1, 0, 2)
    taken = picked.reshape(tok, 8, 8).transpose(1, 0, 2)
    gated = gate_of.reshape(tok, 8, 8).transpose(1, 0, 2)
    weight = jnp.where((ranks[..., None] == slots) & taken[..., None], gated[..., None], 0.0)
    weight = weight.reshape(8, tok, 8 * SLOTS)
    high = weight.astype(BF16)
    low = (weight - high.astype(F32)).astype(BF16)
    hidden_out = run_experts(
        mixed, w_expand, w_out, own_in, pick, high, low, moe_gain[None, :], w_gate, w_up, w_down, tok
    )

    page_rows = latent.reshape(-1, PAGE * (LATENT + ROPE))
    slots_here = page_rows.shape[0] // n_head
    wanted = head_index * slots_here + jnp.arange(slots_here, dtype=jnp.int32)
    select = (page_table[0][None, :] == wanted[:, None]).astype(BF16)
    latent_cache = dot(select, page_rows).astype(BF16)
    return (hidden_out, latent_cache)


def solution(mesh):
    return jax.shard_map(
        local,
        mesh=mesh,
        in_specs=(
            P("seq", None),
            P(),
            P(None, "head"),
            P(None, "head"),
            P(),
            P(None, "head"),
            P("head", None),
            P(),
            P("seq", None, "head"),
            P("seq", None, "head"),
            P("seq", "head", None),
            P("seq", None),
            P("seq", None),
            P("seq"),
            P("seq", None),
        ),
        out_specs=(P("seq", None), P(("seq", "head"), None)),
        check_vma=False,
    )
```

```python
import jax
import jax.numpy as jnp
from jax import lax
from jax.experimental import pallas as pl
from jax.experimental.pallas import tpu as pltpu
from jax.sharding import PartitionSpec as P

D = 2048
NOPE = 128
ROPE = 64
VDIM = 128
LATENT = 512
TOPK = 6
TOK = 128
HEADS = 4
LONGEST = 6144
SLOTS = 16
KT = 512
PART = 32
WIDTH = 640

EPS = 1e-06
THETA = 50000.0
F32 = jnp.float32
BF16 = jnp.bfloat16


def rope_tables(positions, feat_width):
    half_width = feat_width // 2
    inv_freq = THETA ** (-jnp.arange(half_width, dtype=F32) * 2.0 / feat_width)
    angles = positions.astype(F32)[:, None] * inv_freq[None, :]
    return (jnp.cos(angles), jnp.sin(angles))


def dot(a, b):
    return jnp.dot(a, b, preferred_element_type=F32)


ORDER = ((0, 1), (7, 2), (6, 3), (5, 4))


def nt(a, b):
    return lax.dot_general(a, b, (((1,), (1,)), ((), ())), preferred_element_type=F32)


def place_of():
    seq, head = lax.axis_index("seq"), lax.axis_index("head")
    return seq // 8, (seq // 2) % 4, (seq % 2) * 2 + head // 2, head % 2


def device(z, x, y, core):
    return (z * 8 + x * 2 + y // 2, (y % 2) * 2 + core)


def remote(src, dst, send_sem, recv_sem, target):
    return pltpu.make_async_remote_copy(
        src_ref=src, dst_ref=dst, send_sem=send_sem, recv_sem=recv_sem,
        device_id=target, device_id_type=pl.DeviceIdType.MESH,
    )


def gather_keys(mine_ref, keys, work, own_sem, zs, zr, ps, pr, cs, cr):
    z, x, y, core = place_of()
    partner = device(z, x, y, 1 - core)
    up = lambda v: (v + 1) % 4
    down = lambda v: (v + 3) % 4
    z_peers = [device((z + d) % 8, x, y, core) for d in range(1, 8)]
    x_peers = (device(z, up(x), y, core), device(z, down(x), y, core))
    y_peers = (device(z, x, up(y), core), device(z, x, down(y), core))
    own = pltpu.make_async_copy(mine_ref, keys.at[z, x, y, core], own_sem)
    own.start()
    z_sends = []
    for d in (4, 3, 5, 2, 6, 1, 7):
        copy = remote(mine_ref, keys.at[z, x, y, core], zs.at[d - 1], zr.at[d - 1], z_peers[d - 1])
        copy.start()
        z_sends.append(copy)
    work()
    own.wait()
    for d in range(1, 8):
        there = keys.at[(z + 8 - d) % 8, x, y, core]
        remote(there, there, zs.at[d - 1], zr.at[d - 1], partner).wait_recv()

    def pieces(c, first):
        def one(along, lo, n, step):
            if along == "x":
                return keys.at[pl.ds(lo, n), (x + step) % 4, y, c]
            return keys.at[pl.ds(lo, n), x, (y + step) % 4, c]

        def two(along, lo, n, step):
            if along == "x":
                return keys.at[pl.ds(lo, n), (x + step) % 4, :, c]
            return keys.at[pl.ds(lo, n), :, (y + step) % 4, c]

        other = "y" if first == "x" else "x"
        out = [one(first, 0, 8, 0)]
        for form, along in ((one, first), (two, other)):
            out += [form(along, 0, 8, 3), form(along, 0, 8, 1), form(along, 0, 4, 2), form(along, 4, 4, 2)]
        return out, one, two

    def run(c, first):
        mine, one, two = pieces(c, first)
        theirs = pieces(1 - c, "y" if first == "x" else "x")[0]
        sends = []

        def share(i):
            copy = remote(mine[i], mine[i], cs.at[i], cr.at[i], partner)
            copy.start()
            sends.append(copy)

        share(0)
        other = "y" if first == "x" else "x"
        for ring, (form, along) in enumerate(((one, first), (two, other))):
            right, left = x_peers if along == "x" else y_peers
            base = 4 * ring

            def push(k, region, target):
                copy = remote(region, region, ps.at[base + k], pr.at[base + k], target)
                copy.start()
                sends.append(copy)

            def arrive(k):
                region = mine[1 + base + k]
                remote(region, region, ps.at[base + k], pr.at[base + k], partner).wait_recv()

            push(0, form(along, 0, 8, 0), right)
            push(1, form(along, 0, 8, 0), left)
            arrive(0)
            push(2, form(along, 0, 4, 3), right)
            share(1 + base)
            arrive(1)
            push(3, form(along, 4, 4, 1), left)
            share(2 + base)
            arrive(2)
            share(3 + base)
            arrive(3)
            share(4 + base)
        for i, region in enumerate(theirs):
            remote(region, region, cs.at[i], cr.at[i], partner).wait_recv()
        for copy in sends:
            copy.wait_send()

    @pl.when(core == 0)
    def _():
        run(0, "x")

    @pl.when(core == 1)
    def _():
        run(1, "y")

    for copy in z_sends:
        copy.wait_send()


def rotated(tile, cos, sin):
    lane = lax.broadcasted_iota(jnp.int32, tile.shape, 1)
    swapped = jnp.where(lane < ROPE // 2, pltpu.roll(tile, 96, 1), pltpu.roll(tile, 32, 1))
    return tile * cos + swapped * sin


def layer_kernel(
    hid_ref, again_ref, lgain_ref, mgain_ref, cos_ref, sin_ref, seg_ref, routes_ref, gates_ref, pages_ref,
    wl_hbm, wq_hbm, we_hbm, wo_hbm, wg_hbm, wu_hbm, wd_hbm, o_ref, cache_ref,
    wl, wq, we, wo, wg, wu, wd, normed, lpart, lall, tagged, keys, ql, qm, qbuf, m_ref, l_ref, acc_ref, mixed,
    pick, high, low, mix, apart, ain, res, outgoing, items, xin, pout, cin, ysend, yin, back, ret, acc, fin,
    w_sem, own_sem, ls, lr, zs_, zr_, ps, pr, cs, cr,
    rs, rr, a0s, a0r, as_, ar, fys, fyr, fps, fpr, fqs, fqr, xs, xr, ys, yr, b0s, b0r, bs, br, es, er,
):
    z, x, y, core = place_of()
    seq, head = lax.axis_index("seq"), lax.axis_index("head")
    yl, yh = head // 2, seq % 2
    partner = (seq, yl * 2 + 1 - core)
    across = (seq, (1 - yl) * 2 + core)
    q_partner = yl * 2 + 1 - core
    q_across = (1 - yl) * 2 + core
    q_far = (1 - yl) * 2 + 1 - core
    tok = TOK
    mesh_id = pl.DeviceIdType.MESH
    half_y = (y, 3 - y)
    half_h = (yh, 1 - yh)

    loads = [
        pltpu.make_async_copy(src, dst, w_sem.at[i])
        for i, (src, dst) in enumerate(
            (
                (wl_hbm, wl), (wq_hbm, wq), (we_hbm, we), (wo_hbm, wo),
                (wg_hbm.at[0], wg), (wu_hbm.at[0], wu), (wd_hbm.at[0], wd),
            )
        )
    ]
    for copy in loads:
        copy.start()

    barrier = pltpu.get_barrier_semaphore()
    column = z * 4 + x

    def greet(half, k):
        at = (column + k) % 32
        pl.semaphore_signal(
            barrier, inc=1, device_id=device(at // 4, at % 4, half_y[half], core), device_id_type=mesh_id
        )

    def greet_both(k, carry):
        greet(0, k)
        greet(1, k)
        return carry

    greet(1, 0)
    for d in range(1, 4):
        pl.semaphore_signal(barrier, inc=1, device_id=(seq, (head + d) % 4), device_id_type=mesh_id)
    lax.fori_loop(1, 32, greet_both, 0)

    sends = []

    def push(src, dst, send_sem, recv_sem, target):
        copy = remote(src, dst, send_sem, recv_sem, target)
        copy.start()
        sends.append(copy)

    def arrive(region, recv_sem):
        remote(region, region, own_sem.at[2], recv_sem, partner).wait_recv()

    v = hid_ref[...].astype(F32)
    inv = lax.rsqrt(jnp.sum(v * v, axis=1, keepdims=True) * (1.0 / D) + EPS)
    normed[...] = (v * inv * again_ref[...]).astype(BF16)
    lpart[...] = jnp.zeros_like(lpart)
    loads[0].wait()
    lpart[:, :144] = nt(normed[...], wl[...]).astype(BF16)
    pl.semaphore_wait(barrier, 66)

    for d in range(1, 4):
        push(lpart, lall.at[d - 1], ls.at[d - 1], lr.at[d - 1], (seq, (head + d) % 4))
    place_r = lax.broadcasted_iota(jnp.int32, (256, WIDTH), 0)
    place_c = lax.broadcasted_iota(jnp.int32, (256, WIDTH), 1)

    def spread(part, q):
        put = ((place_c == q * 144 + place_r) & (place_r < 144)).astype(F32).astype(BF16)
        return dot(part, put)

    raw = spread(lpart[...], head)
    for d in range(1, 4):
        arrive(lall.at[d - 1], lr.at[d - 1])
        raw = raw + spread(lall[d - 1], (head + 4 - d) % 4)
    comp = raw[:, :LATENT]
    inv = lax.rsqrt(jnp.sum(comp * comp, axis=1, keepdims=True) * (1.0 / LATENT) + EPS)
    tagged[:, :LATENT] = (comp * inv * lgain_ref[...]).astype(BF16)
    turned = rotated(raw[:, LATENT:], cos_ref[...], sin_ref[...])
    lane = lax.broadcasted_iota(jnp.int32, (tok, 128), 1)
    tagged[:, LATENT:] = jnp.where(lane == ROPE, seg_ref[...], turned).astype(BF16)

    scale = (NOPE + ROPE) ** (-0.5)

    def work():
        page = jnp.zeros((PART, WIDTH), BF16)
        for p in range(4):
            page = jnp.where(pages_ref[:, p : p + 1] == head, tagged[p * PART : (p + 1) * PART, :], page)
        cache_ref[...] = page[:, : LATENT + ROPE]
        loads[1].wait()
        qbuf[...] = dot(normed[...], wq[...])
        loads[2].wait()
        for k in range(HEADS // 2):
            t0 = qbuf[:, k * 384 : k * 384 + 128]
            t1 = qbuf[:, k * 384 + 128 : k * 384 + 256]
            t2 = pltpu.roll(qbuf[:, k * 384 + 256 : k * 384 + 384], 64, 1)
            nope = (t0, jnp.where(lane < 64, pltpu.roll(t1, 64, 1), t2))
            rope = (t1, t2)
            for i in range(2):
                h = 2 * k + i
                rows = slice(h * tok, (h + 1) * tok)
                key_w = we[:, h * (NOPE + VDIM) : h * (NOPE + VDIM) + NOPE]
                ql[rows, :] = (nt(nope[i].astype(BF16), key_w) * scale).astype(BF16)
                qm[rows, :] = (rotated(rope[i], cos_ref[...], sin_ref[...]) * scale).astype(BF16)
        qm[HEADS * tok :, :] = (lax.broadcasted_iota(jnp.int32, (16, 128), 1) == ROPE).astype(F32).astype(BF16)
        row = lax.broadcasted_iota(jnp.int32, (tok, 128), 0)
        below = (lane < row).astype(F32).astype(BF16)
        cell = lane // SLOTS
        slot = (lane % SLOTS).astype(F32)

        def table(ze, carry):
            expert = ze * 8 + (cell % 4) * 2 + cell // 4
            taken = jnp.zeros((tok, 128), F32)
            gate = jnp.zeros((tok, 128), F32)
            for j in range(TOPK):
                hit = routes_ref[:, j : j + 1] == expert
                taken = jnp.where(hit, 1.0, taken)
                gate = jnp.where(hit, gates_ref[:, j : j + 1], gate)
            rank = dot(below, taken.astype(BF16))
            put = (taken > 0.5) & (rank == slot)
            weight = jnp.where(put, gate, 0.0)
            top = weight.astype(BF16)
            high[ze] = top
            low[ze] = (weight - top.astype(F32)).astype(BF16)
            pick[ze] = put.astype(F32).T.astype(BF16)
            return carry

        lax.fori_loop(0, 8, table, 0)

    mine = tagged.at[pl.ds(pl.multiple_of(head * PART, PART), PART)]
    gather_keys(mine, keys, work, own_sem.at[3], zs_, zr_, ps, pr, cs, cr)

    rows = HEADS * tok
    m_ref[...] = jnp.full_like(m_ref, -1e30)
    l_ref[...] = jnp.zeros_like(l_ref)
    acc_ref[...] = jnp.zeros_like(acc_ref)
    qpos = seq * tok + lax.broadcasted_iota(jnp.int32, (rows, 1), 0) % tok
    qseg = jnp.concatenate([seg_ref[...]] * HEADS, axis=0)
    first = jnp.maximum(seq * tok - (LONGEST - 1), 0) // KT
    last = (seq * tok + tok - 1) // KT + 1

    def step(kt, carry):
        block = keys[kt // 2, pl.ds((kt % 2) * 2, 2)].reshape(KT, WIDTH)
        c = block[:, :LATENT]
        more = nt(qm[...], block[:, LATENT:])
        sc = nt(ql[...], c) + more[:rows]
        kseg = more[rows : rows + 1]
        kpos = kt * KT + lax.broadcasted_iota(jnp.int32, (1, KT), 1)
        ok = (qseg == kseg) & (kpos <= qpos)
        sc = jnp.where(ok, sc, -1e30)
        m_old = m_ref[...]
        m_new = jnp.maximum(m_old, jnp.max(sc, axis=1, keepdims=True))
        p = jnp.where(ok, jnp.exp(sc - m_new), 0.0)
        fade = jnp.exp(m_old - m_new)
        l_ref[...] = l_ref[...] * fade + jnp.sum(p, axis=1, keepdims=True)
        acc_ref[...] = acc_ref[...] * fade + dot(p.astype(BF16), c)
        m_ref[...] = m_new
        return carry

    lax.fori_loop(first, last, step, 0)
    mixed[...] = (acc_ref[...] / l_ref[...]).astype(BF16)

    for h in range(HEADS):
        value = we[:, h * (NOPE + VDIM) + NOPE : (h + 1) * (NOPE + VDIM)]
        mix[:, h * VDIM : (h + 1) * VDIM] = dot(mixed[h * tok : (h + 1) * tok, :], value).astype(BF16)
    loads[3].wait()
    for q in range(4):
        apart[q] = dot(mix[...], wo[:, q * 512 : (q + 1) * 512]).astype(BF16)
    for d in range(1, 4):
        q = (head + d) % 4
        push(apart.at[q], ain.at[d - 1], rs.at[d - 1], rr.at[d - 1], (seq, q))
    total = apart[head].astype(F32)
    for d in range(1, 4):
        arrive(ain.at[d - 1], rr.at[d - 1])
        total = total + ain[d - 1].astype(F32)
    own = hid_ref[:, pl.ds(pl.multiple_of(head * 512, 512), 512)].astype(F32)
    res[...] = (own + total).astype(BF16)

    locals_ = []

    def send_slab(src, dst, slab, j, send0, recv0, send_sem, recv_sem, local_sem):
        for half in range(2):
            if half == 0 and j == 0:
                copy = pltpu.make_async_copy(src.at[slab, yh, x], dst.at[z, yh, x], local_sem)
                copy.start()
                locals_.append(copy)
                for k in range(1, 4):
                    xt = (x + k) % 4
                    push(
                        src.at[slab, yh, xt], dst.at[z, yh, x], send0.at[k - 1], recv0.at[k - 1],
                        device(slab, xt, y, core),
                    )
            else:

                def send(xt, carry, half=half):
                    remote(
                        src.at[slab, half_h[half], xt], dst.at[z, yh, x], send_sem.at[half, j], recv_sem.at[half, j],
                        device(slab, xt, half_y[half], core),
                    ).start()
                    return carry

                lax.fori_loop(0, 4, send, 0)

    def slab_sent(src, slab, j, send_sem):
        for half in range(2):
            if half or j:
                part = src.at[slab, half_h[half]]
                remote(part, part, send_sem.at[half, j], own_sem.at[2], partner).wait_send()

    def slab_arrived(parts, j, recv0, recv_sem, local):
        for half in range(2):
            if half == 0 and j == 0:
                locals_[local].wait()
                for k in range(1, 4):
                    arrive(parts[0].at[(x + 4 - k) % 4], recv0.at[k - 1])
            else:
                arrive(parts[half], recv_sem.at[half, j])

    for pair in ORDER:
        for j in pair:
            zt = (z + j) % 8
            outgoing[zt] = dot(pick[zt], res[...]).astype(BF16).reshape(2, 4, SLOTS, 512)
            send_slab(outgoing, items.at[head], zt, j, a0s, a0r, as_, ar, own_sem.at[0])

    def stage_a(g):
        for j in ORDER[g]:
            zs = (z + 8 - j) % 8
            parts = (items.at[head, zs, yh], items.at[q_across, zs, 1 - yh])
            slab_arrived(parts, j, a0r, ar, 0)
            for half in range(2):
                push(parts[half], parts[half], fys.at[half, j], fyr.at[half, j], across)
                push(parts[half], parts[half], fps.at[half, j], fpr.at[half, j], partner)

    def stage_b(g):
        for j in ORDER[g]:
            zs = (z + 8 - j) % 8
            for half, part in enumerate((items.at[q_across, zs, yh], items.at[head, zs, 1 - yh])):
                arrive(part, fyr.at[half, j])
                push(part, part, fqs.at[half, j], fqr.at[half, j], partner)

    def stage_c(g):
        if g == 0:
            for copy in loads[4:]:
                copy.wait()
        for t, j in enumerate(ORDER[g]):
            zs = (z + 8 - j) % 8
            arrive(items.at[q_partner, zs, yh], fpr.at[0, j])
            arrive(items.at[q_far, zs, 1 - yh], fpr.at[1, j])
            arrive(items.at[q_far, zs, yh], fqr.at[0, j])
            arrive(items.at[q_partner, zs, 1 - yh], fqr.at[1, j])
            mean_sq = jnp.zeros((tok, 1), F32)
            for q in range(4):
                v = items[q, zs].reshape(tok, 512).astype(F32)
                mean_sq = mean_sq + jnp.sum(v * v, axis=1, keepdims=True)
            inv = lax.rsqrt(mean_sq * (1.0 / D) + EPS)
            for q in range(4):
                v = items[q, zs].reshape(tok, 512).astype(F32)
                cols = slice(q * 512, (q + 1) * 512)
                xin[t * tok : (t + 1) * tok, cols] = (v * inv * mgain_ref[:, cols]).astype(BF16)
        gate = nt(xin[...], wg[...])
        up = nt(xin[...], wu[...])
        hidden = (gate / (1.0 + jnp.exp(-gate)) * up).astype(BF16)
        for q in range(4):
            part = dot(hidden, wd[:, q * 512 : (q + 1) * 512]).astype(BF16)
            for t, j in enumerate(ORDER[g]):
                pout[q, (z + 8 - j) % 8] = part[t * tok : (t + 1) * tok].reshape(2, 4, SLOTS, 512)
        for j in ORDER[g]:
            zs = (z + 8 - j) % 8
            for side in range(2):
                push(
                    pout.at[side * 2 + 1 - core, zs], cin.at[side, zs], xs.at[side, j], xr.at[side, j], partner
                )

    def chip_sum(side, zs, h):
        return pout[side * 2 + core, zs, h].astype(F32) + cin[side, zs, h].astype(F32)

    def stage_d(g):
        for j in ORDER[g]:
            zs = (z + 8 - j) % 8
            for side in range(2):
                arrive(cin.at[side, zs], xr.at[side, j])
            ysend[zs, yh] = chip_sum(1 - yl, zs, yh).astype(BF16)
            ysend[zs, 1 - yh] = chip_sum(yl, zs, 1 - yh).astype(BF16)
            push(ysend.at[zs], yin.at[zs], ys.at[j], yr.at[j], across)

    def stage_e(g):
        for j in ORDER[g]:
            zs = (z + 8 - j) % 8
            arrive(yin.at[zs], yr.at[j])
            back[zs, yh] = (chip_sum(yl, zs, yh) + yin[zs, yh].astype(F32)).astype(BF16)
            back[zs, 1 - yh] = (chip_sum(1 - yl, zs, 1 - yh) + yin[zs, 1 - yh].astype(F32)).astype(BF16)
            send_slab(back, ret, zs, j, b0s, b0r, bs, br, own_sem.at[1])

    a, b, c, d, e = stage_a, stage_b, stage_c, stage_d, stage_e
    for stage, g in (
        (a, 0), (b, 0), (a, 1), (c, 0), (b, 1), (d, 0), (a, 2), (c, 1), (e, 0), (b, 2),
        (d, 1), (a, 3), (c, 2), (e, 1), (b, 3), (d, 2), (c, 3), (e, 2), (d, 3), (e, 3),
    ):
        stage(g)

    acc[...] = res[...].astype(F32)
    for pair in ORDER:
        for j in pair:
            ze = (z + j) % 8
            slab_arrived((ret.at[ze, yh], ret.at[ze, 1 - yh]), j, b0r, br, 1)
            got = ret[ze].reshape(tok, 512)
            acc[...] += dot(high[ze], got) + dot(low[ze], got)
    fin[head] = acc[...].astype(BF16)
    push(fin.at[head], fin.at[head], es.at[0], er.at[0], across)
    push(fin.at[head], fin.at[head], es.at[1], er.at[1], partner)
    arrive(fin.at[q_across], er.at[0])
    push(fin.at[q_across], fin.at[q_across], es.at[2], er.at[2], partner)
    arrive(fin.at[q_partner], er.at[1])
    arrive(fin.at[q_far], er.at[2])
    for q in range(4):
        o_ref[:, q * 512 : (q + 1) * 512] = fin[q]
    for copy in sends:
        copy.wait_send()
    for j in range(8):
        slab_sent(outgoing, (z + j) % 8, j, as_)
        slab_sent(back, (z + 8 - j) % 8, j, bs)


def local(
    hidden_in,
    attn_gain,
    w_query,
    w_latent,
    latent_gain,
    w_expand,
    w_out,
    moe_gain,
    w_gate,
    w_up,
    w_down,
    routes,
    gates,
    segment,
    page_table,
):
    positions = lax.axis_index("seq") * TOK + jnp.arange(TOK, dtype=jnp.int32)
    cosine, sine = rope_tables(positions, ROPE)
    rest = jnp.zeros((TOK, 128 - ROPE), F32)
    cos = jnp.concatenate([cosine, cosine, rest], axis=1)
    sin = jnp.concatenate([-sine, sine, rest], axis=1)
    ff = w_gate.shape[2]
    dma = pltpu.SemaphoreType.DMA
    vmem, hbm = pl.BlockSpec(memory_space=pltpu.VMEM), pl.BlockSpec(memory_space=pl.ANY)
    chunks = (8, 2, 4, SLOTS, 512)
    quarter = (TOK, 512)
    rows = HEADS * TOK
    tables = (8, 128, 128)

    def space(*shape):
        return pltpu.VMEM(shape, BF16)

    def two(*shape):
        return [dma(shape), dma(shape)]

    hidden_out, page = pl.pallas_call(
        layer_kernel,
        out_shape=(
            jax.ShapeDtypeStruct((TOK, D), BF16),
            jax.ShapeDtypeStruct((PART, LATENT + ROPE), BF16),
        ),
        in_specs=[vmem] * 10 + [hbm] * 7,
        out_specs=(vmem, vmem),
        scratch_shapes=[
            space(144, D), space(D, 768), space(LATENT, 1024), space(512, D), space(ff, D), space(ff, D),
            space(ff, D), space(TOK, D), space(TOK, 256), space(3, TOK, 256), space(TOK, WIDTH),
            space(8, 4, 4, 2, PART, WIDTH), space(rows, LATENT), space(rows + 16, 128),
            pltpu.VMEM((TOK, 768), F32), pltpu.VMEM((rows, 1), F32), pltpu.VMEM((rows, 1), F32),
            pltpu.VMEM((rows, LATENT), F32), space(rows, LATENT),
            space(*tables), space(*tables), space(*tables), space(*quarter), space(4, *quarter),
            space(3, *quarter), space(*quarter), space(*chunks), space(4, *chunks), space(2 * TOK, D),
            space(4, *chunks), space(2, *chunks), space(*chunks), space(*chunks), space(*chunks), space(*chunks),
            pltpu.VMEM(quarter, F32), space(4, *quarter),
            dma((7,)), dma((4,)), *two(3), *two(7), *two(8), *two(9),
            *two(3), *two(3), *two(2, 8), *two(2, 8), *two(2, 8), *two(2, 8), *two(2, 8), *two(8),
            *two(3), *two(2, 8), *two(3),
        ],
        compiler_params=pltpu.CompilerParams(
            collective_id=0, has_side_effects=True, vmem_limit_bytes=60 << 20
        ),
    )(
        hidden_in,
        attn_gain[None, :],
        latent_gain[None, :],
        moe_gain[None, :],
        cos,
        sin,
        segment[:, None].astype(F32),
        routes,
        gates,
        page_table,
        w_latent.T,
        w_query,
        w_expand,
        w_out,
        w_gate.transpose(0, 2, 1),
        w_up.transpose(0, 2, 1),
        w_down,
    )
    return (hidden_out, page.reshape(1, PART * (LATENT + ROPE)))


def solution(mesh):
    return jax.shard_map(
        local,
        mesh=mesh,
        in_specs=(
            P("seq", None),
            P(),
            P(None, "head"),
            P(None, "head"),
            P(),
            P(None, "head"),
            P("head", None),
            P(),
            P("seq", None, "head"),
            P("seq", None, "head"),
            P("seq", "head", None),
            P("seq", None),
            P("seq", None),
            P("seq"),
            P("seq", None),
        ),
        out_specs=(P("seq", None), P(("seq", "head"), None)),
        check_vma=False,
    )
```

```python
import jax
import jax.numpy as jnp
from jax import lax
from jax.experimental import pallas as pl
from jax.experimental.pallas import tpu as pltpu
from jax.sharding import PartitionSpec as P

D = 2048
NOPE = 128
ROPE = 64
VDIM = 128
LATENT = 512
TOPK = 6
TOK = 128
HEADS = 4
SLOTS = 16
PART = 32
WIDTH = 640

EPS = 1e-06
THETA = 50000.0
F32 = jnp.float32
BF16 = jnp.bfloat16


def rope_tables(positions, feat_width):
    half_width = feat_width // 2
    inv_freq = THETA ** (-jnp.arange(half_width, dtype=F32) * 2.0 / feat_width)
    angles = positions.astype(F32)[:, None] * inv_freq[None, :]
    return (jnp.cos(angles), jnp.sin(angles))


def dot(a, b):
    return jnp.dot(a, b, preferred_element_type=F32)


ORDER = ((0, 1), (7, 2), (6, 3), (5, 4))


def nt(a, b):
    return lax.dot_general(a, b, (((1,), (1,)), ((), ())), preferred_element_type=F32)


def place_of():
    seq, head = lax.axis_index("seq"), lax.axis_index("head")
    return seq // 8, (seq // 2) % 4, (seq % 2) * 2 + head // 2, head % 2


def device(z, x, y, core):
    return (z * 8 + x * 2 + y // 2, (y % 2) * 2 + core)


def remote(src, dst, send_sem, recv_sem, target):
    return pltpu.make_async_remote_copy(
        src_ref=src, dst_ref=dst, send_sem=send_sem, recv_sem=recv_sem,
        device_id=target, device_id_type=pl.DeviceIdType.MESH,
    )


NEAR = 7
HALVES = ((0, 4), (4, 3))


class KeyGather:
    def __init__(self, keys, own_sem, zs, zr, ps, pr, cs, cr):
        self.keys, self.own_sem = keys, own_sem
        self.zs, self.zr, self.ps, self.pr, self.cs, self.cr = zs, zr, ps, pr, cs, cr
        self.z, self.x, self.y, self.core = place_of()
        self.partner = device(self.z, self.x, self.y, 1 - self.core)

    def both(self, act):
        @pl.when(self.core == 0)
        def _():
            act(0)

        @pl.when(self.core == 1)
        def _():
            act(1)

    def region(self, c, ring, lo, n, step):
        along_x = (c == 0) == (ring == 0)
        planes = pl.ds(lo, n)
        if along_x:
            at = (self.x + step) % 4
            return self.keys.at[planes, at, self.y, c] if ring == 0 else self.keys.at[planes, at, :, c]
        at = (self.y + step) % 4
        return self.keys.at[planes, self.x, at, c] if ring == 0 else self.keys.at[planes, :, at, c]

    def piece(self, c, i):
        if i == 0:
            return self.region(c, 0, 0, NEAR, 0)
        lo, n, step = ((0, NEAR, 3), (0, NEAR, 1), (*HALVES[0], 2), (*HALVES[1], 2))[(i - 1) % 4]
        return self.region(c, (i - 1) // 4, lo, n, step)

    def share(self, c, i):
        part = self.piece(c, i)
        return remote(part, part, self.cs.at[i], self.cr.at[i], self.partner)

    def shared(self, c, i):
        part = self.piece(1 - c, i)
        remote(part, part, self.cs.at[i], self.cr.at[i], self.partner).wait_recv()

    def push(self, c, ring, k):
        along_x = (c == 0) == (ring == 0)
        x, y, z = self.x, self.y, self.z
        turn = 1 if k in (0, 2) else 3
        to = device(z, (x + turn) % 4, y, self.core) if along_x else device(z, x, (y + turn) % 4, self.core)
        lo, n, step = ((0, NEAR, 0), (0, NEAR, 0), (*HALVES[0], 3), (*HALVES[1], 1))[k]
        part = self.region(c, ring, lo, n, step)
        return remote(part, part, self.ps.at[4 * ring + k], self.pr.at[4 * ring + k], to)

    def arrive(self, c, ring, k):
        part = self.piece(c, 1 + 4 * ring + k)
        remote(part, part, self.ps.at[4 * ring + k], self.pr.at[4 * ring + k], self.partner).wait_recv()

    def along_z(self, mine_ref):
        slot = lambda r: self.keys.at[r, self.x, self.y, self.core]
        own = pltpu.make_async_copy(mine_ref, slot(NEAR - 1), self.own_sem)
        own.start()
        copies = []
        for d in (4, 3, 5, 2, 6, 1):
            to = device((self.z + d) % 8, self.x, self.y, self.core)
            copy = remote(mine_ref, slot(NEAR - 1 - d), self.zs.at[d - 1], self.zr.at[d - 1], to)
            copy.start()
            copies.append(copy)
        yield
        own.wait()
        for copy in copies:
            copy.wait_send()
        for d in range(1, NEAR):
            there = slot(NEAR - 1 - d)
            remote(there, there, self.zs.at[d - 1], self.zr.at[d - 1], self.partner).wait_recv()
        yield

    def first_rings(self, c):
        self.share(c, 0).start()
        self.push(c, 0, 0).start()
        self.push(c, 0, 1).start()
        for k in range(4):
            self.arrive(c, 0, k)
            if k < 2:
                self.push(c, 0, 2 + k).start()
            if k == 3:
                self.push(c, 1, 0).start()
                self.push(c, 1, 1).start()
        for k in range(4):
            self.share(c, 1 + k).start()
        for i in range(5):
            self.shared(c, i)

    def next_lines(self, c):
        for k in range(2):
            self.arrive(c, 1, k)
            self.push(c, 1, 2 + k).start()
            self.share(c, 5 + k).start()
        for i in (5, 6):
            self.shared(c, i)

    def last_line(self, c):
        for k in (2, 3):
            self.arrive(c, 1, k)
            self.share(c, 5 + k).start()

    def last_shared(self, c):
        for i in (7, 8):
            self.shared(c, i)

    def drain(self, c):
        for i in range(9):
            self.share(c, i).wait_send()
        for ring in range(2):
            for k in range(4):
                self.push(c, ring, k).wait_send()


def rotated(tile, cos, sin):
    lane = lax.broadcasted_iota(jnp.int32, tile.shape, 1)
    swapped = jnp.where(lane < ROPE // 2, pltpu.roll(tile, 96, 1), pltpu.roll(tile, 32, 1))
    return tile * cos + swapped * sin


def layer_kernel(
    hid_ref, again_ref, lgain_ref, mgain_ref, cos_ref, sin_ref, seg_ref, routes_ref, gates_ref, pages_ref,
    wl_hbm, wq_hbm, we_hbm, wo_hbm, wg_hbm, wu_hbm, wd_hbm, o_ref, cache_ref,
    wl, wq, we, wo, wg, wu, wd, normed, lpart, lall, tagged, keys, ql, qm, qbuf, m_ref, l_ref, acc_ref, mixed,
    turn, pick, high, low, mix, apart, ain, res, outgoing, items, xin, pout, cin, ysend, yin, back, ret, acc, fin,
    w_sem, own_sem, ls, lr, zs_, zr_, ps, pr, cs, cr,
    rs, rr, a0s, a0r, as_, ar, fys, fyr, fps, fpr, fqs, fqr, xs, xr, ys, yr, b0s, b0r, bs, br, es, er,
):
    z, x, y, core = place_of()
    seq, head = lax.axis_index("seq"), lax.axis_index("head")
    yl, yh = head // 2, seq % 2
    partner = (seq, yl * 2 + 1 - core)
    across = (seq, (1 - yl) * 2 + core)
    q_partner = yl * 2 + 1 - core
    q_across = (1 - yl) * 2 + core
    q_far = (1 - yl) * 2 + 1 - core
    tok = TOK
    mesh_id = pl.DeviceIdType.MESH
    half_y = (y, 3 - y)
    half_h = (yh, 1 - yh)

    loads = [
        pltpu.make_async_copy(src, dst, w_sem.at[i])
        for i, (src, dst) in enumerate(
            (
                (wl_hbm, wl), (wq_hbm, wq), (we_hbm, we), (wo_hbm, wo),
                (wg_hbm.at[0], wg), (wu_hbm.at[0], wu), (wd_hbm.at[0], wd),
            )
        )
    ]
    for copy in loads:
        copy.start()

    barrier = pltpu.get_barrier_semaphore()
    column = z * 4 + x

    def greet(half, k):
        at = (column + k) % 32
        pl.semaphore_signal(
            barrier, inc=1, device_id=device(at // 4, at % 4, half_y[half], core), device_id_type=mesh_id
        )

    def greet_both(k, carry):
        greet(0, k)
        greet(1, k)
        return carry

    greet(1, 0)
    for d in range(1, 4):
        pl.semaphore_signal(barrier, inc=1, device_id=(seq, (head + d) % 4), device_id_type=mesh_id)
    lax.fori_loop(1, 32, greet_both, 0)

    sends = []

    def push(src, dst, send_sem, recv_sem, target):
        copy = remote(src, dst, send_sem, recv_sem, target)
        copy.start()
        sends.append(copy)

    def arrive(region, recv_sem):
        remote(region, region, own_sem.at[2], recv_sem, partner).wait_recv()

    v = hid_ref[...].astype(F32)
    inv = lax.rsqrt(jnp.sum(v * v, axis=1, keepdims=True) * (1.0 / D) + EPS)
    normed[...] = (v * inv * again_ref[...]).astype(BF16)
    lpart[...] = jnp.zeros_like(lpart)
    turn[...] = jnp.zeros_like(turn)
    turn[0:TOPK, :] = routes_ref[...].astype(F32)
    turn[8 : 8 + TOPK, :] = gates_ref[...]
    turn[16:17, :] = seg_ref[...].astype(F32)
    turn[...] = turn[...].T
    seg_col = turn[:, 16:17]
    loads[0].wait()
    lpart[:, :144] = nt(normed[...], wl[...]).astype(BF16)
    pl.semaphore_wait(barrier, 66)

    for d in range(1, 4):
        push(lpart, lall.at[d - 1], ls.at[d - 1], lr.at[d - 1], (seq, (head + d) % 4))
    place_r = lax.broadcasted_iota(jnp.int32, (256, WIDTH), 0)
    place_c = lax.broadcasted_iota(jnp.int32, (256, WIDTH), 1)

    def spread(part, q):
        put = ((place_c == q * 144 + place_r) & (place_r < 144)).astype(F32).astype(BF16)
        return dot(part, put)

    raw = spread(lpart[...], head)
    for d in range(1, 4):
        arrive(lall.at[d - 1], lr.at[d - 1])
        raw = raw + spread(lall[d - 1], (head + 4 - d) % 4)
    comp = raw[:, :LATENT]
    inv = lax.rsqrt(jnp.sum(comp * comp, axis=1, keepdims=True) * (1.0 / LATENT) + EPS)
    tagged[:, :LATENT] = (comp * inv * lgain_ref[...]).astype(BF16)
    turned = rotated(raw[:, LATENT:], cos_ref[...], sin_ref[...])
    lane = lax.broadcasted_iota(jnp.int32, (tok, 128), 1)
    tagged[:, LATENT:] = jnp.where(lane == ROPE, seg_col, turned).astype(BF16)

    scale = (NOPE + ROPE) ** (-0.5)

    def work():
        page = jnp.zeros((PART, WIDTH), BF16)
        for p in range(4):
            page = jnp.where(pages_ref[:, p : p + 1] == head, tagged[p * PART : (p + 1) * PART, :], page)
        cache_ref[...] = page[:, : LATENT + ROPE]
        loads[1].wait()
        qbuf[...] = dot(normed[...], wq[...])
        loads[2].wait()
        for k in range(HEADS // 2):
            t0 = qbuf[:, k * 384 : k * 384 + 128]
            t1 = qbuf[:, k * 384 + 128 : k * 384 + 256]
            t2 = pltpu.roll(qbuf[:, k * 384 + 256 : k * 384 + 384], 64, 1)
            nope = (t0, jnp.where(lane < 64, pltpu.roll(t1, 64, 1), t2))
            rope = (t1, t2)
            for i in range(2):
                h = 2 * k + i
                rows = slice(h * tok, (h + 1) * tok)
                key_w = we[:, h * (NOPE + VDIM) : h * (NOPE + VDIM) + NOPE]
                ql[rows, :] = (nt(nope[i].astype(BF16), key_w) * scale).astype(BF16)
                qm[rows, :] = (rotated(rope[i], cos_ref[...], sin_ref[...]) * scale).astype(BF16)
        qm[HEADS * tok :, :] = (lax.broadcasted_iota(jnp.int32, (16, 128), 1) == ROPE).astype(F32).astype(BF16)
        row = lax.broadcasted_iota(jnp.int32, (tok, 128), 0)
        below = (lane < row).astype(F32).astype(BF16)
        cell = lane // SLOTS
        slot = (lane % SLOTS).astype(F32)

        def table(ze, carry):
            expert = (ze * 8 + (cell % 4) * 2 + cell // 4).astype(F32)
            taken = jnp.zeros((tok, 128), F32)
            gate = jnp.zeros((tok, 128), F32)
            for j in range(TOPK):
                hit = turn[:, j : j + 1] == expert
                taken = jnp.where(hit, 1.0, taken)
                gate = jnp.where(hit, turn[:, 8 + j : 9 + j], gate)
            rank = dot(below, taken.astype(BF16))
            put = (taken > 0.5) & (rank == slot)
            weight = jnp.where(put, gate, 0.0)
            top = weight.astype(BF16)
            high[ze] = top
            low[ze] = (weight - top.astype(F32)).astype(BF16)
            pick[ze] = put.astype(F32).T.astype(BF16)
            return carry

        lax.fori_loop(0, 8, table, 0)

    mine = tagged.at[pl.ds(pl.multiple_of(head * PART, PART), PART)]
    gather = KeyGather(keys, own_sem.at[3], zs_, zr_, ps, pr, cs, cr)
    first = gather.along_z(mine)
    next(first)
    work()
    rows = HEADS * tok
    m_ref[...] = jnp.full_like(m_ref, -1e30)
    l_ref[...] = jnp.zeros_like(l_ref)
    acc_ref[...] = jnp.zeros_like(acc_ref)
    qpos = seq * tok + lax.broadcasted_iota(jnp.int32, (rows, 1), 0) % tok
    qseg = jnp.concatenate([seg_col] * HEADS, axis=0)

    def attend(color, line):
        for lo, n in HALVES:
            parts = []
            for k in range(4):
                xx = jnp.where(color == 0, k, line)
                yy = jnp.where(color == 0, line, k)
                parts.append(keys[pl.ds(lo, n), xx, yy, color].reshape(n * PART, WIDTH))
            block = jnp.concatenate(parts, axis=0)
            at = lax.broadcasted_iota(jnp.int32, (1, n * 128), 1)
            turn_k = at // (n * PART)
            plane = (z + 2 + lo + (at // PART) % n) % 8
            kpos = plane * 1024 + color * PART + at % PART
            kpos = kpos + jnp.where(color == 0, turn_k * 256 + line * 64, line * 256 + turn_k * 64)
            c = block[:, :LATENT]
            more = nt(qm[...], block[:, LATENT:])
            sc = nt(ql[...], c) + more[:rows]
            kseg = more[rows : rows + 1]
            ok = (qseg == kseg) & (kpos <= qpos)
            sc = jnp.where(ok, sc, -1e30)
            m_old = m_ref[...]
            m_new = jnp.maximum(m_old, jnp.max(sc, axis=1, keepdims=True))
            p = jnp.where(ok, jnp.exp(sc - m_new), 0.0)
            fade = jnp.exp(m_old - m_new)
            l_ref[...] = l_ref[...] * fade + jnp.sum(p, axis=1, keepdims=True)
            acc_ref[...] = acc_ref[...] * fade + dot(p.astype(BF16), c)
            m_ref[...] = m_new

    def attend_lines(steps):
        def one(t, carry):
            color = t % 2
            step = steps[0] if len(steps) == 1 else 1 + 2 * (t // 2)
            attend(color, (jnp.where(color == 0, y, x) + step) % 4)
            return carry

        lax.fori_loop(0, 2 * len(steps), one, 0)

    next(first)
    gather.both(gather.first_rings)
    attend_lines((0,))
    gather.both(gather.next_lines)
    attend_lines((1, 3))
    gather.both(gather.last_line)

    def last(t, carry):
        @pl.when(t == 1)
        def _():
            gather.both(gather.last_shared)

        color = (core + t) % 2
        attend(color, (jnp.where(color == 0, y, x) + 2) % 4)
        return carry

    lax.fori_loop(0, 2, last, 0)
    gather.both(gather.drain)
    mixed[...] = (acc_ref[...] / l_ref[...]).astype(BF16)

    for h in range(HEADS):
        value = we[:, h * (NOPE + VDIM) + NOPE : (h + 1) * (NOPE + VDIM)]
        mix[:, h * VDIM : (h + 1) * VDIM] = dot(mixed[h * tok : (h + 1) * tok, :], value).astype(BF16)
    loads[3].wait()
    for q in range(4):
        apart[q] = dot(mix[...], wo[:, q * 512 : (q + 1) * 512]).astype(BF16)
    for d in range(1, 4):
        q = (head + d) % 4
        push(apart.at[q], ain.at[d - 1], rs.at[d - 1], rr.at[d - 1], (seq, q))
    total = apart[head].astype(F32)
    for d in range(1, 4):
        arrive(ain.at[d - 1], rr.at[d - 1])
        total = total + ain[d - 1].astype(F32)
    own = hid_ref[:, pl.ds(pl.multiple_of(head * 512, 512), 512)].astype(F32)
    res[...] = (own + total).astype(BF16)

    locals_ = []

    def send_slab(src, dst, slab, j, send0, recv0, send_sem, recv_sem, local_sem):
        for half in range(2):
            if half == 0 and j == 0:
                copy = pltpu.make_async_copy(src.at[slab, yh, x], dst.at[z, yh, x], local_sem)
                copy.start()
                locals_.append(copy)
                for k in range(1, 4):
                    xt = (x + k) % 4
                    push(
                        src.at[slab, yh, xt], dst.at[z, yh, x], send0.at[k - 1], recv0.at[k - 1],
                        device(slab, xt, y, core),
                    )
            else:

                def send(xt, carry, half=half):
                    remote(
                        src.at[slab, half_h[half], xt], dst.at[z, yh, x], send_sem.at[half, j], recv_sem.at[half, j],
                        device(slab, xt, half_y[half], core),
                    ).start()
                    return carry

                lax.fori_loop(0, 4, send, 0)

    def slab_sent(src, slab, j, send_sem):
        for half in range(2):
            if half or j:
                part = src.at[slab, half_h[half]]
                remote(part, part, send_sem.at[half, j], own_sem.at[2], partner).wait_send()

    def slab_arrived(parts, j, recv0, recv_sem, local):
        for half in range(2):
            if half == 0 and j == 0:
                locals_[local].wait()
                for k in range(1, 4):
                    arrive(parts[0].at[(x + 4 - k) % 4], recv0.at[k - 1])
            else:
                arrive(parts[half], recv_sem.at[half, j])

    for pair in ORDER:
        for j in pair:
            zt = (z + j) % 8
            outgoing[zt] = dot(pick[zt], res[...]).astype(BF16).reshape(2, 4, SLOTS, 512)
            send_slab(outgoing, items.at[head], zt, j, a0s, a0r, as_, ar, own_sem.at[0])

    def stage_a(g):
        for j in ORDER[g]:
            zs = (z + 8 - j) % 8
            parts = (items.at[head, zs, yh], items.at[q_across, zs, 1 - yh])
            slab_arrived(parts, j, a0r, ar, 0)
            for half in range(2):
                push(parts[half], parts[half], fys.at[half, j], fyr.at[half, j], across)
                push(parts[half], parts[half], fps.at[half, j], fpr.at[half, j], partner)

    def stage_b(g):
        for j in ORDER[g]:
            zs = (z + 8 - j) % 8
            for half, part in enumerate((items.at[q_across, zs, yh], items.at[head, zs, 1 - yh])):
                arrive(part, fyr.at[half, j])
                push(part, part, fqs.at[half, j], fqr.at[half, j], partner)

    def stage_c(g):
        if g == 0:
            for copy in loads[4:]:
                copy.wait()
        for t, j in enumerate(ORDER[g]):
            zs = (z + 8 - j) % 8
            arrive(items.at[q_partner, zs, yh], fpr.at[0, j])
            arrive(items.at[q_far, zs, 1 - yh], fpr.at[1, j])
            arrive(items.at[q_far, zs, yh], fqr.at[0, j])
            arrive(items.at[q_partner, zs, 1 - yh], fqr.at[1, j])
            mean_sq = jnp.zeros((tok, 1), F32)
            for q in range(4):
                v = items[q, zs].reshape(tok, 512).astype(F32)
                mean_sq = mean_sq + jnp.sum(v * v, axis=1, keepdims=True)
            inv = lax.rsqrt(mean_sq * (1.0 / D) + EPS)
            for q in range(4):
                v = items[q, zs].reshape(tok, 512).astype(F32)
                cols = slice(q * 512, (q + 1) * 512)
                xin[t * tok : (t + 1) * tok, cols] = (v * inv * mgain_ref[:, cols]).astype(BF16)
        gate = nt(xin[...], wg[...])
        up = nt(xin[...], wu[...])
        hidden = (gate / (1.0 + jnp.exp(-gate)) * up).astype(BF16)
        for q in range(4):
            part = dot(hidden, wd[:, q * 512 : (q + 1) * 512]).astype(BF16)
            for t, j in enumerate(ORDER[g]):
                pout[q, (z + 8 - j) % 8] = part[t * tok : (t + 1) * tok].reshape(2, 4, SLOTS, 512)
        for j in ORDER[g]:
            zs = (z + 8 - j) % 8
            for side in range(2):
                push(
                    pout.at[side * 2 + 1 - core, zs], cin.at[side, zs], xs.at[side, j], xr.at[side, j], partner
                )

    def chip_sum(side, zs, h):
        return pout[side * 2 + core, zs, h].astype(F32) + cin[side, zs, h].astype(F32)

    def stage_d(g):
        for j in ORDER[g]:
            zs = (z + 8 - j) % 8
            for side in range(2):
                arrive(cin.at[side, zs], xr.at[side, j])
            ysend[zs, yh] = chip_sum(1 - yl, zs, yh).astype(BF16)
            ysend[zs, 1 - yh] = chip_sum(yl, zs, 1 - yh).astype(BF16)
            push(ysend.at[zs], yin.at[zs], ys.at[j], yr.at[j], across)

    def stage_e(g):
        for j in ORDER[g]:
            zs = (z + 8 - j) % 8
            arrive(yin.at[zs], yr.at[j])
            back[zs, yh] = (chip_sum(yl, zs, yh) + yin[zs, yh].astype(F32)).astype(BF16)
            back[zs, 1 - yh] = (chip_sum(1 - yl, zs, 1 - yh) + yin[zs, 1 - yh].astype(F32)).astype(BF16)
            send_slab(back, ret, zs, j, b0s, b0r, bs, br, own_sem.at[1])

    a, b, c, d, e = stage_a, stage_b, stage_c, stage_d, stage_e
    for stage, g in (
        (a, 0), (b, 0), (a, 1), (c, 0), (b, 1), (d, 0), (a, 2), (c, 1), (e, 0), (b, 2),
        (d, 1), (a, 3), (c, 2), (e, 1), (b, 3), (d, 2), (c, 3), (e, 2), (d, 3), (e, 3),
    ):
        stage(g)

    acc[...] = res[...].astype(F32)
    for pair in ORDER:
        for j in pair:
            ze = (z + j) % 8
            slab_arrived((ret.at[ze, yh], ret.at[ze, 1 - yh]), j, b0r, br, 1)
            got = ret[ze].reshape(tok, 512)
            acc[...] += dot(high[ze], got) + dot(low[ze], got)
    fin[head] = acc[...].astype(BF16)
    parts = (pl.ds(0, tok // 2), pl.ds(tok // 2, tok // 2))
    for i, at in enumerate(parts):
        push(fin.at[head, at], fin.at[head, at], es.at[i], er.at[i], across)
    push(fin.at[head], fin.at[head], es.at[4], er.at[4], partner)
    for i, at in enumerate(parts):
        arrive(fin.at[q_across, at], er.at[i])
        push(fin.at[q_across, at], fin.at[q_across, at], es.at[2 + i], er.at[2 + i], partner)
    arrive(fin.at[q_partner], er.at[4])
    for i, at in enumerate(parts):
        arrive(fin.at[q_far, at], er.at[2 + i])
    for q in range(4):
        o_ref[:, q * 512 : (q + 1) * 512] = fin[q]
    for copy in sends:
        copy.wait_send()
    for j in range(8):
        slab_sent(outgoing, (z + j) % 8, j, as_)
        slab_sent(back, (z + 8 - j) % 8, j, bs)


def local(
    hidden_in,
    attn_gain,
    w_query,
    w_latent,
    latent_gain,
    w_expand,
    w_out,
    moe_gain,
    w_gate,
    w_up,
    w_down,
    routes,
    gates,
    segment,
    page_table,
):
    positions = lax.axis_index("seq") * TOK + jnp.arange(TOK, dtype=jnp.int32)
    cosine, sine = rope_tables(positions, ROPE)
    rest = jnp.zeros((TOK, 128 - ROPE), F32)
    cos = jnp.concatenate([cosine, cosine, rest], axis=1)
    sin = jnp.concatenate([-sine, sine, rest], axis=1)
    ff = w_gate.shape[2]
    dma = pltpu.SemaphoreType.DMA
    vmem, hbm = pl.BlockSpec(memory_space=pltpu.VMEM), pl.BlockSpec(memory_space=pl.ANY)
    chunks = (8, 2, 4, SLOTS, 512)
    quarter = (TOK, 512)
    rows = HEADS * TOK
    tables = (8, 128, 128)

    def space(*shape):
        return pltpu.VMEM(shape, BF16)

    def two(*shape):
        return [dma(shape), dma(shape)]

    hidden_out, page = pl.pallas_call(
        layer_kernel,
        out_shape=(
            jax.ShapeDtypeStruct((TOK, D), BF16),
            jax.ShapeDtypeStruct((PART, LATENT + ROPE), BF16),
        ),
        in_specs=[vmem] * 10 + [hbm] * 7,
        out_specs=(vmem, vmem),
        scratch_shapes=[
            space(144, D), space(D, 768), space(LATENT, 1024), space(512, D), space(ff, D), space(ff, D),
            space(ff, D), space(TOK, D), space(TOK, 256), space(3, TOK, 256), space(TOK, WIDTH),
            space(NEAR, 4, 4, 2, PART, WIDTH), space(rows, LATENT), space(rows + 16, 128),
            pltpu.VMEM((TOK, 768), F32), pltpu.VMEM((rows, 1), F32), pltpu.VMEM((rows, 1), F32),
            pltpu.VMEM((rows, LATENT), F32), space(rows, LATENT),
            pltpu.VMEM((TOK, 128), F32), space(*tables), space(*tables), space(*tables), space(*quarter),
            space(4, *quarter),
            space(3, *quarter), space(*quarter), space(*chunks), space(4, *chunks), space(2 * TOK, D),
            space(4, *chunks), space(2, *chunks), space(*chunks), space(*chunks), space(*chunks), space(*chunks),
            pltpu.VMEM(quarter, F32), space(4, *quarter),
            dma((7,)), dma((4,)), *two(3), *two(6), *two(8), *two(9),
            *two(3), *two(3), *two(2, 8), *two(2, 8), *two(2, 8), *two(2, 8), *two(2, 8), *two(8),
            *two(3), *two(2, 8), *two(5),
        ],
        compiler_params=pltpu.CompilerParams(
            collective_id=0, has_side_effects=True, vmem_limit_bytes=60 << 20
        ),
    )(
        hidden_in,
        attn_gain[None, :],
        latent_gain[None, :],
        moe_gain[None, :],
        cos,
        sin,
        segment[None, :],
        routes.T,
        gates.T,
        page_table,
        w_latent.T,
        w_query,
        w_expand,
        w_out,
        w_gate.transpose(0, 2, 1),
        w_up.transpose(0, 2, 1),
        w_down,
    )
    return (hidden_out, page.reshape(1, PART * (LATENT + ROPE)))


def solution(mesh):
    return jax.shard_map(
        local,
        mesh=mesh,
        in_specs=(
            P("seq", None),
            P(),
            P(None, "head"),
            P(None, "head"),
            P(),
            P(None, "head"),
            P("head", None),
            P(),
            P("seq", None, "head"),
            P("seq", None, "head"),
            P("seq", "head", None),
            P("seq", None),
            P("seq", None),
            P("seq"),
            P("seq", None),
        ),
        out_specs=(P("seq", None), P(("seq", "head"), None)),
        check_vma=False,
    )
```

```python
import jax
import jax.numpy as jnp
from jax import lax
from jax.experimental import pallas as pl
from jax.experimental.pallas import tpu as pltpu
from jax.sharding import PartitionSpec as P

D = 2048
NOPE = 128
ROPE = 64
VDIM = 128
LATENT = 512
TOPK = 6
TOK = 128
HEADS = 4
SLOTS = 16
PART = 32
WIDTH = 640

EPS = 1e-06
THETA = 50000.0
F32 = jnp.float32
BF16 = jnp.bfloat16


def rope_tables(positions, feat_width):
    half_width = feat_width // 2
    inv_freq = THETA ** (-jnp.arange(half_width, dtype=F32) * 2.0 / feat_width)
    angles = positions.astype(F32)[:, None] * inv_freq[None, :]
    return (jnp.cos(angles), jnp.sin(angles))


def dot(a, b):
    return jnp.dot(a, b, preferred_element_type=F32)


ORDER = ((7, 6), (4, 5), (3, 2), (1, 0))


def nt(a, b):
    return lax.dot_general(a, b, (((1,), (1,)), ((), ())), preferred_element_type=F32)


def place_of():
    seq, head = lax.axis_index("seq"), lax.axis_index("head")
    return seq // 8, (seq // 2) % 4, (seq % 2) * 2 + head // 2, head % 2


def device(z, x, y, core):
    return (z * 8 + x * 2 + y // 2, (y % 2) * 2 + core)


def remote(src, dst, send_sem, recv_sem, target):
    return pltpu.make_async_remote_copy(
        src_ref=src, dst_ref=dst, send_sem=send_sem, recv_sem=recv_sem,
        device_id=target, device_id_type=pl.DeviceIdType.MESH,
    )


NEAR = 7
HALVES = ((0, 4), (4, 3))


class KeyGather:
    def __init__(self, keys, own_sem, zs, zr, ps, pr, cs, cr):
        self.keys, self.own_sem = keys, own_sem
        self.zs, self.zr, self.ps, self.pr, self.cs, self.cr = zs, zr, ps, pr, cs, cr
        self.z, self.x, self.y, self.core = place_of()
        self.partner = device(self.z, self.x, self.y, 1 - self.core)

    def both(self, act):
        @pl.when(self.core == 0)
        def _():
            act(0)

        @pl.when(self.core == 1)
        def _():
            act(1)

    def region(self, c, ring, lo, n, step):
        along_x = (c == 0) == (ring == 0)
        planes = pl.ds(lo, n)
        if along_x:
            at = (self.x + step) % 4
            return self.keys.at[planes, at, self.y, c] if ring == 0 else self.keys.at[planes, at, :, c]
        at = (self.y + step) % 4
        return self.keys.at[planes, self.x, at, c] if ring == 0 else self.keys.at[planes, :, at, c]

    def piece(self, c, i):
        if i == 0:
            return self.region(c, 0, 0, NEAR, 0)
        lo, n, step = ((0, NEAR, 3), (0, NEAR, 1), (*HALVES[0], 2), (*HALVES[1], 2))[(i - 1) % 4]
        return self.region(c, (i - 1) // 4, lo, n, step)

    def share(self, c, i):
        part = self.piece(c, i)
        return remote(part, part, self.cs.at[i], self.cr.at[i], self.partner)

    def shared(self, c, i):
        part = self.piece(1 - c, i)
        remote(part, part, self.cs.at[i], self.cr.at[i], self.partner).wait_recv()

    def push(self, c, ring, k):
        along_x = (c == 0) == (ring == 0)
        x, y, z = self.x, self.y, self.z
        turn = 1 if k in (0, 2, 4) else 3
        to = device(z, (x + turn) % 4, y, self.core) if along_x else device(z, x, (y + turn) % 4, self.core)
        half, step = ((0, 0), (1, 0), (0, 3), (1, 1), (1, 0), (0, 0))[k]
        part = self.region(c, ring, *HALVES[half], step)
        return remote(part, part, self.ps.at[6 * ring + k], self.pr.at[6 * ring + k], to)

    def arrive(self, c, ring, k):
        half, step = ((0, 3), (1, 1), (0, 2), (1, 2), (1, 3), (0, 1))[k]
        part = self.region(c, ring, *HALVES[half], step)
        remote(part, part, self.ps.at[6 * ring + k], self.pr.at[6 * ring + k], self.partner).wait_recv()

    def along_z(self, mine_ref):
        slot = lambda r: self.keys.at[r, self.x, self.y, self.core]
        own = pltpu.make_async_copy(mine_ref, slot(NEAR - 1), self.own_sem)
        own.start()
        copies = []
        for d in (4, 3, 5, 2, 6, 1):
            to = device((self.z + d) % 8, self.x, self.y, self.core)
            copy = remote(mine_ref, slot(NEAR - 1 - d), self.zs.at[d - 1], self.zr.at[d - 1], to)
            copy.start()
            copies.append(copy)
        yield
        own.wait()
        for copy in copies:
            copy.wait_send()
        for d in range(1, NEAR):
            there = slot(NEAR - 1 - d)
            remote(there, there, self.zs.at[d - 1], self.zr.at[d - 1], self.partner).wait_recv()
        yield

    def first_rings(self, c):
        self.share(c, 0).start()
        for k in (0, 1, 4, 5):
            self.push(c, 0, k).start()
        for k in range(2):
            self.arrive(c, 0, k)
            self.push(c, 0, 2 + k).start()
        for k in (4, 5, 2, 3):
            self.arrive(c, 0, k)
        for k in (0, 1, 4, 5):
            self.push(c, 1, k).start()
        for k in range(4):
            self.share(c, 1 + k).start()
        for i in range(5):
            self.shared(c, i)

    def next_lines(self, c):
        for k in range(2):
            self.arrive(c, 1, k)
            self.push(c, 1, 2 + k).start()
        for k in range(2):
            self.arrive(c, 1, 4 + k)
            self.share(c, 5 + k).start()
        for i in (5, 6):
            self.shared(c, i)

    def last_line(self, c):
        for k in (2, 3):
            self.arrive(c, 1, k)
            self.share(c, 5 + k).start()

    def last_shared(self, c):
        for i in (7, 8):
            self.shared(c, i)

    def drain(self, c):
        for i in range(9):
            self.share(c, i).wait_send()
        for ring in range(2):
            for k in range(6):
                self.push(c, ring, k).wait_send()


def rotated(tile, cos, sin):
    lane = lax.broadcasted_iota(jnp.int32, tile.shape, 1)
    swapped = jnp.where(lane < ROPE // 2, pltpu.roll(tile, 96, 1), pltpu.roll(tile, 32, 1))
    return tile * cos + swapped * sin


def layer_kernel(
    hid_ref, again_ref, lgain_ref, mgain_ref, cos_ref, sin_ref, seg_ref, routes_ref, gates_ref, pages_ref,
    wl_hbm, wq_hbm, we_hbm, wo_hbm, wg_hbm, wu_hbm, wd_hbm, o_ref, cache_ref,
    wl, wq, we, wo, wg, wu, wd, normed, lpart, lall, tagged, keys, qf, qbuf, m_ref, l_ref, acc_ref, mixed,
    turn, pick, high, low, mix, apart, ain, res, outgoing, items, xin, pout, cin, ysend, yin, back, ret, acc, fin,
    w_sem, own_sem, ls, lr, zs_, zr_, ps, pr, cs, cr,
    rs, rr, a0s, a0r, as_, ar, fys, fyr, fps, fpr, fqs, fqr, xs, xr, ys, yr, b0s, b0r, bs, br, es, er,
):
    z, x, y, core = place_of()
    seq, head = lax.axis_index("seq"), lax.axis_index("head")
    yl, yh = head // 2, seq % 2
    partner = (seq, yl * 2 + 1 - core)
    across = (seq, (1 - yl) * 2 + core)
    q_partner = yl * 2 + 1 - core
    q_across = (1 - yl) * 2 + core
    q_far = (1 - yl) * 2 + 1 - core
    tok = TOK
    mesh_id = pl.DeviceIdType.MESH
    half_y = (y, 3 - y)
    half_h = (yh, 1 - yh)

    loads = [
        pltpu.make_async_copy(src, dst, w_sem.at[i])
        for i, (src, dst) in enumerate(
            (
                (wl_hbm, wl), (wq_hbm, wq), (we_hbm, we), (wo_hbm, wo),
                (wg_hbm.at[0], wg), (wu_hbm.at[0], wu), (wd_hbm.at[0], wd),
            )
        )
    ]
    for copy in loads:
        copy.start()

    barrier = pltpu.get_barrier_semaphore()
    column = z * 4 + x

    def greet(half, k):
        at = (column + k) % 32
        pl.semaphore_signal(
            barrier, inc=1, device_id=device(at // 4, at % 4, half_y[half], core), device_id_type=mesh_id
        )

    def greet_both(k, carry):
        greet(0, k)
        greet(1, k)
        return carry

    greet(1, 0)
    for d in range(1, 4):
        pl.semaphore_signal(barrier, inc=1, device_id=(seq, (head + d) % 4), device_id_type=mesh_id)
    lax.fori_loop(1, 32, greet_both, 0)

    sends = []

    def push(src, dst, send_sem, recv_sem, target):
        copy = remote(src, dst, send_sem, recv_sem, target)
        copy.start()
        sends.append(copy)

    def arrive(region, recv_sem):
        remote(region, region, own_sem.at[2], recv_sem, partner).wait_recv()

    v = hid_ref[...].astype(F32)
    inv = lax.rsqrt(jnp.sum(v * v, axis=1, keepdims=True) * (1.0 / D) + EPS)
    normed[...] = (v * inv * again_ref[...]).astype(BF16)
    lpart[...] = jnp.zeros_like(lpart)
    turn[...] = jnp.zeros_like(turn)
    turn[0:TOPK, :] = routes_ref[...].astype(F32)
    turn[8 : 8 + TOPK, :] = gates_ref[...]
    turn[16:17, :] = seg_ref[...].astype(F32)
    turn[...] = turn[...].T
    seg_col = turn[:, 16:17]
    loads[0].wait()
    lpart[:, :144] = nt(normed[...], wl[...]).astype(BF16)
    pl.semaphore_wait(barrier, 66)

    for d in range(1, 4):
        push(lpart, lall.at[d - 1], ls.at[d - 1], lr.at[d - 1], (seq, (head + d) % 4))
    place_r = lax.broadcasted_iota(jnp.int32, (256, WIDTH), 0)
    place_c = lax.broadcasted_iota(jnp.int32, (256, WIDTH), 1)

    def spread(part, q):
        put = ((place_c == q * 144 + place_r) & (place_r < 144)).astype(F32).astype(BF16)
        return dot(part, put)

    raw = spread(lpart[...], head)
    for d in range(1, 4):
        arrive(lall.at[d - 1], lr.at[d - 1])
        raw = raw + spread(lall[d - 1], (head + 4 - d) % 4)
    comp = raw[:, :LATENT]
    inv = lax.rsqrt(jnp.sum(comp * comp, axis=1, keepdims=True) * (1.0 / LATENT) + EPS)
    tagged[:, :LATENT] = (comp * inv * lgain_ref[...]).astype(BF16)
    turned = rotated(raw[:, LATENT:], cos_ref[...], sin_ref[...])
    lane = lax.broadcasted_iota(jnp.int32, (tok, 128), 1)
    tagged[:, LATENT:] = jnp.where(lane == ROPE, seg_col, turned).astype(BF16)

    scale = (NOPE + ROPE) ** (-0.5) * 1.4426950408889634

    def work():
        page = jnp.zeros((PART, WIDTH), BF16)
        for p in range(4):
            page = jnp.where(pages_ref[:, p : p + 1] == head, tagged[p * PART : (p + 1) * PART, :], page)
        cache_ref[...] = page[:, : LATENT + ROPE]
        loads[1].wait()
        qbuf[...] = dot(normed[...], wq[...])
        loads[2].wait()
        for k in range(HEADS // 2):
            t0 = qbuf[:, k * 384 : k * 384 + 128]
            t1 = qbuf[:, k * 384 + 128 : k * 384 + 256]
            t2 = pltpu.roll(qbuf[:, k * 384 + 256 : k * 384 + 384], 64, 1)
            nope = (t0, jnp.where(lane < 64, pltpu.roll(t1, 64, 1), t2))
            rope = (t1, t2)
            for i in range(2):
                h = 2 * k + i
                rows = slice(h * tok, (h + 1) * tok)
                key_w = we[:, h * (NOPE + VDIM) : h * (NOPE + VDIM) + NOPE]
                qf[rows, :LATENT] = (nt(nope[i].astype(BF16), key_w) * scale).astype(BF16)
                qf[rows, LATENT:] = (rotated(rope[i], cos_ref[...], sin_ref[...]) * scale).astype(BF16)
        row = lax.broadcasted_iota(jnp.int32, (tok, 128), 0)
        below = (lane < row).astype(F32).astype(BF16)
        cell = lane // SLOTS
        slot = (lane % SLOTS).astype(F32)

        def table(ze, carry):
            expert = (ze * 8 + (cell % 4) * 2 + cell // 4).astype(F32)
            taken = jnp.zeros((tok, 128), F32)
            gate = jnp.zeros((tok, 128), F32)
            for j in range(TOPK):
                hit = turn[:, j : j + 1] == expert
                taken = jnp.where(hit, 1.0, taken)
                gate = jnp.where(hit, turn[:, 8 + j : 9 + j], gate)
            rank = dot(below, taken.astype(BF16))
            put = (taken > 0.5) & (rank == slot)
            weight = jnp.where(put, gate, 0.0)
            top = weight.astype(BF16)
            high[ze] = top
            low[ze] = (weight - top.astype(F32)).astype(BF16)
            pick[ze] = put.astype(F32).T.astype(BF16)
            return carry

        lax.fori_loop(0, 8, table, 0)

    mine = tagged.at[pl.ds(pl.multiple_of(head * PART, PART), PART)]
    gather = KeyGather(keys, own_sem.at[3], zs_, zr_, ps, pr, cs, cr)
    first = gather.along_z(mine)
    next(first)
    work()
    rows = HEADS * tok
    qseg = jnp.concatenate([seg_col] * HEADS, axis=0)
    at_seg = (lax.broadcasted_iota(jnp.int32, (16, 128), 1) == ROPE).astype(F32).astype(BF16)

    def segments(block):
        return nt(at_seg, block[:, LATENT:])[0:1]

    block = tagged[...]
    query = lax.broadcasted_iota(jnp.int32, (rows, 1), 0) % tok
    ok = (qseg == segments(block)) & (lax.broadcasted_iota(jnp.int32, (1, tok), 1) <= query)
    sc = jnp.where(ok, nt(qf[...], block), -1e30)
    top = jnp.max(sc, axis=1, keepdims=True)
    p = jnp.exp2(sc - top)
    m_ref[...] = top
    l_ref[...] = jnp.sum(p, axis=1, keepdims=True)
    acc_ref[...] = dot(p.astype(BF16), block[:, :LATENT])

    def attend(color, line):
        parts = []
        for k in range(4):
            xx = jnp.where(color == 0, k, line)
            yy = jnp.where(color == 0, line, k)
            parts.append(keys[:, xx, yy, color].reshape(NEAR * PART, WIDTH))
        block = jnp.concatenate(parts, axis=0)
        at = lax.broadcasted_iota(jnp.int32, (1, NEAR * 128), 1)
        place = at // (NEAR * PART)
        plane = (z + 2 + (at // PART) % NEAR) % 8
        source = plane * 8 + jnp.where(color == 0, place * 2 + line // 2, line * 2 + place // 2)
        kseg = jnp.where(source < seq, segments(block), -1.0)
        sc = jnp.where(qseg == kseg, nt(qf[...], block), -1e30)
        m_old = m_ref[...]
        m_new = jnp.maximum(m_old, jnp.max(sc, axis=1, keepdims=True))
        p = jnp.exp2(sc - m_new)
        fade = jnp.exp2(m_old - m_new)
        l_ref[...] = l_ref[...] * fade + jnp.sum(p, axis=1, keepdims=True)
        acc_ref[...] = acc_ref[...] * fade + dot(p.astype(BF16), block[:, :LATENT])
        m_ref[...] = m_new

    def attend_lines(steps):
        def one(t, carry):
            color = t % 2
            step = steps[0] if len(steps) == 1 else 1 + 2 * (t // 2)
            attend(color, (jnp.where(color == 0, y, x) + step) % 4)
            return carry

        lax.fori_loop(0, 2 * len(steps), one, 0)

    next(first)
    gather.both(gather.first_rings)
    attend_lines((0,))
    gather.both(gather.next_lines)
    attend_lines((1, 3))
    gather.both(gather.last_line)

    def last(t, carry):
        @pl.when(t == 1)
        def _():
            gather.both(gather.last_shared)

        color = (core + t) % 2
        attend(color, (jnp.where(color == 0, y, x) + 2) % 4)
        return carry

    lax.fori_loop(0, 2, last, 0)
    gather.both(gather.drain)
    mixed[...] = (acc_ref[...] / l_ref[...]).astype(BF16)

    for h in range(HEADS):
        value = we[:, h * (NOPE + VDIM) + NOPE : (h + 1) * (NOPE + VDIM)]
        mix[:, h * VDIM : (h + 1) * VDIM] = dot(mixed[h * tok : (h + 1) * tok, :], value).astype(BF16)
    loads[3].wait()
    for q in range(4):
        apart[q] = dot(mix[...], wo[:, q * 512 : (q + 1) * 512]).astype(BF16)
    for d in range(1, 4):
        q = (head + d) % 4
        push(apart.at[q], ain.at[d - 1], rs.at[d - 1], rr.at[d - 1], (seq, q))
    total = apart[head].astype(F32)
    for d in range(1, 4):
        arrive(ain.at[d - 1], rr.at[d - 1])
        total = total + ain[d - 1].astype(F32)
    own = hid_ref[:, pl.ds(pl.multiple_of(head * 512, 512), 512)].astype(F32)
    res[...] = (own + total).astype(BF16)

    locals_ = []

    def send_slab(src, dst, slab, j, send0, recv0, send_sem, recv_sem, local_sem):
        for half in range(2):
            if half == 0 and j == 0:
                copy = pltpu.make_async_copy(src.at[slab, yh, x], dst.at[z, yh, x], local_sem)
                copy.start()
                locals_.append(copy)
                for k in range(1, 4):
                    xt = (x + k) % 4
                    push(
                        src.at[slab, yh, xt], dst.at[z, yh, x], send0.at[k - 1], recv0.at[k - 1],
                        device(slab, xt, y, core),
                    )
            else:

                def send(xt, carry, half=half):
                    remote(
                        src.at[slab, half_h[half], xt], dst.at[z, yh, x], send_sem.at[half, j], recv_sem.at[half, j],
                        device(slab, xt, half_y[half], core),
                    ).start()
                    return carry

                lax.fori_loop(0, 4, send, 0)

    def slab_sent(src, slab, j, send_sem):
        for half in range(2):
            if half or j:
                part = src.at[slab, half_h[half]]
                remote(part, part, send_sem.at[half, j], own_sem.at[2], partner).wait_send()

    def slab_arrived(parts, j, recv0, recv_sem, local):
        for half in range(2):
            if half == 0 and j == 0:
                locals_[local].wait()
                for k in range(1, 4):
                    arrive(parts[0].at[(x + 4 - k) % 4], recv0.at[k - 1])
            else:
                arrive(parts[half], recv_sem.at[half, j])

    for pair in ORDER:
        for j in pair:
            zt = (z + j) % 8
            outgoing[zt] = dot(pick[zt], res[...]).astype(BF16).reshape(2, 4, SLOTS, 512)
            send_slab(outgoing, items.at[head], zt, j, a0s, a0r, as_, ar, own_sem.at[0])

    def stage_a(g):
        for j in ORDER[g]:
            zs = (z + 8 - j) % 8
            parts = (items.at[head, zs, yh], items.at[q_across, zs, 1 - yh])
            slab_arrived(parts, j, a0r, ar, 0)
            for half in range(2):
                push(parts[half], parts[half], fys.at[half, j], fyr.at[half, j], across)
                push(parts[half], parts[half], fps.at[half, j], fpr.at[half, j], partner)

    def stage_b(g):
        for j in ORDER[g]:
            zs = (z + 8 - j) % 8
            for half, part in enumerate((items.at[q_across, zs, yh], items.at[head, zs, 1 - yh])):
                arrive(part, fyr.at[half, j])
                push(part, part, fqs.at[half, j], fqr.at[half, j], partner)

    def stage_c(g):
        if g == 0:
            for copy in loads[4:]:
                copy.wait()
        for t, j in enumerate(ORDER[g]):
            zs = (z + 8 - j) % 8
            arrive(items.at[q_partner, zs, yh], fpr.at[0, j])
            arrive(items.at[q_far, zs, 1 - yh], fpr.at[1, j])
            arrive(items.at[q_far, zs, yh], fqr.at[0, j])
            arrive(items.at[q_partner, zs, 1 - yh], fqr.at[1, j])
            mean_sq = jnp.zeros((tok, 1), F32)
            for q in range(4):
                v = items[q, zs].reshape(tok, 512).astype(F32)
                mean_sq = mean_sq + jnp.sum(v * v, axis=1, keepdims=True)
            inv = lax.rsqrt(mean_sq * (1.0 / D) + EPS)
            for q in range(4):
                v = items[q, zs].reshape(tok, 512).astype(F32)
                cols = slice(q * 512, (q + 1) * 512)
                xin[t * tok : (t + 1) * tok, cols] = (v * inv * mgain_ref[:, cols]).astype(BF16)
        gate = nt(xin[...], wg[...])
        up = nt(xin[...], wu[...])
        hidden = (gate / (1.0 + jnp.exp(-gate)) * up).astype(BF16)
        for q in range(4):
            part = dot(hidden, wd[:, q * 512 : (q + 1) * 512]).astype(BF16)
            for t, j in enumerate(ORDER[g]):
                pout[q, (z + 8 - j) % 8] = part[t * tok : (t + 1) * tok].reshape(2, 4, SLOTS, 512)
        for j in ORDER[g]:
            zs = (z + 8 - j) % 8
            for side in range(2):
                push(
                    pout.at[side * 2 + 1 - core, zs], cin.at[side, zs], xs.at[side, j], xr.at[side, j], partner
                )

    def chip_sum(side, zs, h):
        return pout[side * 2 + core, zs, h].astype(F32) + cin[side, zs, h].astype(F32)

    def stage_d(g):
        for j in ORDER[g]:
            zs = (z + 8 - j) % 8
            for side in range(2):
                arrive(cin.at[side, zs], xr.at[side, j])
            ysend[zs, yh] = chip_sum(1 - yl, zs, yh).astype(BF16)
            ysend[zs, 1 - yh] = chip_sum(yl, zs, 1 - yh).astype(BF16)
            push(ysend.at[zs], yin.at[zs], ys.at[j], yr.at[j], across)

    def stage_e(g):
        for j in ORDER[g]:
            zs = (z + 8 - j) % 8
            arrive(yin.at[zs], yr.at[j])
            back[zs, yh] = (chip_sum(yl, zs, yh) + yin[zs, yh].astype(F32)).astype(BF16)
            back[zs, 1 - yh] = (chip_sum(1 - yl, zs, 1 - yh) + yin[zs, 1 - yh].astype(F32)).astype(BF16)
            send_slab(back, ret, zs, j, b0s, b0r, bs, br, own_sem.at[1])

    a, b, c, d, e = stage_a, stage_b, stage_c, stage_d, stage_e
    for stage, g in (
        (a, 0), (b, 0), (a, 1), (c, 0), (b, 1), (d, 0), (a, 2), (c, 1), (e, 0), (b, 2),
        (d, 1), (a, 3), (c, 2), (e, 1), (b, 3), (d, 2), (c, 3), (e, 2), (d, 3), (e, 3),
    ):
        stage(g)

    acc[...] = res[...].astype(F32)
    for pair in ORDER:
        for j in pair:
            ze = (z + j) % 8
            slab_arrived((ret.at[ze, yh], ret.at[ze, 1 - yh]), j, b0r, br, 1)
            got = ret[ze].reshape(tok, 512)
            acc[...] += dot(high[ze], got) + dot(low[ze], got)
    fin[head] = acc[...].astype(BF16)
    parts = (pl.ds(0, tok // 2), pl.ds(tok // 2, tok // 2))
    for i, at in enumerate(parts):
        push(fin.at[head, at], fin.at[head, at], es.at[i], er.at[i], across)
    push(fin.at[head], fin.at[head], es.at[4], er.at[4], partner)
    for i, at in enumerate(parts):
        arrive(fin.at[q_across, at], er.at[i])
        push(fin.at[q_across, at], fin.at[q_across, at], es.at[2 + i], er.at[2 + i], partner)
    arrive(fin.at[q_partner], er.at[4])
    for i, at in enumerate(parts):
        arrive(fin.at[q_far, at], er.at[2 + i])
    for q in range(4):
        o_ref[:, q * 512 : (q + 1) * 512] = fin[q]
    for copy in sends:
        copy.wait_send()
    for j in range(8):
        slab_sent(outgoing, (z + j) % 8, j, as_)
        slab_sent(back, (z + 8 - j) % 8, j, bs)


def local(
    hidden_in,
    attn_gain,
    w_query,
    w_latent,
    latent_gain,
    w_expand,
    w_out,
    moe_gain,
    w_gate,
    w_up,
    w_down,
    routes,
    gates,
    segment,
    page_table,
):
    positions = lax.axis_index("seq") * TOK + jnp.arange(TOK, dtype=jnp.int32)
    cosine, sine = rope_tables(positions, ROPE)
    rest = jnp.zeros((TOK, 128 - ROPE), F32)
    cos = jnp.concatenate([cosine, cosine, rest], axis=1)
    sin = jnp.concatenate([-sine, sine, rest], axis=1)
    ff = w_gate.shape[2]
    dma = pltpu.SemaphoreType.DMA
    vmem, hbm = pl.BlockSpec(memory_space=pltpu.VMEM), pl.BlockSpec(memory_space=pl.ANY)
    chunks = (8, 2, 4, SLOTS, 512)
    quarter = (TOK, 512)
    rows = HEADS * TOK
    tables = (8, 128, 128)

    def space(*shape):
        return pltpu.VMEM(shape, BF16)

    def two(*shape):
        return [dma(shape), dma(shape)]

    hidden_out, page = pl.pallas_call(
        layer_kernel,
        out_shape=(
            jax.ShapeDtypeStruct((TOK, D), BF16),
            jax.ShapeDtypeStruct((PART, LATENT + ROPE), BF16),
        ),
        in_specs=[vmem] * 10 + [hbm] * 7,
        out_specs=(vmem, vmem),
        scratch_shapes=[
            space(144, D), space(D, 768), space(LATENT, 1024), space(512, D), space(ff, D), space(ff, D),
            space(ff, D), space(TOK, D), space(TOK, 256), space(3, TOK, 256), space(TOK, WIDTH),
            space(NEAR, 4, 4, 2, PART, WIDTH), space(rows, WIDTH),
            pltpu.VMEM((TOK, 768), F32), pltpu.VMEM((rows, 1), F32), pltpu.VMEM((rows, 1), F32),
            pltpu.VMEM((rows, LATENT), F32), space(rows, LATENT),
            pltpu.VMEM((TOK, 128), F32), space(*tables), space(*tables), space(*tables), space(*quarter),
            space(4, *quarter),
            space(3, *quarter), space(*quarter), space(*chunks), space(4, *chunks), space(2 * TOK, D),
            space(4, *chunks), space(2, *chunks), space(*chunks), space(*chunks), space(*chunks), space(*chunks),
            pltpu.VMEM(quarter, F32), space(4, *quarter),
            dma((7,)), dma((4,)), *two(3), *two(6), *two(12), *two(9),
            *two(3), *two(3), *two(2, 8), *two(2, 8), *two(2, 8), *two(2, 8), *two(2, 8), *two(8),
            *two(3), *two(2, 8), *two(5),
        ],
        compiler_params=pltpu.CompilerParams(
            collective_id=0, has_side_effects=True, vmem_limit_bytes=60 << 20
        ),
    )(
        hidden_in,
        attn_gain[None, :],
        latent_gain[None, :],
        moe_gain[None, :],
        cos,
        sin,
        segment[None, :],
        routes.T,
        gates.T,
        page_table,
        w_latent.T,
        w_query,
        w_expand,
        w_out,
        w_gate.transpose(0, 2, 1),
        w_up.transpose(0, 2, 1),
        w_down,
    )
    return (hidden_out, page.reshape(1, PART * (LATENT + ROPE)))


def solution(mesh):
    return jax.shard_map(
        local,
        mesh=mesh,
        in_specs=(
            P("seq", None),
            P(),
            P(None, "head"),
            P(None, "head"),
            P(),
            P(None, "head"),
            P("head", None),
            P(),
            P("seq", None, "head"),
            P("seq", None, "head"),
            P("seq", "head", None),
            P("seq", None),
            P("seq", None),
            P("seq"),
            P("seq", None),
        ),
        out_specs=(P("seq", None), P(("seq", "head"), None)),
        check_vma=False,
    )
```

```python
import jax
import jax.numpy as jnp
from jax import lax
from jax.experimental import pallas as pl
from jax.experimental.pallas import tpu as pltpu
from jax.sharding import PartitionSpec as P

D = 2048
NOPE = 128
ROPE = 64
VDIM = 128
LATENT = 512
TOPK = 6
TOK = 128
HEADS = 4
SLOTS = 16
PART = 32
WIDTH = 640

EPS = 1e-06
THETA = 50000.0
F32 = jnp.float32
BF16 = jnp.bfloat16


def rope_tables(positions, feat_width):
    half_width = feat_width // 2
    inv_freq = THETA ** (-jnp.arange(half_width, dtype=F32) * 2.0 / feat_width)
    angles = positions.astype(F32)[:, None] * inv_freq[None, :]
    return (jnp.cos(angles), jnp.sin(angles))


def dot(a, b):
    return jnp.dot(a, b, preferred_element_type=F32)


ORDER = ((7, 1), (4, 0), (5, 3), (6, 2))


def nt(a, b):
    return lax.dot_general(a, b, (((1,), (1,)), ((), ())), preferred_element_type=F32)


def place_of():
    seq, head = lax.axis_index("seq"), lax.axis_index("head")
    return seq // 8, (seq // 2) % 4, (seq % 2) * 2 + head // 2, head % 2


def device(z, x, y, core):
    return (z * 8 + x * 2 + y // 2, (y % 2) * 2 + core)


def remote(src, dst, send_sem, recv_sem, target):
    return pltpu.make_async_remote_copy(
        src_ref=src, dst_ref=dst, send_sem=send_sem, recv_sem=recv_sem,
        device_id=target, device_id_type=pl.DeviceIdType.MESH,
    )


NEAR = 7
HALVES = ((0, 4), (4, 3))


class KeyGather:
    def __init__(self, keys, own_sem, zs, zr, ps, pr, cs, cr):
        self.keys, self.own_sem = keys, own_sem
        self.zs, self.zr, self.ps, self.pr, self.cs, self.cr = zs, zr, ps, pr, cs, cr
        self.z, self.x, self.y, self.core = place_of()
        self.partner = device(self.z, self.x, self.y, 1 - self.core)

    def both(self, act):
        @pl.when(self.core == 0)
        def _():
            act(0)

        @pl.when(self.core == 1)
        def _():
            act(1)

    def region(self, c, ring, lo, n, step):
        along_x = (c == 0) == (ring == 0)
        planes = pl.ds(lo, n)
        if along_x:
            at = (self.x + step) % 4
            return self.keys.at[planes, at, self.y, c] if ring == 0 else self.keys.at[planes, at, :, c]
        at = (self.y + step) % 4
        return self.keys.at[planes, self.x, at, c] if ring == 0 else self.keys.at[planes, :, at, c]

    def piece(self, c, i):
        if i == 0:
            return self.region(c, 0, 0, NEAR, 0)
        lo, n, step = ((0, NEAR, 3), (0, NEAR, 1), (*HALVES[0], 2), (*HALVES[1], 2))[(i - 1) % 4]
        return self.region(c, (i - 1) // 4, lo, n, step)

    def share(self, c, i):
        part = self.piece(c, i)
        return remote(part, part, self.cs.at[i], self.cr.at[i], self.partner)

    def shared(self, c, i):
        part = self.piece(1 - c, i)
        remote(part, part, self.cs.at[i], self.cr.at[i], self.partner).wait_recv()

    def push(self, c, ring, k):
        along_x = (c == 0) == (ring == 0)
        x, y, z = self.x, self.y, self.z
        turn = 1 if k in (0, 2, 4) else 3
        to = device(z, (x + turn) % 4, y, self.core) if along_x else device(z, x, (y + turn) % 4, self.core)
        half, step = ((0, 0), (1, 0), (0, 3), (1, 1), (1, 0), (0, 0))[k]
        part = self.region(c, ring, *HALVES[half], step)
        return remote(part, part, self.ps.at[6 * ring + k], self.pr.at[6 * ring + k], to)

    def arrive(self, c, ring, k):
        half, step = ((0, 3), (1, 1), (0, 2), (1, 2), (1, 3), (0, 1))[k]
        part = self.region(c, ring, *HALVES[half], step)
        remote(part, part, self.ps.at[6 * ring + k], self.pr.at[6 * ring + k], self.partner).wait_recv()

    def along_z(self, mine_ref):
        slot = lambda r: self.keys.at[r, self.x, self.y, self.core]
        own = pltpu.make_async_copy(mine_ref, slot(NEAR - 1), self.own_sem)
        own.start()
        copies = []
        for d in (4, 3, 5, 2, 6, 1):
            to = device((self.z + d) % 8, self.x, self.y, self.core)
            copy = remote(mine_ref, slot(NEAR - 1 - d), self.zs.at[d - 1], self.zr.at[d - 1], to)
            copy.start()
            copies.append(copy)
        yield
        own.wait()
        for copy in copies:
            copy.wait_send()
        for d in range(1, NEAR):
            there = slot(NEAR - 1 - d)
            remote(there, there, self.zs.at[d - 1], self.zr.at[d - 1], self.partner).wait_recv()
        yield

    def first_rings(self, c):
        self.share(c, 0).start()
        for k in (0, 1, 4, 5):
            self.push(c, 0, k).start()
        for k in range(2):
            self.arrive(c, 0, k)
            self.push(c, 0, 2 + k).start()
        for k in (4, 5, 2, 3):
            self.arrive(c, 0, k)
        for k in (0, 1, 4, 5):
            self.push(c, 1, k).start()
        for k in range(4):
            self.share(c, 1 + k).start()
        for i in range(5):
            self.shared(c, i)

    def next_lines(self, c):
        for k in range(2):
            self.arrive(c, 1, k)
            self.push(c, 1, 2 + k).start()
        for k in range(2):
            self.arrive(c, 1, 4 + k)
            self.share(c, 5 + k).start()
        for i in (5, 6):
            self.shared(c, i)

    def last_line(self, c):
        for k in (2, 3):
            self.arrive(c, 1, k)
            self.share(c, 5 + k).start()

    def last_shared(self, c):
        for i in (7, 8):
            self.shared(c, i)

    def drain(self, c):
        for i in range(9):
            self.share(c, i).wait_send()
        for ring in range(2):
            for k in range(6):
                self.push(c, ring, k).wait_send()


def rotated(tile, cos, sin):
    lane = lax.broadcasted_iota(jnp.int32, tile.shape, 1)
    swapped = jnp.where(lane < ROPE // 2, pltpu.roll(tile, 96, 1), pltpu.roll(tile, 32, 1))
    return tile * cos + swapped * sin


def layer_kernel(
    hid_ref, again_ref, lgain_ref, mgain_ref, cos_ref, sin_ref, seg_ref, routes_ref, gates_ref, pages_ref,
    wl_hbm, wq_hbm, we_hbm, wo_hbm, wg_hbm, wu_hbm, wd_hbm, o_ref, cache_ref,
    wl, wq, we, wo, wg, wu, wd, normed, lpart, lall, tagged, keys, qf, qbuf, m_ref, l_ref, acc_ref, mixed,
    turn, pick, high, low, mix, apart, asend, ain, res, outgoing, items, xin, pout, cin, ysend, yin, back, ret, acc, fin,
    w_sem, own_sem, ls, lr, zs_, zr_, ps, pr, cs, cr,
    rs, rr, a0s, a0r, as_, ar, fys, fyr, fps, fpr, fqs, fqr, xs, xr, ys, yr, b0s, b0r, bs, br, es, er,
):
    z, x, y, core = place_of()
    seq, head = lax.axis_index("seq"), lax.axis_index("head")
    yl, yh = head // 2, seq % 2
    partner = (seq, yl * 2 + 1 - core)
    across = (seq, (1 - yl) * 2 + core)
    q_partner = yl * 2 + 1 - core
    q_across = (1 - yl) * 2 + core
    q_far = (1 - yl) * 2 + 1 - core
    tok = TOK
    mesh_id = pl.DeviceIdType.MESH
    half_y = (y, 3 - y)
    half_h = (yh, 1 - yh)

    loads = [
        pltpu.make_async_copy(src, dst, w_sem.at[i])
        for i, (src, dst) in enumerate(
            (
                (wl_hbm, wl), (wq_hbm, wq), (we_hbm, we), (wo_hbm, wo),
                (wg_hbm.at[0], wg), (wu_hbm.at[0], wu), (wd_hbm.at[0], wd),
            )
        )
    ]
    for copy in loads:
        copy.start()

    barrier = pltpu.get_barrier_semaphore()
    column = z * 4 + x

    def greet(half, k):
        at = (column + k) % 32
        pl.semaphore_signal(
            barrier, inc=1, device_id=device(at // 4, at % 4, half_y[half], core), device_id_type=mesh_id
        )

    def greet_both(k, carry):
        greet(0, k)
        greet(1, k)
        return carry

    greet(1, 0)
    for d in range(1, 4):
        pl.semaphore_signal(barrier, inc=1, device_id=(seq, (head + d) % 4), device_id_type=mesh_id)
    lax.fori_loop(1, 32, greet_both, 0)

    sends = []

    def push(src, dst, send_sem, recv_sem, target):
        copy = remote(src, dst, send_sem, recv_sem, target)
        copy.start()
        sends.append(copy)

    def arrive(region, recv_sem):
        remote(region, region, own_sem.at[2], recv_sem, partner).wait_recv()

    v = hid_ref[...].astype(F32)
    inv = lax.rsqrt(jnp.sum(v * v, axis=1, keepdims=True) * (1.0 / D) + EPS)
    normed[...] = (v * inv * again_ref[...]).astype(BF16)
    lpart[...] = jnp.zeros_like(lpart)
    turn[...] = jnp.zeros_like(turn)
    turn[0:TOPK, :] = routes_ref[...].astype(F32)
    turn[8 : 8 + TOPK, :] = gates_ref[...]
    turn[16:17, :] = seg_ref[...].astype(F32)
    turn[...] = turn[...].T
    seg_col = turn[:, 16:17]
    loads[0].wait()
    lpart[:, :144] = nt(normed[...], wl[...]).astype(BF16)
    pl.semaphore_wait(barrier, 66)

    for d in range(1, 4):
        push(lpart, lall.at[d - 1], ls.at[d - 1], lr.at[d - 1], (seq, (head + d) % 4))
    place_r = lax.broadcasted_iota(jnp.int32, (256, WIDTH), 0)
    place_c = lax.broadcasted_iota(jnp.int32, (256, WIDTH), 1)

    def spread(part, q):
        put = ((place_c == q * 144 + place_r) & (place_r < 144)).astype(F32).astype(BF16)
        return dot(part, put)

    raw = spread(lpart[...], head)
    for d in range(1, 4):
        arrive(lall.at[d - 1], lr.at[d - 1])
        raw = raw + spread(lall[d - 1], (head + 4 - d) % 4)
    comp = raw[:, :LATENT]
    inv = lax.rsqrt(jnp.sum(comp * comp, axis=1, keepdims=True) * (1.0 / LATENT) + EPS)
    tagged[:, :LATENT] = (comp * inv * lgain_ref[...]).astype(BF16)
    turned = rotated(raw[:, LATENT:], cos_ref[...], sin_ref[...])
    lane = lax.broadcasted_iota(jnp.int32, (tok, 128), 1)
    tagged[:, LATENT:] = jnp.where(lane == ROPE, seg_col, turned).astype(BF16)

    scale = (NOPE + ROPE) ** (-0.5) * 1.4426950408889634

    def work():
        page = jnp.zeros((PART, WIDTH), BF16)
        for p in range(4):
            page = jnp.where(pages_ref[:, p : p + 1] == head, tagged[p * PART : (p + 1) * PART, :], page)
        cache_ref[...] = page[:, : LATENT + ROPE]
        loads[1].wait()
        qbuf[...] = dot(normed[...], wq[...])
        loads[2].wait()
        for k in range(HEADS // 2):
            t0 = qbuf[:, k * 384 : k * 384 + 128]
            t1 = qbuf[:, k * 384 + 128 : k * 384 + 256]
            t2 = pltpu.roll(qbuf[:, k * 384 + 256 : k * 384 + 384], 64, 1)
            nope = (t0, jnp.where(lane < 64, pltpu.roll(t1, 64, 1), t2))
            rope = (t1, t2)
            for i in range(2):
                h = 2 * k + i
                rows = slice(h * tok, (h + 1) * tok)
                key_w = we[:, h * (NOPE + VDIM) : h * (NOPE + VDIM) + NOPE]
                qf[rows, :LATENT] = (nt(nope[i].astype(BF16), key_w) * scale).astype(BF16)
                qf[rows, LATENT:] = (rotated(rope[i], cos_ref[...], sin_ref[...]) * scale).astype(BF16)
        row = lax.broadcasted_iota(jnp.int32, (tok, 128), 0)
        below = (lane < row).astype(F32).astype(BF16)
        cell = lane // SLOTS
        slot = (lane % SLOTS).astype(F32)

        def table(ze, carry):
            expert = (ze * 8 + (cell % 4) * 2 + cell // 4).astype(F32)
            taken = jnp.zeros((tok, 128), F32)
            gate = jnp.zeros((tok, 128), F32)
            for j in range(TOPK):
                hit = turn[:, j : j + 1] == expert
                taken = jnp.where(hit, 1.0, taken)
                gate = jnp.where(hit, turn[:, 8 + j : 9 + j], gate)
            rank = dot(below, taken.astype(BF16))
            put = (taken > 0.5) & (rank == slot)
            weight = jnp.where(put, gate, 0.0)
            top = weight.astype(BF16)
            high[ze] = top
            low[ze] = (weight - top.astype(F32)).astype(BF16)
            pick[ze] = put.astype(F32).T.astype(BF16)
            return carry

        lax.fori_loop(0, 8, table, 0)

    mine = tagged.at[pl.ds(pl.multiple_of(head * PART, PART), PART)]
    gather = KeyGather(keys, own_sem.at[3], zs_, zr_, ps, pr, cs, cr)
    first = gather.along_z(mine)
    next(first)
    work()
    rows = HEADS * tok
    qseg = jnp.concatenate([seg_col] * HEADS, axis=0)
    at_seg = (lax.broadcasted_iota(jnp.int32, (16, 128), 1) == ROPE).astype(F32).astype(BF16)

    def segments(block):
        return nt(at_seg, block[:, LATENT:])[0:1]

    block = tagged[...]
    query = lax.broadcasted_iota(jnp.int32, (rows, 1), 0) % tok
    ok = (qseg == segments(block)) & (lax.broadcasted_iota(jnp.int32, (1, tok), 1) <= query)
    sc = jnp.where(ok, nt(qf[...], block), -1e30)
    top = jnp.max(sc, axis=1, keepdims=True)
    p = jnp.exp2(sc - top)
    m_ref[...] = top
    l_ref[...] = jnp.sum(p, axis=1, keepdims=True)
    acc_ref[...] = dot(p.astype(BF16), block[:, :LATENT])

    def attend(color, line):
        parts = []
        for k in range(4):
            xx = jnp.where(color == 0, k, line)
            yy = jnp.where(color == 0, line, k)
            parts.append(keys[:, xx, yy, color].reshape(NEAR * PART, WIDTH))
        block = jnp.concatenate(parts, axis=0)
        at = lax.broadcasted_iota(jnp.int32, (1, NEAR * 128), 1)
        place = at // (NEAR * PART)
        plane = (z + 2 + (at // PART) % NEAR) % 8
        source = plane * 8 + jnp.where(color == 0, place * 2 + line // 2, line * 2 + place // 2)
        kseg = jnp.where(source < seq, segments(block), -1.0)
        sc = jnp.where(qseg == kseg, nt(qf[...], block), -1e30)
        m_old = m_ref[...]
        m_new = jnp.maximum(m_old, jnp.max(sc, axis=1, keepdims=True))
        p = jnp.exp2(sc - m_new)
        fade = jnp.exp2(m_old - m_new)
        l_ref[...] = l_ref[...] * fade + jnp.sum(p, axis=1, keepdims=True)
        acc_ref[...] = acc_ref[...] * fade + dot(p.astype(BF16), block[:, :LATENT])
        m_ref[...] = m_new

    def attend_lines(steps):
        def one(t, carry):
            color = t % 2
            step = steps[0] if len(steps) == 1 else 1 + 2 * (t // 2)
            attend(color, (jnp.where(color == 0, y, x) + step) % 4)
            return carry

        lax.fori_loop(0, 2 * len(steps), one, 0)

    next(first)
    gather.both(gather.first_rings)
    attend_lines((0,))
    gather.both(gather.next_lines)
    attend_lines((1, 3))
    gather.both(gather.last_line)

    def last(t, carry):
        @pl.when(t == 1)
        def _():
            gather.both(gather.last_shared)

        color = (core + t) % 2
        attend(color, (jnp.where(color == 0, y, x) + 2) % 4)
        return carry

    lax.fori_loop(0, 2, last, 0)
    gather.both(gather.drain)
    mixed[...] = (acc_ref[...] / l_ref[...]).astype(BF16)

    for h in range(HEADS):
        value = we[:, h * (NOPE + VDIM) + NOPE : (h + 1) * (NOPE + VDIM)]
        mix[:, h * VDIM : (h + 1) * VDIM] = dot(mixed[h * tok : (h + 1) * tok, :], value).astype(BF16)
    loads[3].wait()
    for q in range(4):
        apart[q] = dot(mix[...], wo[:, q * 512 : (q + 1) * 512]).astype(BF16)
    for side in range(2):
        push(apart.at[side * 2 + 1 - core], ain.at[side], rs.at[side], rr.at[side], partner)
    for side in range(2):
        arrive(ain.at[side], rr.at[side])
    asend[...] = (apart[q_across].astype(F32) + ain[1 - yl].astype(F32)).astype(BF16)
    push(asend, ain.at[2], rs.at[2], rr.at[2], across)
    total = apart[head].astype(F32) + ain[yl].astype(F32)
    arrive(ain.at[2], rr.at[2])
    total = total + ain[2].astype(F32)
    own = hid_ref[:, pl.ds(pl.multiple_of(head * 512, 512), 512)].astype(F32)
    res[...] = (own + total).astype(BF16)

    locals_ = []

    def send_slab(src, dst, slab, j, send0, recv0, send_sem, recv_sem, local_sem):
        for half in range(2):
            if half == 0 and j == 0:
                copy = pltpu.make_async_copy(src.at[slab, yh, x], dst.at[z, yh, x], local_sem)
                copy.start()
                locals_.append(copy)
                for k in range(1, 4):
                    xt = (x + k) % 4
                    push(
                        src.at[slab, yh, xt], dst.at[z, yh, x], send0.at[k - 1], recv0.at[k - 1],
                        device(slab, xt, y, core),
                    )
            else:

                def send(xt, carry, half=half):
                    remote(
                        src.at[slab, half_h[half], xt], dst.at[z, yh, x], send_sem.at[half, j], recv_sem.at[half, j],
                        device(slab, xt, half_y[half], core),
                    ).start()
                    return carry

                lax.fori_loop(0, 4, send, 0)

    def slab_sent(src, slab, j, send_sem):
        for half in range(2):
            if half or j:
                part = src.at[slab, half_h[half]]
                remote(part, part, send_sem.at[half, j], own_sem.at[2], partner).wait_send()

    def slab_arrived(parts, j, recv0, recv_sem, local):
        for half in range(2):
            if half == 0 and j == 0:
                locals_[local].wait()
                for k in range(1, 4):
                    arrive(parts[0].at[(x + 4 - k) % 4], recv0.at[k - 1])
            else:
                arrive(parts[half], recv_sem.at[half, j])

    for pair in ORDER:
        for j in pair:
            zt = (z + j) % 8
            outgoing[zt] = dot(pick[zt], res[...]).astype(BF16).reshape(2, 4, SLOTS, 512)
            send_slab(outgoing, items.at[head], zt, j, a0s, a0r, as_, ar, own_sem.at[0])

    def stage_a(g):
        for j in ORDER[g]:
            zs = (z + 8 - j) % 8
            parts = (items.at[head, zs, yh], items.at[q_across, zs, 1 - yh])
            slab_arrived(parts, j, a0r, ar, 0)
            for half in range(2):
                push(parts[half], parts[half], fys.at[half, j], fyr.at[half, j], across)
                push(parts[half], parts[half], fps.at[half, j], fpr.at[half, j], partner)

    def stage_b(g):
        for j in ORDER[g]:
            zs = (z + 8 - j) % 8
            for half, part in enumerate((items.at[q_across, zs, yh], items.at[head, zs, 1 - yh])):
                arrive(part, fyr.at[half, j])
                push(part, part, fqs.at[half, j], fqr.at[half, j], partner)

    def stage_c(g):
        if g == 0:
            for copy in loads[4:]:
                copy.wait()
        for t, j in enumerate(ORDER[g]):
            zs = (z + 8 - j) % 8
            arrive(items.at[q_partner, zs, yh], fpr.at[0, j])
            arrive(items.at[q_far, zs, 1 - yh], fpr.at[1, j])
            arrive(items.at[q_far, zs, yh], fqr.at[0, j])
            arrive(items.at[q_partner, zs, 1 - yh], fqr.at[1, j])
            mean_sq = jnp.zeros((tok, 1), F32)
            for q in range(4):
                v = items[q, zs].reshape(tok, 512).astype(F32)
                mean_sq = mean_sq + jnp.sum(v * v, axis=1, keepdims=True)
            inv = lax.rsqrt(mean_sq * (1.0 / D) + EPS)
            for q in range(4):
                v = items[q, zs].reshape(tok, 512).astype(F32)
                cols = slice(q * 512, (q + 1) * 512)
                xin[t * tok : (t + 1) * tok, cols] = (v * inv * mgain_ref[:, cols]).astype(BF16)
        gate = nt(xin[...], wg[...])
        up = nt(xin[...], wu[...])
        hidden = (gate / (1.0 + jnp.exp(-gate)) * up).astype(BF16)
        for q in range(4):
            part = dot(hidden, wd[:, q * 512 : (q + 1) * 512]).astype(BF16)
            for t, j in enumerate(ORDER[g]):
                pout[q, (z + 8 - j) % 8] = part[t * tok : (t + 1) * tok].reshape(2, 4, SLOTS, 512)
        for j in ORDER[g]:
            zs = (z + 8 - j) % 8
            for side in range(2):
                push(
                    pout.at[side * 2 + 1 - core, zs], cin.at[side, zs], xs.at[side, j], xr.at[side, j], partner
                )

    def chip_sum(side, zs, h):
        return pout[side * 2 + core, zs, h].astype(F32) + cin[side, zs, h].astype(F32)

    def stage_d(g):
        for j in ORDER[g]:
            zs = (z + 8 - j) % 8
            for side in range(2):
                arrive(cin.at[side, zs], xr.at[side, j])
            ysend[zs, yh] = chip_sum(1 - yl, zs, yh).astype(BF16)
            ysend[zs, 1 - yh] = chip_sum(yl, zs, 1 - yh).astype(BF16)
            push(ysend.at[zs], yin.at[zs], ys.at[j], yr.at[j], across)

    def stage_e(g):
        for j in ORDER[g]:
            zs = (z + 8 - j) % 8
            arrive(yin.at[zs], yr.at[j])
            back[zs, yh] = (chip_sum(yl, zs, yh) + yin[zs, yh].astype(F32)).astype(BF16)
            back[zs, 1 - yh] = (chip_sum(1 - yl, zs, 1 - yh) + yin[zs, 1 - yh].astype(F32)).astype(BF16)
            send_slab(back, ret, zs, j, b0s, b0r, bs, br, own_sem.at[1])

    a, b, c, d, e = stage_a, stage_b, stage_c, stage_d, stage_e
    for stage, g in (
        (a, 0), (b, 0), (a, 1), (c, 0), (b, 1), (d, 0), (a, 2), (c, 1), (e, 0), (b, 2),
        (d, 1), (a, 3), (c, 2), (e, 1), (b, 3), (d, 2), (c, 3), (e, 2), (d, 3), (e, 3),
    ):
        stage(g)

    acc[...] = res[...].astype(F32)
    for pair in ORDER:
        for j in pair:
            ze = (z + j) % 8
            slab_arrived((ret.at[ze, yh], ret.at[ze, 1 - yh]), j, b0r, br, 1)
            got = ret[ze].reshape(tok, 512)
            acc[...] += dot(high[ze], got) + dot(low[ze], got)
    fin[head] = acc[...].astype(BF16)
    parts = (pl.ds(0, tok // 2), pl.ds(tok // 2, tok // 2))
    for i, at in enumerate(parts):
        push(fin.at[head, at], fin.at[head, at], es.at[i], er.at[i], across)
    push(fin.at[head], fin.at[head], es.at[4], er.at[4], partner)
    for i, at in enumerate(parts):
        arrive(fin.at[q_across, at], er.at[i])
        push(fin.at[q_across, at], fin.at[q_across, at], es.at[2 + i], er.at[2 + i], partner)
    arrive(fin.at[q_partner], er.at[4])
    for i, at in enumerate(parts):
        arrive(fin.at[q_far, at], er.at[2 + i])
    for q in range(4):
        o_ref[:, q * 512 : (q + 1) * 512] = fin[q]
    for copy in sends:
        copy.wait_send()
    for j in range(8):
        slab_sent(outgoing, (z + j) % 8, j, as_)
        slab_sent(back, (z + 8 - j) % 8, j, bs)


def local(
    hidden_in,
    attn_gain,
    w_query,
    w_latent,
    latent_gain,
    w_expand,
    w_out,
    moe_gain,
    w_gate,
    w_up,
    w_down,
    routes,
    gates,
    segment,
    page_table,
):
    positions = lax.axis_index("seq") * TOK + jnp.arange(TOK, dtype=jnp.int32)
    cosine, sine = rope_tables(positions, ROPE)
    rest = jnp.zeros((TOK, 128 - ROPE), F32)
    cos = jnp.concatenate([cosine, cosine, rest], axis=1)
    sin = jnp.concatenate([-sine, sine, rest], axis=1)
    ff = w_gate.shape[2]
    dma = pltpu.SemaphoreType.DMA
    vmem, hbm = pl.BlockSpec(memory_space=pltpu.VMEM), pl.BlockSpec(memory_space=pl.ANY)
    chunks = (8, 2, 4, SLOTS, 512)
    quarter = (TOK, 512)
    rows = HEADS * TOK
    tables = (8, 128, 128)

    def space(*shape):
        return pltpu.VMEM(shape, BF16)

    def two(*shape):
        return [dma(shape), dma(shape)]

    hidden_out, page = pl.pallas_call(
        layer_kernel,
        out_shape=(
            jax.ShapeDtypeStruct((TOK, D), BF16),
            jax.ShapeDtypeStruct((PART, LATENT + ROPE), BF16),
        ),
        in_specs=[vmem] * 10 + [hbm] * 7,
        out_specs=(vmem, vmem),
        scratch_shapes=[
            space(144, D), space(D, 768), space(LATENT, 1024), space(512, D), space(ff, D), space(ff, D),
            space(ff, D), space(TOK, D), space(TOK, 256), space(3, TOK, 256), space(TOK, WIDTH),
            space(NEAR, 4, 4, 2, PART, WIDTH), space(rows, WIDTH),
            pltpu.VMEM((TOK, 768), F32), pltpu.VMEM((rows, 1), F32), pltpu.VMEM((rows, 1), F32),
            pltpu.VMEM((rows, LATENT), F32), space(rows, LATENT),
            pltpu.VMEM((TOK, 128), F32), space(*tables), space(*tables), space(*tables), space(*quarter),
            space(4, *quarter), space(*quarter),
            space(3, *quarter), space(*quarter), space(*chunks), space(4, *chunks), space(2 * TOK, D),
            space(4, *chunks), space(2, *chunks), space(*chunks), space(*chunks), space(*chunks), space(*chunks),
            pltpu.VMEM(quarter, F32), space(4, *quarter),
            dma((7,)), dma((4,)), *two(3), *two(6), *two(12), *two(9),
            *two(3), *two(3), *two(2, 8), *two(2, 8), *two(2, 8), *two(2, 8), *two(2, 8), *two(8),
            *two(3), *two(2, 8), *two(5),
        ],
        compiler_params=pltpu.CompilerParams(
            collective_id=0, has_side_effects=True, vmem_limit_bytes=60 << 20
        ),
    )(
        hidden_in,
        attn_gain[None, :],
        latent_gain[None, :],
        moe_gain[None, :],
        cos,
        sin,
        segment[None, :],
        routes.T,
        gates.T,
        page_table,
        w_latent.T,
        w_query,
        w_expand,
        w_out,
        w_gate.transpose(0, 2, 1),
        w_up.transpose(0, 2, 1),
        w_down,
    )
    return (hidden_out, page.reshape(1, PART * (LATENT + ROPE)))


def solution(mesh):
    return jax.shard_map(
        local,
        mesh=mesh,
        in_specs=(
            P("seq", None),
            P(),
            P(None, "head"),
            P(None, "head"),
            P(),
            P(None, "head"),
            P("head", None),
            P(),
            P("seq", None, "head"),
            P("seq", None, "head"),
            P("seq", "head", None),
            P("seq", None),
            P("seq", None),
            P("seq"),
            P("seq", None),
        ),
        out_specs=(P("seq", None), P(("seq", "head"), None)),
        check_vma=False,
    )
```

```python
import jax
import jax.numpy as jnp
from jax import lax
from jax.experimental import pallas as pl
from jax.experimental.pallas import tpu as pltpu
from jax.sharding import PartitionSpec as P

D = 2048
NOPE = 128
ROPE = 64
VDIM = 128
LATENT = 512
TOPK = 6
TOK = 128
HEADS = 4
SLOTS = 16
PART = 32
WIDTH = 640

EPS = 1e-06
THETA = 50000.0
F32 = jnp.float32
BF16 = jnp.bfloat16


def rope_tables(positions, feat_width):
    half_width = feat_width // 2
    inv_freq = THETA ** (-jnp.arange(half_width, dtype=F32) * 2.0 / feat_width)
    angles = positions.astype(F32)[:, None] * inv_freq[None, :]
    return (jnp.cos(angles), jnp.sin(angles))


def dot(a, b):
    return jnp.dot(a, b, preferred_element_type=F32)


ORDER = ((7, 1), (4, 0), (5, 3), (6, 2))


def nt(a, b):
    return lax.dot_general(a, b, (((1,), (1,)), ((), ())), preferred_element_type=F32)


def place_of():
    seq, head = lax.axis_index("seq"), lax.axis_index("head")
    return seq // 8, (seq // 2) % 4, (seq % 2) * 2 + head // 2, head % 2


def device(z, x, y, core):
    return (z * 8 + x * 2 + y // 2, (y % 2) * 2 + core)


def remote(src, dst, send_sem, recv_sem, target):
    return pltpu.make_async_remote_copy(
        src_ref=src, dst_ref=dst, send_sem=send_sem, recv_sem=recv_sem,
        device_id=target, device_id_type=pl.DeviceIdType.MESH,
    )


NEAR = 7
HALVES = ((0, 4), (4, 3))


class KeyGather:
    def __init__(self, keys, own_sem, zs, zr, ps, pr, cs, cr):
        self.keys, self.own_sem = keys, own_sem
        self.zs, self.zr, self.ps, self.pr, self.cs, self.cr = zs, zr, ps, pr, cs, cr
        self.z, self.x, self.y, self.core = place_of()
        self.partner = device(self.z, self.x, self.y, 1 - self.core)

    def both(self, act):
        @pl.when(self.core == 0)
        def _():
            act(0)

        @pl.when(self.core == 1)
        def _():
            act(1)

    def region(self, c, ring, lo, n, step):
        along_x = (c == 0) == (ring == 0)
        planes = pl.ds(lo, n)
        if along_x:
            at = (self.x + step) % 4
            return self.keys.at[planes, at, self.y, c] if ring == 0 else self.keys.at[planes, at, :, c]
        at = (self.y + step) % 4
        return self.keys.at[planes, self.x, at, c] if ring == 0 else self.keys.at[planes, :, at, c]

    def piece(self, c, i):
        if i == 0:
            return self.region(c, 0, 0, NEAR, 0)
        lo, n, step = ((0, NEAR, 3), (0, NEAR, 1), (*HALVES[0], 2), (*HALVES[1], 2))[(i - 1) % 4]
        return self.region(c, (i - 1) // 4, lo, n, step)

    def share(self, c, i):
        part = self.piece(c, i)
        return remote(part, part, self.cs.at[i], self.cr.at[i], self.partner)

    def shared(self, c, i):
        part = self.piece(1 - c, i)
        remote(part, part, self.cs.at[i], self.cr.at[i], self.partner).wait_recv()

    def push(self, c, ring, k):
        along_x = (c == 0) == (ring == 0)
        x, y, z = self.x, self.y, self.z
        turn = 1 if k in (0, 2, 4) else 3
        to = device(z, (x + turn) % 4, y, self.core) if along_x else device(z, x, (y + turn) % 4, self.core)
        half, step = ((0, 0), (1, 0), (0, 3), (1, 1), (1, 0), (0, 0))[k]
        part = self.region(c, ring, *HALVES[half], step)
        return remote(part, part, self.ps.at[6 * ring + k], self.pr.at[6 * ring + k], to)

    def arrive(self, c, ring, k):
        half, step = ((0, 3), (1, 1), (0, 2), (1, 2), (1, 3), (0, 1))[k]
        part = self.region(c, ring, *HALVES[half], step)
        remote(part, part, self.ps.at[6 * ring + k], self.pr.at[6 * ring + k], self.partner).wait_recv()

    def along_z(self, mine_ref):
        slot = lambda r: self.keys.at[r, self.x, self.y, self.core]
        own = pltpu.make_async_copy(mine_ref, slot(NEAR - 1), self.own_sem)
        own.start()
        copies = []
        for d in (4, 3, 5, 2, 6, 1):
            to = device((self.z + d) % 8, self.x, self.y, self.core)
            copy = remote(mine_ref, slot(NEAR - 1 - d), self.zs.at[d - 1], self.zr.at[d - 1], to)
            copy.start()
            copies.append(copy)
        yield
        own.wait()
        for copy in copies:
            copy.wait_send()
        for d in range(1, NEAR):
            there = slot(NEAR - 1 - d)
            remote(there, there, self.zs.at[d - 1], self.zr.at[d - 1], self.partner).wait_recv()
        yield

    def first_rings(self, c):
        self.share(c, 0).start()
        for k in (0, 1, 4, 5):
            self.push(c, 0, k).start()
        for k in range(2):
            self.arrive(c, 0, k)
            self.push(c, 0, 2 + k).start()
        for k in (4, 5, 2, 3):
            self.arrive(c, 0, k)
        for k in (0, 1, 4, 5):
            self.push(c, 1, k).start()
        for k in range(4):
            self.share(c, 1 + k).start()
        for i in range(5):
            self.shared(c, i)

    def next_lines(self, c):
        for k in range(2):
            self.arrive(c, 1, k)
            self.push(c, 1, 2 + k).start()
        for k in range(2):
            self.arrive(c, 1, 4 + k)
            self.share(c, 5 + k).start()
        for i in (5, 6):
            self.shared(c, i)

    def last_line(self, c):
        for k in (2, 3):
            self.arrive(c, 1, k)
            self.share(c, 5 + k).start()

    def last_shared(self, c):
        for i in (7, 8):
            self.shared(c, i)

    def drain(self, c):
        for i in range(9):
            self.share(c, i).wait_send()
        for ring in range(2):
            for k in range(6):
                self.push(c, ring, k).wait_send()


def rotated(tile, cos, sin):
    lane = lax.broadcasted_iota(jnp.int32, tile.shape, 1)
    swapped = jnp.where(lane < ROPE // 2, pltpu.roll(tile, 96, 1), pltpu.roll(tile, 32, 1))
    return tile * cos + swapped * sin


def layer_kernel(
    hid_ref, again_ref, lgain_ref, mgain_ref, cos_ref, sin_ref, seg_ref, routes_ref, gates_ref, pages_ref,
    wl_hbm, wq_hbm, we_hbm, wo_hbm, wg_hbm, wu_hbm, wd_hbm, o_ref, cache_ref,
    wl, wq, we, wo, wg, wu, wd, normed, lpart, lall, tagged, keys, qf, qbuf, m_ref, l_ref, acc_ref, mixed,
    turn, pick, high, low, mix, apart, asend, ain, res, outgoing, items, xin, pout, cin, ysend, yin, back, ret, acc, fin,
    w_sem, own_sem, ls, lr, zs_, zr_, ps, pr, cs, cr,
    rs, rr, a0s, a0r, as_, ar, fys, fyr, fps, fpr, fqs, fqr, xs, xr, ys, yr, b0s, b0r, bs, br, es, er,
):
    z, x, y, core = place_of()
    seq, head = lax.axis_index("seq"), lax.axis_index("head")
    yl, yh = head // 2, seq % 2
    partner = (seq, yl * 2 + 1 - core)
    across = (seq, (1 - yl) * 2 + core)
    q_partner = yl * 2 + 1 - core
    q_across = (1 - yl) * 2 + core
    q_far = (1 - yl) * 2 + 1 - core
    tok = TOK
    mesh_id = pl.DeviceIdType.MESH
    half_y = (y, 3 - y)
    half_h = (yh, 1 - yh)

    loads = [
        pltpu.make_async_copy(src, dst, w_sem.at[i])
        for i, (src, dst) in enumerate(
            (
                (wl_hbm, wl), (wq_hbm, wq), (we_hbm, we), (wo_hbm, wo),
                (wg_hbm.at[0], wg), (wu_hbm.at[0], wu), (wd_hbm.at[0], wd),
            )
        )
    ]
    for copy in loads:
        copy.start()

    barrier = pltpu.get_barrier_semaphore()
    column = z * 4 + x

    def greet(half, k):
        at = (column + k) % 32
        pl.semaphore_signal(
            barrier, inc=1, device_id=device(at // 4, at % 4, half_y[half], core), device_id_type=mesh_id
        )

    def greet_both(k, carry):
        greet(0, k)
        greet(1, k)
        return carry

    greet(1, 0)
    for d in range(1, 4):
        pl.semaphore_signal(barrier, inc=1, device_id=(seq, (head + d) % 4), device_id_type=mesh_id)
    lax.fori_loop(1, 32, greet_both, 0)

    sends = []

    def push(src, dst, send_sem, recv_sem, target):
        copy = remote(src, dst, send_sem, recv_sem, target)
        copy.start()
        sends.append(copy)

    def arrive(region, recv_sem):
        remote(region, region, own_sem.at[2], recv_sem, partner).wait_recv()

    v = hid_ref[...].astype(F32)
    inv = lax.rsqrt(jnp.sum(v * v, axis=1, keepdims=True) * (1.0 / D) + EPS)
    normed[...] = (v * inv * again_ref[...]).astype(BF16)
    lpart[...] = jnp.zeros_like(lpart)
    turn[...] = jnp.zeros_like(turn)
    turn[0:TOPK, :] = routes_ref[...].astype(F32)
    turn[8 : 8 + TOPK, :] = gates_ref[...]
    turn[16:17, :] = seg_ref[...].astype(F32)
    turn[...] = turn[...].T
    seg_col = turn[:, 16:17]
    loads[0].wait()
    lpart[:, :144] = nt(normed[...], wl[...]).astype(BF16)
    pl.semaphore_wait(barrier, 66)

    for d in range(1, 4):
        push(lpart, lall.at[d - 1], ls.at[d - 1], lr.at[d - 1], (seq, (head + d) % 4))
    place_r = lax.broadcasted_iota(jnp.int32, (256, WIDTH), 0)
    place_c = lax.broadcasted_iota(jnp.int32, (256, WIDTH), 1)

    def spread(part, q):
        put = ((place_c == q * 144 + place_r) & (place_r < 144)).astype(F32).astype(BF16)
        return dot(part, put)

    raw = spread(lpart[...], head)
    for d in range(1, 4):
        arrive(lall.at[d - 1], lr.at[d - 1])
        raw = raw + spread(lall[d - 1], (head + 4 - d) % 4)
    comp = raw[:, :LATENT]
    inv = lax.rsqrt(jnp.sum(comp * comp, axis=1, keepdims=True) * (1.0 / LATENT) + EPS)
    tagged[:, :LATENT] = (comp * inv * lgain_ref[...]).astype(BF16)
    turned = rotated(raw[:, LATENT:], cos_ref[...], sin_ref[...])
    lane = lax.broadcasted_iota(jnp.int32, (tok, 128), 1)
    tagged[:, LATENT:] = jnp.where(lane == ROPE, seg_col, turned).astype(BF16)

    scale = (NOPE + ROPE) ** (-0.5) * 1.4426950408889634

    def work():
        page = jnp.zeros((PART, WIDTH), BF16)
        for p in range(4):
            page = jnp.where(pages_ref[:, p : p + 1] == head, tagged[p * PART : (p + 1) * PART, :], page)
        cache_ref[...] = page[:, : LATENT + ROPE]
        loads[1].wait()
        qbuf[...] = dot(normed[...], wq[...])
        loads[2].wait()
        for k in range(HEADS // 2):
            t0 = qbuf[:, k * 384 : k * 384 + 128]
            t1 = qbuf[:, k * 384 + 128 : k * 384 + 256]
            t2 = pltpu.roll(qbuf[:, k * 384 + 256 : k * 384 + 384], 64, 1)
            nope = (t0, jnp.where(lane < 64, pltpu.roll(t1, 64, 1), t2))
            rope = (t1, t2)
            for i in range(2):
                h = 2 * k + i
                rows = slice(h * tok, (h + 1) * tok)
                key_w = we[:, h * (NOPE + VDIM) : h * (NOPE + VDIM) + NOPE]
                qf[rows, :LATENT] = (nt(nope[i].astype(BF16), key_w) * scale).astype(BF16)
                qf[rows, LATENT:] = (rotated(rope[i], cos_ref[...], sin_ref[...]) * scale).astype(BF16)
        row = lax.broadcasted_iota(jnp.int32, (tok, 128), 0)
        below = (lane < row).astype(F32).astype(BF16)
        cell = lane // SLOTS
        slot = (lane % SLOTS).astype(F32)

        def table(ze, carry):
            expert = (ze * 8 + (cell % 4) * 2 + cell // 4).astype(F32)
            taken = jnp.zeros((tok, 128), F32)
            gate = jnp.zeros((tok, 128), F32)
            for j in range(TOPK):
                hit = turn[:, j : j + 1] == expert
                taken = jnp.where(hit, 1.0, taken)
                gate = jnp.where(hit, turn[:, 8 + j : 9 + j], gate)
            rank = dot(below, taken.astype(BF16))
            put = (taken > 0.5) & (rank == slot)
            weight = jnp.where(put, gate, 0.0)
            top = weight.astype(BF16)
            high[ze] = top
            low[ze] = (weight - top.astype(F32)).astype(BF16)
            pick[ze] = put.astype(F32).T.astype(BF16)
            return carry

        lax.fori_loop(0, 8, table, 0)

    mine = tagged.at[pl.ds(pl.multiple_of(head * PART, PART), PART)]
    gather = KeyGather(keys, own_sem.at[3], zs_, zr_, ps, pr, cs, cr)
    first = gather.along_z(mine)
    next(first)
    work()
    rows = HEADS * tok
    qseg = jnp.concatenate([seg_col] * HEADS, axis=0)
    at_seg = (lax.broadcasted_iota(jnp.int32, (16, 128), 1) == ROPE).astype(F32).astype(BF16)

    def segments(block):
        return nt(at_seg, block[:, LATENT:])[0:1]

    block = tagged[...]
    query = lax.broadcasted_iota(jnp.int32, (rows, 1), 0) % tok
    ok = (qseg == segments(block)) & (lax.broadcasted_iota(jnp.int32, (1, tok), 1) <= query)
    sc = jnp.where(ok, nt(qf[...], block), -1e30)
    top = jnp.max(sc, axis=1, keepdims=True)
    p = jnp.exp2(sc - top)
    m_ref[...] = top
    l_ref[...] = jnp.sum(p, axis=1, keepdims=True)
    acc_ref[...] = dot(p.astype(BF16), block[:, :LATENT])

    def attend(color, line):
        parts = []
        for k in range(4):
            xx = jnp.where(color == 0, k, line)
            yy = jnp.where(color == 0, line, k)
            parts.append(keys[:, xx, yy, color].reshape(NEAR * PART, WIDTH))
        block = jnp.concatenate(parts, axis=0)
        at = lax.broadcasted_iota(jnp.int32, (1, NEAR * 128), 1)
        place = at // (NEAR * PART)
        plane = (z + 2 + (at // PART) % NEAR) % 8
        source = plane * 8 + jnp.where(color == 0, place * 2 + line // 2, line * 2 + place // 2)
        kseg = jnp.where(source < seq, segments(block), -1.0)
        sc = jnp.where(qseg == kseg, nt(qf[...], block), -1e30)
        m_old = m_ref[...]
        m_new = jnp.maximum(m_old, jnp.max(sc, axis=1, keepdims=True))
        p = jnp.exp2(sc - m_new)
        fade = jnp.exp2(m_old - m_new)
        l_ref[...] = l_ref[...] * fade + jnp.sum(p, axis=1, keepdims=True)
        acc_ref[...] = acc_ref[...] * fade + dot(p.astype(BF16), block[:, :LATENT])
        m_ref[...] = m_new

    def attend_lines(steps):
        def one(t, carry):
            color = t % 2
            step = steps[0] if len(steps) == 1 else 1 + 2 * (t // 2)
            attend(color, (jnp.where(color == 0, y, x) + step) % 4)
            return carry

        lax.fori_loop(0, 2 * len(steps), one, 0)

    next(first)
    gather.both(gather.first_rings)
    attend_lines((0,))
    gather.both(gather.next_lines)
    attend_lines((1, 3))
    gather.both(gather.last_line)

    def last(t, carry):
        @pl.when(t == 1)
        def _():
            gather.both(gather.last_shared)

        color = (core + t) % 2
        attend(color, (jnp.where(color == 0, y, x) + 2) % 4)
        return carry

    lax.fori_loop(0, 2, last, 0)
    gather.both(gather.drain)
    mixed[...] = (acc_ref[...] / l_ref[...]).astype(BF16)

    for h in range(HEADS):
        value = we[:, h * (NOPE + VDIM) + NOPE : (h + 1) * (NOPE + VDIM)]
        mix[:, h * VDIM : (h + 1) * VDIM] = dot(mixed[h * tok : (h + 1) * tok, :], value).astype(BF16)
    loads[3].wait()
    for q in range(4):
        apart[q] = dot(mix[...], wo[:, q * 512 : (q + 1) * 512]).astype(BF16)
    for side in range(2):
        push(apart.at[side * 2 + 1 - core], ain.at[side], rs.at[side], rr.at[side], partner)
    for side in range(2):
        arrive(ain.at[side], rr.at[side])
    asend[...] = (apart[q_across].astype(F32) + ain[1 - yl].astype(F32)).astype(BF16)
    push(asend, ain.at[2], rs.at[2], rr.at[2], across)
    total = apart[head].astype(F32) + ain[yl].astype(F32)
    arrive(ain.at[2], rr.at[2])
    total = total + ain[2].astype(F32)
    own = hid_ref[:, pl.ds(pl.multiple_of(head * 512, 512), 512)].astype(F32)
    res[...] = (own + total).astype(BF16)

    locals_ = []

    def send_slab(src, dst, slab, j, send0, recv0, send_sem, recv_sem, local_sem):
        for half in range(2):
            if half == 0 and j == 0:
                copy = pltpu.make_async_copy(src.at[slab, yh, x], dst.at[z, yh, x], local_sem)
                copy.start()
                locals_.append(copy)
                for k in range(1, 4):
                    xt = (x + k) % 4
                    push(
                        src.at[slab, yh, xt], dst.at[z, yh, x], send0.at[k - 1], recv0.at[k - 1],
                        device(slab, xt, y, core),
                    )
            else:

                def send(xt, carry, half=half):
                    remote(
                        src.at[slab, half_h[half], xt], dst.at[z, yh, x], send_sem.at[half, j], recv_sem.at[half, j],
                        device(slab, xt, half_y[half], core),
                    ).start()
                    return carry

                lax.fori_loop(0, 4, send, 0)

    def slab_sent(src, slab, j, send_sem):
        for half in range(2):
            if half or j:
                part = src.at[slab, half_h[half]]
                remote(part, part, send_sem.at[half, j], own_sem.at[2], partner).wait_send()

    def slab_arrived(parts, j, recv0, recv_sem, local):
        for half in range(2):
            if half == 0 and j == 0:
                locals_[local].wait()
                for k in range(1, 4):
                    arrive(parts[0].at[(x + 4 - k) % 4], recv0.at[k - 1])
            else:
                arrive(parts[half], recv_sem.at[half, j])

    for pair in ORDER:
        for j in pair:
            zt = (z + j) % 8
            outgoing[zt] = dot(pick[zt], res[...]).astype(BF16).reshape(2, 4, SLOTS, 512)
            send_slab(outgoing, items.at[head], zt, j, a0s, a0r, as_, ar, own_sem.at[0])

    def stage_a(g):
        for j in ORDER[g]:
            zs = (z + 8 - j) % 8
            parts = (items.at[head, zs, yh], items.at[q_across, zs, 1 - yh])
            slab_arrived(parts, j, a0r, ar, 0)
            for half in range(2):
                push(parts[half], parts[half], fys.at[half, j], fyr.at[half, j], across)
                push(parts[half], parts[half], fps.at[half, j], fpr.at[half, j], partner)

    def stage_b(g):
        for j in ORDER[g]:
            zs = (z + 8 - j) % 8
            for half, part in enumerate((items.at[q_across, zs, yh], items.at[head, zs, 1 - yh])):
                arrive(part, fyr.at[half, j])
                push(part, part, fqs.at[half, j], fqr.at[half, j], partner)

    def stage_c(g):
        if g == 0:
            for copy in loads[4:]:
                copy.wait()
        for t, j in enumerate(ORDER[g]):
            zs = (z + 8 - j) % 8
            arrive(items.at[q_partner, zs, yh], fpr.at[0, j])
            arrive(items.at[q_far, zs, 1 - yh], fpr.at[1, j])
            arrive(items.at[q_far, zs, yh], fqr.at[0, j])
            arrive(items.at[q_partner, zs, 1 - yh], fqr.at[1, j])
            mean_sq = jnp.zeros((tok, 1), F32)
            for q in range(4):
                v = items[q, zs].reshape(tok, 512).astype(F32)
                mean_sq = mean_sq + jnp.sum(v * v, axis=1, keepdims=True)
            inv = lax.rsqrt(mean_sq * (1.0 / D) + EPS)
            for q in range(4):
                v = items[q, zs].reshape(tok, 512).astype(F32)
                cols = slice(q * 512, (q + 1) * 512)
                xin[t * tok : (t + 1) * tok, cols] = (v * inv * mgain_ref[:, cols]).astype(BF16)
        gate = nt(xin[...], wg[...])
        up = nt(xin[...], wu[...])
        hidden = (gate / (1.0 + jnp.exp(-gate)) * up).astype(BF16)
        for q in range(4):
            part = dot(hidden, wd[:, q * 512 : (q + 1) * 512]).astype(BF16)
            for t, j in enumerate(ORDER[g]):
                pout[q, (z + 8 - j) % 8] = part[t * tok : (t + 1) * tok].reshape(2, 4, SLOTS, 512)
        for j in ORDER[g]:
            zs = (z + 8 - j) % 8
            for side in range(2):
                push(
                    pout.at[side * 2 + 1 - core, zs], cin.at[side, zs], xs.at[side, j], xr.at[side, j], partner
                )

    def chip_sum(side, zs, h):
        return pout[side * 2 + core, zs, h].astype(F32) + cin[side, zs, h].astype(F32)

    def stage_d(g):
        for j in ORDER[g]:
            zs = (z + 8 - j) % 8
            for side in range(2):
                arrive(cin.at[side, zs], xr.at[side, j])
            ysend[zs, yh] = chip_sum(1 - yl, zs, yh).astype(BF16)
            ysend[zs, 1 - yh] = chip_sum(yl, zs, 1 - yh).astype(BF16)
            push(ysend.at[zs], yin.at[zs], ys.at[j], yr.at[j], across)

    def stage_e(g):
        for j in ORDER[g]:
            zs = (z + 8 - j) % 8
            arrive(yin.at[zs], yr.at[j])
            back[zs, yh] = (chip_sum(yl, zs, yh) + yin[zs, yh].astype(F32)).astype(BF16)
            back[zs, 1 - yh] = (chip_sum(1 - yl, zs, 1 - yh) + yin[zs, 1 - yh].astype(F32)).astype(BF16)
            send_slab(back, ret, zs, j, b0s, b0r, bs, br, own_sem.at[1])

    a, b, c, d, e = stage_a, stage_b, stage_c, stage_d, stage_e
    for stage, g in (
        (a, 0), (b, 0), (c, 0), (a, 1), (d, 0), (b, 1), (c, 1), (e, 0), (a, 2), (d, 1),
        (b, 2), (c, 2), (e, 1), (a, 3), (d, 2), (b, 3), (c, 3), (e, 2), (d, 3), (e, 3),
    ):
        stage(g)

    acc[...] = res[...].astype(F32)
    for pair in ORDER:
        for j in pair:
            ze = (z + j) % 8
            slab_arrived((ret.at[ze, yh], ret.at[ze, 1 - yh]), j, b0r, br, 1)
            got = ret[ze].reshape(tok, 512)
            acc[...] += dot(high[ze], got) + dot(low[ze], got)
    fin[head] = acc[...].astype(BF16)
    parts = (pl.ds(0, tok // 2), pl.ds(tok // 2, tok // 2))
    for i, at in enumerate(parts):
        push(fin.at[head, at], fin.at[head, at], es.at[i], er.at[i], across)
    push(fin.at[head], fin.at[head], es.at[4], er.at[4], partner)
    for i, at in enumerate(parts):
        arrive(fin.at[q_across, at], er.at[i])
        push(fin.at[q_across, at], fin.at[q_across, at], es.at[2 + i], er.at[2 + i], partner)
    arrive(fin.at[q_partner], er.at[4])
    for i, at in enumerate(parts):
        arrive(fin.at[q_far, at], er.at[2 + i])
    for q in range(4):
        o_ref[:, q * 512 : (q + 1) * 512] = fin[q]
    for copy in sends:
        copy.wait_send()
    for j in range(8):
        slab_sent(outgoing, (z + j) % 8, j, as_)
        slab_sent(back, (z + 8 - j) % 8, j, bs)


def local(
    hidden_in,
    attn_gain,
    w_query,
    w_latent,
    latent_gain,
    w_expand,
    w_out,
    moe_gain,
    w_gate,
    w_up,
    w_down,
    routes,
    gates,
    segment,
    page_table,
):
    positions = lax.axis_index("seq") * TOK + jnp.arange(TOK, dtype=jnp.int32)
    cosine, sine = rope_tables(positions, ROPE)
    rest = jnp.zeros((TOK, 128 - ROPE), F32)
    cos = jnp.concatenate([cosine, cosine, rest], axis=1)
    sin = jnp.concatenate([-sine, sine, rest], axis=1)
    ff = w_gate.shape[2]
    dma = pltpu.SemaphoreType.DMA
    vmem, hbm = pl.BlockSpec(memory_space=pltpu.VMEM), pl.BlockSpec(memory_space=pl.ANY)
    chunks = (8, 2, 4, SLOTS, 512)
    quarter = (TOK, 512)
    rows = HEADS * TOK
    tables = (8, 128, 128)

    def space(*shape):
        return pltpu.VMEM(shape, BF16)

    def two(*shape):
        return [dma(shape), dma(shape)]

    hidden_out, page = pl.pallas_call(
        layer_kernel,
        out_shape=(
            jax.ShapeDtypeStruct((TOK, D), BF16),
            jax.ShapeDtypeStruct((PART, LATENT + ROPE), BF16),
        ),
        in_specs=[vmem] * 10 + [hbm] * 7,
        out_specs=(vmem, vmem),
        scratch_shapes=[
            space(144, D), space(D, 768), space(LATENT, 1024), space(512, D), space(ff, D), space(ff, D),
            space(ff, D), space(TOK, D), space(TOK, 256), space(3, TOK, 256), space(TOK, WIDTH),
            space(NEAR, 4, 4, 2, PART, WIDTH), space(rows, WIDTH),
            pltpu.VMEM((TOK, 768), F32), pltpu.VMEM((rows, 1), F32), pltpu.VMEM((rows, 1), F32),
            pltpu.VMEM((rows, LATENT), F32), space(rows, LATENT),
            pltpu.VMEM((TOK, 128), F32), space(*tables), space(*tables), space(*tables), space(*quarter),
            space(4, *quarter), space(*quarter),
            space(3, *quarter), space(*quarter), space(*chunks), space(4, *chunks), space(2 * TOK, D),
            space(4, *chunks), space(2, *chunks), space(*chunks), space(*chunks), space(*chunks), space(*chunks),
            pltpu.VMEM(quarter, F32), space(4, *quarter),
            dma((7,)), dma((4,)), *two(3), *two(6), *two(12), *two(9),
            *two(3), *two(3), *two(2, 8), *two(2, 8), *two(2, 8), *two(2, 8), *two(2, 8), *two(8),
            *two(3), *two(2, 8), *two(5),
        ],
        compiler_params=pltpu.CompilerParams(
            collective_id=0, has_side_effects=True, vmem_limit_bytes=60 << 20
        ),
    )(
        hidden_in,
        attn_gain[None, :],
        latent_gain[None, :],
        moe_gain[None, :],
        cos,
        sin,
        segment[None, :],
        routes.T,
        gates.T,
        page_table,
        w_latent.T,
        w_query,
        w_expand,
        w_out,
        w_gate.transpose(0, 2, 1),
        w_up.transpose(0, 2, 1),
        w_down,
    )
    return (hidden_out, page.reshape(1, PART * (LATENT + ROPE)))


def solution(mesh):
    return jax.shard_map(
        local,
        mesh=mesh,
        in_specs=(
            P("seq", None),
            P(),
            P(None, "head"),
            P(None, "head"),
            P(),
            P(None, "head"),
            P("head", None),
            P(),
            P("seq", None, "head"),
            P("seq", None, "head"),
            P("seq", "head", None),
            P("seq", None),
            P("seq", None),
            P("seq"),
            P("seq", None),
        ),
        out_specs=(P("seq", None), P(("seq", "head"), None)),
        check_vma=False,
    )
```
